256 devices in a mesh: site: 64 (over z_lo, y, x), cons: 4 (over z_hi, core).
Axes of the slice: x: 4, y: 4, z: 8 (z_hi: 2, z_lo: 4; z = z_hi * 4 + z_lo), core: 2. Of those that a mesh axis runs over, the one named last changes fastest.
Arguments:
- tile_values: bfloat16 [5120, 128, 128], P(('site', 'cons')), may hold values from 0 to 64, as said below
- patient_block: int32 [5120], P(('site', 'cons')), may hold values from 0 to 7
- code_block: int32 [5120], P(('site', 'cons')), may hold values from 0 to 19
- month_index: int32 [5120], P(('site', 'cons')), may hold values from 0 to 119
- live_count: int32 [256], P(('site', 'cons')), may hold values from 4 to 20, as said below
- patient_factor: bfloat16 [65536, 256], P('site'), may hold values from 0.0009 to 0.5, as said below
- month_factor: float32 [120, 256], replicated, may hold values from 0.001 to 0.01
- consensus: float32 [2560, 1024], P('site', 'cons'), may hold values from 0.05 to 1
- scaled_duals: float32 [163840, 1024], P('site', 'cons'), may hold values from -1.2 to 1.2
Outputs:
- new_consensus: float32 [2560, 1024], P('site', 'cons')
- new_duals: float32 [163840, 1024], P('site', 'cons')
- new_months: float32 [120, 256], replicated
The draws below stay inside these ranges and needn't reach their ends.
Inputs may be any that keep to these rules, and one draw needn't show every extreme that they name: `tile_values`: entries are whole counts. `live_count`: no device has more than 20 live slots, and some device has exactly 20. `patient_factor`: entries are positive.
All inputs are finite; a program needn't handle non-finite values.
Results may differ from the reference program's by a relative error of at most 0.0003.
Values may be sent and summed in bfloat16 or wider, within the bound.
No kernel may reach another device: no remote copies, remote signals or barrier semaphores. Data moves between devices by JAX's collectives and lax.ppermute only.
A program may use at most 64 MiB of HBM per device.

```python
import math
import jax
import jax.numpy as jnp
from jax import lax

R = 256
MONTHS = 120
CODES = 10240
BLOCK = 128
ITERS = 2
PAT_DEV = 1024
CAP = 20
PATIENTS = 65536
CODE_ROWS = 2560
TILES = 5120
N_SITE = 64
N_CONS = 4


def draw_tile_values(key, part):
    unit = jax.random.uniform(key, (TILES, BLOCK, BLOCK), jnp.float32, 1e-06, 1.0)
    mean_count = 1.5
    counts = jnp.minimum(jnp.floor(-jnp.log(unit) * mean_count), 64.0)
    planted = jax.random.randint(jax.random.fold_in(key, 7), (), 0, TILES * BLOCK * BLOCK)
    flat_ids = jnp.arange(TILES * BLOCK * BLOCK).reshape(TILES, BLOCK, BLOCK)
    return jnp.where(flat_ids == planted, 64.0, counts).astype(jnp.bfloat16)


def draw_live_count(key, part):
    devices = TILES // CAP
    base = jax.random.randint(jax.random.fold_in(key, 1), (devices,), CAP // 5, 3 * CAP // 5 + 1)
    busiest = jax.random.randint(jax.random.fold_in(key, 2), (), 0, devices)
    return jnp.where(jnp.arange(devices) == busiest, CAP, base).astype(jnp.int32)


def draw_patient_factor(key, part):
    site_count = PATIENTS // PAT_DEV
    row_site = (jnp.arange(PATIENTS) // PAT_DEV).astype(jnp.float32)
    site_scale = 1.0 + 2.0 * row_site / max(site_count - 1, 1)
    base_key = jax.random.fold_in(key, 11)
    column_key = jax.random.fold_in(key, 12)
    base = jnp.exp(jax.random.uniform(base_key, (PATIENTS, R), jnp.float32, math.log(0.001), math.log(0.01)))
    column = jnp.exp(jax.random.uniform(column_key, (R,), jnp.float32, 0.0, math.log(10.0)))
    return (base * column[None, :] * site_scale[:, None]).astype(jnp.bfloat16)


def with_ends(entries, stream_key, least, high):
    dims = entries.shape
    index_at = [jax.random.randint(jax.random.fold_in(stream_key, axis), (), 0, dims[axis]) for axis in range(len(dims))]
    entries = entries.at[tuple(index_at)].set(least)
    longest = dims.index(max(dims))
    index_at[longest] = (index_at[longest] + 1) % dims[longest]
    return entries.at[tuple(index_at)].set(high)


def block_levels(stream_key, extent, cuts, smallest, largest):
    def one(axis_at, parts):
        draws = jax.random.uniform(jax.random.fold_in(jax.random.fold_in(stream_key, 6), axis_at), (parts,), jnp.float32, smallest / len(cuts), largest / len(cuts))
        return jnp.repeat(jnp.exp(draws), extent[axis_at] // parts).reshape((-1,) + (1,) * (len(extent) - axis_at - 1))

    level = one(*cuts[0])
    for cut in cuts[1:]:
        level = level * one(*cut)
    return level


def bell_draw(own_key, dims, spread, limit, split=(), kind=jnp.bfloat16):
    values = jax.random.normal(own_key, dims, jnp.float32) * spread
    if len(split) > 0:
        values = block_levels(own_key, dims, split, -0.22, 0.18) * values
    return jnp.clip(values, min=-limit, max=limit).astype(kind)


def setup_inputs(seed: int = 0) -> dict:
    keys = jax.random.split(jax.random.key(seed), 10)
    tile_values = draw_tile_values(jax.random.fold_in(keys[9], 71), 0)
    patient_block = with_ends(jax.random.randint(keys[1], (TILES,), 0, PAT_DEV // BLOCK), jax.random.fold_in(keys[1], 1), 0, (PAT_DEV // BLOCK) - 1).astype(jnp.int32)
    code_block = with_ends(jax.random.randint(keys[2], (TILES,), 0, CODE_ROWS // BLOCK), jax.random.fold_in(keys[2], 1), 0, (CODE_ROWS // BLOCK) - 1).astype(jnp.int32)
    month_index = with_ends(jax.random.randint(keys[3], (TILES,), 0, MONTHS), jax.random.fold_in(keys[3], 1), 0, MONTHS - 1).astype(jnp.int32)
    live_count = draw_live_count(jax.random.fold_in(keys[9], 71), 0)
    patient_factor = draw_patient_factor(jax.random.fold_in(keys[9], 71), 0)
    month_factor = jnp.clip(jnp.exp(jax.random.uniform(keys[6], (MONTHS, R), jnp.float32, math.log(0.001), math.log(0.01))), 0.001, 0.01)
    consensus = jnp.clip(jnp.exp(math.log(1.0) - 2.9957323 * jax.random.uniform(keys[7], (CODE_ROWS, N_CONS * R), jnp.float32) ** block_levels(keys[7], (CODE_ROWS, N_CONS * R), ((0, 64), (1, 4)), -0.2, 0.2)), 0.05, 1.0)
    scaled_duals = bell_draw(keys[8], (N_SITE * CODE_ROWS, N_CONS * R), 0.2, 1.2, ((0, 64), (1, 4)), jnp.float32)
    return {"tile_values": tile_values, "patient_block": patient_block, "code_block": code_block, "month_index": month_index, "live_count": live_count, "patient_factor": patient_factor, "month_factor": month_factor, "consensus": consensus, "scaled_duals": scaled_duals}


highest = lax.Precision.HIGHEST

def invert(matrix):
    factor = jnp.linalg.cholesky(matrix)
    identity = jnp.eye(matrix.shape[0], dtype=matrix.dtype)
    lower_inv = lax.linalg.triangular_solve(factor, identity, left_side=True, lower=True)
    return jnp.dot(lower_inv.T.astype(jnp.float32), lower_inv.astype(jnp.float32), precision=highest, preferred_element_type=jnp.float32)

def reference(tile_values, patient_block, code_block, month_index, live_count, patient_factor, month_factor, consensus, scaled_duals):
    rank_size = patient_factor.shape[1]
    tile_size = tile_values.shape[1]
    devices = N_SITE * N_CONS
    capacity = tile_values.shape[0] // devices
    code_rows = CODES // N_CONS
    month_count = month_factor.shape[0]
    identity = jnp.eye(rank_size, dtype=jnp.float32)
    month_gram = jnp.dot(month_factor.T.astype(jnp.float32), month_factor.astype(jnp.float32), precision=highest, preferred_element_type=jnp.float32)
    site_factors = patient_factor.reshape(N_SITE, PAT_DEV, rank_size)

    def site_gram(patient_rows):
        return jnp.dot(patient_rows.T.astype(jnp.float32), patient_rows.astype(jnp.float32), preferred_element_type=jnp.float32)
    grams = lax.map(site_gram, site_factors)
    hessians = grams * month_gram
    rhos = jnp.trace(hessians, axis1=1, axis2=2) / rank_size

    def site_inverse(pair):
        return invert(pair[0] + pair[1] * identity)
    inverses = lax.map(site_inverse, (hessians, rhos))
    rho_total = jnp.sum(rhos)
    global_gram = jnp.sum(grams, axis=0)
    tiles = tile_values.reshape(devices, capacity, tile_size, tile_size)
    patient_at = patient_block.reshape(devices, capacity)
    code_at = code_block.reshape(devices, capacity)
    month_at = month_index.reshape(devices, capacity)
    device_ids = jnp.arange(devices, dtype=jnp.int32)
    slot_ids = jnp.arange(capacity, dtype=jnp.int32)

    def device_gradient(inputs):
        values, prow_all, cblk_all, month_all, live, device = inputs
        factor = site_factors[device // N_CONS]

        def visit(totals, item):
            tile, prow_one, cblk_one, month_one, slot = item
            patient_rows = lax.dynamic_slice_in_dim(factor, prow_one * tile_size, tile_size, 0)
            scale = lax.dynamic_slice_in_dim(month_factor, month_one, 1, 0)
            product = jnp.dot(tile.T.astype(jnp.float32), patient_rows.astype(jnp.float32), precision=highest)
            contrib = jnp.where(slot < live, product * scale, 0.0)
            start = cblk_one * tile_size
            current = lax.dynamic_slice_in_dim(totals, start, tile_size, 0)
            return (lax.dynamic_update_slice_in_dim(totals, current + contrib, start, 0), None)
        totals, _ = lax.scan(visit, jnp.zeros((code_rows, rank_size), jnp.float32), (values, prow_all, cblk_all, month_all, slot_ids))
        return totals
    gradients = lax.map(device_gradient, (tiles, patient_at, code_at, month_at, live_count, device_ids))
    gradients = gradients.reshape(N_SITE, N_CONS, code_rows, rank_size)
    full_block = consensus.reshape(code_rows, N_CONS, rank_size).transpose(1, 0, 2)
    duals = scaled_duals.reshape(N_SITE, code_rows, N_CONS, rank_size).transpose(0, 2, 1, 3)
    for sweep in range(ITERS):

        def solve_site(inputs):
            gradient, dual, rho, inverse = inputs
            target = (gradient + rho * (full_block - dual)).reshape(N_CONS * code_rows, rank_size)
            solved_rows = jnp.dot(target.astype(jnp.float32), inverse.astype(jnp.float32), precision=highest, preferred_element_type=jnp.float32)
            return solved_rows.reshape(N_CONS, code_rows, rank_size)
        copies = lax.map(solve_site, (gradients, duals, rhos, inverses))
        summed = jnp.sum(rhos[:, None, None, None] * (copies + duals), axis=0)
        full_block = jnp.maximum(summed / rho_total, 0.0)
        duals = duals + copies - full_block

    def device_month(inputs):
        values, prow_all, cblk_all, month_all, live, device = inputs
        factor = site_factors[device // N_CONS]
        anchor = full_block[device % N_CONS]

        def visit(totals, item):
            tile, prow_one, cblk_one, month_one, slot = item
            patient_rows = lax.dynamic_slice_in_dim(factor, prow_one * tile_size, tile_size, 0)
            product = jnp.dot(tile.T.astype(jnp.float32), patient_rows.astype(jnp.float32), precision=highest)
            anchor_rows = lax.dynamic_slice_in_dim(anchor, cblk_one * tile_size, tile_size, 0)
            column = jnp.sum(product * anchor_rows, axis=0, keepdims=True)
            column = jnp.where(slot < live, column, 0.0)
            current = lax.dynamic_slice_in_dim(totals, month_one, 1, 0)
            return (lax.dynamic_update_slice_in_dim(totals, current + column, month_one, 0), None)
        totals, _ = lax.scan(visit, jnp.zeros((month_count, rank_size), jnp.float32), (values, prow_all, cblk_all, month_all, slot_ids))
        return totals
    month_grad = jnp.sum(lax.map(device_month, (tiles, patient_at, code_at, month_at, live_count, device_ids)), axis=0)
    flat = full_block.reshape(CODES, rank_size)
    code_gram = jnp.dot(flat.T.astype(jnp.float32), flat.astype(jnp.float32), precision=highest, preferred_element_type=jnp.float32)
    month_hess = global_gram * code_gram
    month_rho = jnp.trace(month_hess) / rank_size
    solved = jnp.dot((month_grad + month_rho * month_factor).astype(jnp.float32), invert(month_hess + month_rho * identity).astype(jnp.float32), precision=highest, preferred_element_type=jnp.float32)
    solved = jnp.maximum(solved, 0.0)
    new_months = solved / (jnp.mean(solved, axis=0, keepdims=True) + 1e-06)
    new_consensus = full_block.transpose(1, 0, 2).reshape(code_rows, N_CONS * rank_size)
    new_duals = duals.transpose(0, 2, 1, 3).reshape(N_SITE * code_rows, N_CONS * rank_size)
    return (new_consensus, new_duals, new_months)
```

```python
import functools

import jax
import jax.numpy as jnp
from jax import lax
from jax.experimental import pallas as pl
from jax.experimental.pallas import tpu as pltpu
from jax.sharding import PartitionSpec as P

R = 256
MONTHS = 120
BLOCK = 128
SHARE = 40
CHUNK = 640
ROWS = 2560
F32 = jnp.float32
BF16 = jnp.bfloat16
AXES = ("site", "cons")


def number(z, y, x, h, c):
    return ((z * 4 + y) * 4 + x) * 4 + h * 2 + c


def pairs_of(move):
    out = []
    for z in range(4):
        for y in range(4):
            for x in range(4):
                for h in range(2):
                    for c in range(2):
                        out.append((number(z, y, x, h, c), number(*move(z, y, x, h, c))))
    return out


def first_move(k):
    def move(z, y, x, h, c):
        return (z, y, (x + k) % 4, h, c) if c == 0 else (z, (y + k) % 4, x, h, c)

    return pairs_of(move)


def second_move(k):
    def move(z, y, x, h, c):
        return (z, (y + k) % 4, x, h, c) if c == 0 else (z, y, (x + k) % 4, h, c)

    return pairs_of(move)


def depth_move(k):
    return pairs_of(lambda z, y, x, h, c: ((z + k) % 4, y, x, h, c))


HALF_MOVE = pairs_of(lambda z, y, x, h, c: (z, y, x, 1 - h, c))
CORE_MOVE = pairs_of(lambda z, y, x, h, c: (z, y, x, h, 1 - c))


def send(value, pairs):
    return lax.ppermute(value, AXES, pairs)


def scatter_sum(parts, moves):
    return [parts[0]] + [send(parts[k], moves(k)) for k in (1, 2, 3)]


def gather(value, moves):
    return [value] + [send(value, moves((4 - k) % 4)) for k in (1, 2, 3)]


def full_sum(value, moves):
    got = [send(value, moves(k)) for k in (1, 2, 3)]
    return (value + got[0]) + (got[1] + got[2])


def gather_rows(own):
    rows = jnp.concatenate(gather(own, depth_move), 0)
    rows = jnp.concatenate(gather(rows, second_move), 0)
    return gather(rows, first_move)


def split(a):
    hi = a.astype(BF16)
    return hi, (a - hi.astype(F32)).astype(BF16)


def dot3(a, b):
    ah, al = a
    bh, bl = b
    dot = functools.partial(jnp.dot, preferred_element_type=F32)
    return dot(ah, bh) + (dot(ah, bl) + dot(al, bh))


def dot6(a, b):
    return jnp.dot(a, b, precision=lax.Precision.HIGHEST, preferred_element_type=F32)


def eye(n):
    return (
        lax.broadcasted_iota(jnp.int32, (n, n), 0) == lax.broadcasted_iota(jnp.int32, (n, n), 1)
    ).astype(F32)


def total(a):
    return jnp.sum(jnp.sum(a, axis=1, keepdims=True), axis=0, keepdims=True)


def shifted_inverse(hess):
    n = hess.shape[0]
    ident = eye(n)
    rho = total(hess * ident) * (1.0 / n)
    mat = hess * (1.0 / rho) + ident
    low, high = 0.999, n + 1.5
    c0 = 2.0 / (low + high)
    a = low * c0
    mat_parts = split(mat)

    def grow(a):
        up = a * (2.0 - a)
        s = 2.0 / (1.0 + up)
        return s, s * up

    s, a = grow(a)
    x = (s * c0) * (2.0 * ident - c0 * mat)
    for step in range(5):
        s, a = grow(a)
        x_parts = split(x)
        y = 2.0 * ident - dot3(mat_parts, x_parts)
        x = s * dot3(x_parts, split(y))
    for step in range(2):
        y = 2.0 * ident - dot6(mat, x)
        x = dot6(x, y)
    return rho, x


def inverse_kernel(place, patient, month, gram_ref, near_ref, rho_ref, m0, m1, m2, m3, mat):
    rows = patient[...]
    gram = lax.dot_general(rows, rows, (((0,), (0,)), ((), ())), preferred_element_type=F32)
    gram_ref[...] = gram
    mf = month[...]
    month_gram = lax.dot_general(
        mf, mf, (((0,), (0,)), ((), ())), precision=lax.Precision.HIGHEST, preferred_element_type=F32
    )
    rho, near = shifted_inverse(gram * month_gram)
    near_ref[...] = near
    rho_ref[...] = jnp.broadcast_to(rho, rho_ref.shape)
    core = place[4]
    square = dot6(near, near)
    mat[...] = rho * jnp.where(core == 0, near, square)
    for k, ref in enumerate((m0, m1, m2, m3)):
        at = lax.rem(place[0] + k, 4)
        ref[0:64, :] = mat[pl.ds(pl.multiple_of(at * 64, 64), 64), :]
        ref[64:72, :] = jnp.broadcast_to(rho, (8, R))


def block_row(place, k, b):
    j, i = b // 4, b % 4
    first = lax.rem(place[0] + k, 4)
    second = lax.rem(place[1] + j, 4)
    depth = lax.rem(place[2] + i, 4)
    block = depth * 16 + first * place[5] + second * place[6]
    return pl.multiple_of(block * SHARE, 8)


def local_kernel(
    place, live, patient_at, code_at, month_at,
    tiles, patient, month, duals, near, rho_ref,
    prod, a0, a1, a2, a3, grad, u_part, g_part,
):
    grad[...] = jnp.zeros_like(grad)

    def visit(k, _):
        pat = patient[pl.ds(pl.multiple_of(patient_at[k] * BLOCK, BLOCK), BLOCK), :]
        product = lax.dot_general(
            tiles[k], pat, (((0,), (0,)), ((), ())), preferred_element_type=F32
        )
        prod[k] = product
        at = pl.ds(pl.multiple_of(code_at[k] * BLOCK, BLOCK), BLOCK)
        grad[at, :] += product * month[pl.ds(month_at[k], 1), :]
        return 0

    lax.fori_loop(0, live[0], visit, 0)
    rho = rho_ref[0:1, 0:1]
    near_parts = split(near[...])
    for k, out in enumerate((a0, a1, a2, a3)):
        for b in range(16):
            at = pl.ds(block_row(place, k, b), SHARE)
            u_part[b * SHARE : (b + 1) * SHARE, :] = duals[at, :]
            g_part[b * SHARE : (b + 1) * SHARE, :] = grad[at, :]
        u = u_part[...]
        g = g_part[...] * (1.0 / rho)
        once = u + dot3(split(g - u), near_parts)
        twice = once + dot3(split(g - once), near_parts)
        once = rho * once
        twice = rho * twice
        for b in range(16):
            out[b * 80 : b * 80 + SHARE, :] = once[b * SHARE : (b + 1) * SHARE]
            out[b * 80 + SHARE : b * 80 + 80, :] = twice[b * SHARE : (b + 1) * SHARE]


def owner_kernel(place, s0, s1, s2, s3, z0_ref, mine, other, z1_ref, z2_ref, code_ref, own, oth):
    summed = (s0[...] + s1[...]) + (s2[...] + s3[...])
    for k in range(4):
        at = pl.ds(pl.multiple_of(lax.rem(place[0] + k, 4) * 64, 64), 64)
        own[at, :] = mine[k * 72 : k * 72 + 64, :]
        at = pl.ds(pl.multiple_of(lax.rem(place[1] + k, 4) * 64, 64), 64)
        oth[at, :] = other[k * 72 : k * 72 + 64, :]
    rho_total = mine[64:65, :]
    core = place[4]
    a = own[...]
    b = oth[...]
    plain = jnp.where(core == 0, a, b)
    square = jnp.where(core == 0, b, a)
    z0 = z0_ref[...]
    first = summed[0:SHARE] + dot6(z0, plain)
    z1 = jnp.maximum(first / rho_total, 0.0)
    second = summed[SHARE:] + dot6(z0, plain - square) + 2.0 * dot6(z1, plain) - rho_total * z1
    z2 = jnp.maximum(second / rho_total, 0.0)
    z1_ref[...] = z1
    z2_ref[...] = z2
    code_ref[...] = lax.dot_general(
        z2, z2, (((0,), (0,)), ((), ())), precision=lax.Precision.HIGHEST, preferred_element_type=F32
    )


def month_kernel(place, live, code_at, month_at, w0, w1, w2, w3, prod, out, natural):
    for k, w in enumerate((w0, w1, w2, w3)):
        for b in range(16):
            natural[pl.ds(block_row(place, k, b), SHARE), :] = w[b * SHARE : (b + 1) * SHARE, :]
    out[...] = jnp.zeros_like(out)

    def visit(k, _):
        at = pl.ds(pl.multiple_of(code_at[k] * BLOCK, BLOCK), BLOCK)
        column = jnp.sum(prod[k] * natural[at, :], axis=0, keepdims=True)
        out[pl.ds(month_at[k], 1), :] += column
        return 0

    lax.fori_loop(0, live[0], visit, 0)


def duals_kernel(place, *refs):
    a = refs[0:4]
    zero = refs[4:8]
    one = refs[8:12]
    two = refs[12:16]
    near, rho_ref, out, v_part = refs[16:]
    scale = 1.0 / rho_ref[0:1, 0:1]
    near_parts = split(near[...])
    for k in range(4):
        for b in range(16):
            v_part[b * SHARE : (b + 1) * SHARE, :] = a[k][b * 80 + SHARE : b * 80 + 80, :]
        z0 = zero[k][...]
        z1 = one[k][...]
        inner = z0 - dot3(split(z0), near_parts) + 2.0 * z1
        value = scale * v_part[...] + dot3(split(inner), near_parts) - z1 - two[k][...]
        for b in range(16):
            out[pl.ds(block_row(place, k, b), SHARE), :] = value[b * SHARE : (b + 1) * SHARE]


def month_inverse_kernel(place, mine, other, near_ref, rho_ref, own, oth):
    for k in range(4):
        at = pl.ds(pl.multiple_of(lax.rem(place[0] + k, 4) * 64, 64), 64)
        own[at, :] = mine[k * 64 : k * 64 + 64, :]
        at = pl.ds(pl.multiple_of(lax.rem(place[1] + k, 4) * 64, 64), 64)
        oth[at, :] = other[k * 64 : k * 64 + 64, :]
    rho, near = shifted_inverse(own[...] * (0.5 * oth[...]))
    near_ref[...] = near
    rho_ref[...] = jnp.broadcast_to(rho, rho_ref.shape)


def solve_kernel(place, top, bottom, month, near, rho_ref, out, grad):
    for k in range(4):
        at = pl.ds(pl.multiple_of(lax.rem(place[0] + k, 4) * 16, 16), 16)
        upper = jnp.where(place[4] == 0, 0, 64)
        grad[pl.ds(pl.multiple_of(upper + lax.rem(place[0] + k, 4) * 16, 16), 16), :] = top[
            k * 16 : k * 16 + 16, :
        ]
        grad[pl.ds(pl.multiple_of(64 - upper + lax.rem(place[1] + k, 4) * 16, 16), 16), :] = bottom[
            k * 16 : k * 16 + 16, :
        ]
    scaled = grad[0:MONTHS, :] * (1.0 / rho_ref[0:1, 0:1]) + month[...]
    solved = jnp.maximum(dot6(scaled, near[...]), 0.0)
    mean = jnp.sum(solved, axis=0, keepdims=True) * (1.0 / MONTHS)
    out[...] = solved / (mean + 1e-06)


def call(body, outs, scalars, scratch, *args):
    specs = [pl.BlockSpec(memory_space=pltpu.SMEM)] * scalars
    specs += [pl.BlockSpec(memory_space=pltpu.VMEM)] * (len(args) - scalars)
    shapes = [jax.ShapeDtypeStruct(s, F32) for s in outs]
    return pl.pallas_call(
        body,
        out_shape=shapes,
        in_specs=specs,
        out_specs=[pl.BlockSpec(memory_space=pltpu.VMEM)] * len(outs),
        scratch_shapes=[pltpu.VMEM(s, F32) for s in scratch],
        compiler_params=pltpu.CompilerParams(vmem_limit_bytes=48 << 20),
    )(*args)


def on_device(
    tile_values, patient_block, code_block, month_index, live_count,
    patient_factor, month_factor, consensus, scaled_duals,
):
    site = lax.axis_index("site")
    cons = lax.axis_index("cons")
    z, y, x = site // 16, (site // 4) % 4, site % 4
    h, core = cons // 2, cons % 2
    flat = core == 0
    place = jnp.stack(
        [jnp.where(flat, x, y), jnp.where(flat, y, x), z, h, core,
         jnp.where(flat, 1, 4), jnp.where(flat, 4, 1), cons]
    ).astype(jnp.int32)

    gram, near, rho, *mats = call(
        inverse_kernel, [(R, R), (R, R), (8, 128)] + [(72, R)] * 4, 1, [(R, R)],
        place, patient_factor, month_factor,
    )
    m = scatter_sum(mats, first_move)
    m = (m[0] + m[1]) + (m[2] + m[3])
    m = full_sum(m, second_move)
    m = full_sum(m, depth_move)
    mine = jnp.concatenate(gather(m, first_move), 0)
    other = send(mine, CORE_MOVE)

    prod, *parts = call(
        local_kernel, [(tile_values.shape[0], BLOCK, R)] + [(2 * CHUNK, R)] * 4, 5,
        [(ROWS, R), (CHUNK, R), (CHUNK, R)],
        place, live_count, patient_block, code_block, month_index,
        tile_values, patient_factor, month_factor, scaled_duals, near, rho,
    )
    zero = gather_rows(consensus)
    s = scatter_sum(parts, first_move)
    s = [
        (s[0][j : j + 320] + s[1][j : j + 320]) + (s[2][j : j + 320] + s[3][j : j + 320])
        for j in (0, 320, 640, 960)
    ]
    s = scatter_sum(s, second_move)
    s = [
        (s[0][i : i + 80] + s[1][i : i + 80]) + (s[2][i : i + 80] + s[3][i : i + 80])
        for i in (0, 80, 160, 240)
    ]
    s = scatter_sum(s, depth_move)
    z1, z2, code_gram = call(
        owner_kernel, [(SHARE, R), (SHARE, R), (R, R)], 1, [(R, R), (R, R)],
        place, *s, consensus, mine, other,
    )

    two = gather_rows(z2)
    one = gather_rows(z1)

    code_gram = code_gram + send(code_gram, CORE_MOVE)
    pair = jnp.where(flat, code_gram, gram)
    pair = [
        lax.dynamic_slice_in_dim(pair, ((place[0] + k) % 4) * 64, 64, 0) for k in range(4)
    ]
    g = scatter_sum(pair, first_move)
    g = (g[0] + g[1]) + (g[2] + g[3])
    g = full_sum(g, second_move)
    g = full_sum(g, depth_move)
    g = g + send(g, HALF_MOVE)
    g = jnp.concatenate(gather(g, first_move), 0)
    g_other = send(g, CORE_MOVE)
    near_m, rho_m = call(
        month_inverse_kernel, [(R, R), (8, 128)], 1, [(R, R), (R, R)], place, g, g_other
    )

    (month_sum,) = call(
        month_kernel, [(BLOCK, R)], 4, [(ROWS, R)],
        place, live_count, code_block, month_index, *two, prod,
    )
    keep = lax.dynamic_slice_in_dim(month_sum, core * 64, 64, 0)
    give = lax.dynamic_slice_in_dim(month_sum, 64 - core * 64, 64, 0)
    t = keep + send(give, CORE_MOVE)
    t = [lax.dynamic_slice_in_dim(t, ((place[0] + k) % 4) * 16, 16, 0) for k in range(4)]
    t = scatter_sum(t, first_move)
    t = (t[0] + t[1]) + (t[2] + t[3])
    t = full_sum(t, second_move)
    t = full_sum(t, depth_move)
    t = t + send(t, HALF_MOVE)
    t = jnp.concatenate(gather(t, first_move), 0)
    t_other = send(t, CORE_MOVE)

    (duals,) = call(
        duals_kernel, [(ROWS, R)], 1, [(CHUNK, R)],
        place, *parts, *zero, *one, *two, near, rho,
    )
    (new_months,) = call(
        solve_kernel, [(MONTHS, R)], 1, [(BLOCK, R)],
        place, t, t_other, month_factor, near_m, rho_m,
    )
    return (z2, duals, new_months)


def solution(mesh):
    placed = (
        P(("site", "cons"), None, None),
        P(("site", "cons")),
        P(("site", "cons")),
        P(("site", "cons")),
        P(("site", "cons")),
        P("site", None),
        P(),
        P("site", "cons"),
        P("site", "cons"),
    )
    return jax.shard_map(
        on_device,
        mesh=mesh,
        in_specs=placed,
        out_specs=(P("site", "cons"), P("site", "cons"), P()),
        check_vma=False,
    )
```

```python
import functools

import jax
import jax.numpy as jnp
from jax import lax
from jax.experimental import pallas as pl
from jax.experimental.pallas import tpu as pltpu
from jax.sharding import Mesh
from jax.sharding import PartitionSpec as P

R = 256
MONTHS = 120
BLOCK = 128
SHARE = 40
CHUNK = 640
ROWS = 2560
CAP = 20
F32 = jnp.float32
BF16 = jnp.bfloat16
AXES = ("z", "y", "x", "h", "c")
PLANE = ("y", "x")
COLUMN = ("z", "h", "c")


def number(z, y, x, h, c):
    return ((z * 4 + y) * 4 + x) * 4 + h * 2 + c


def pairs_of(move):
    out = []
    for z in range(4):
        for y in range(4):
            for x in range(4):
                for h in range(2):
                    for c in range(2):
                        out.append((number(z, y, x, h, c), number(*move(z, y, x, h, c))))
    return out


def first_move(k):
    def move(z, y, x, h, c):
        return (z, y, (x + k) % 4, h, c) if c == 0 else (z, (y + k) % 4, x, h, c)

    return pairs_of(move)


def second_move(k):
    def move(z, y, x, h, c):
        return (z, (y + k) % 4, x, h, c) if c == 0 else (z, y, (x + k) % 4, h, c)

    return pairs_of(move)


def depth_move(k):
    return pairs_of(lambda z, y, x, h, c: ((z + k) % 4, y, x, h, c))


CORE_MOVE = pairs_of(lambda z, y, x, h, c: (z, y, x, h, 1 - c))


def send(value, pairs):
    return lax.ppermute(value, AXES, pairs)


def scatter_sum(parts, moves):
    return [parts[0]] + [send(parts[k], moves(k)) for k in (1, 2, 3)]


def gather(value, moves):
    return [value] + [send(value, moves((4 - k) % 4)) for k in (1, 2, 3)]


def gather_rows(own, name):
    with jax.named_scope(name + "_depth"):
        rows = jnp.concatenate(gather(own, depth_move), 0)
    with jax.named_scope(name + "_second"):
        rows = jnp.concatenate(gather(rows, second_move), 0)
    with jax.named_scope(name + "_first"):
        return gather(rows, first_move)


def exchange(value, axes):
    return lax.all_to_all(value, axes, 0, 0, tiled=True)


def sum_to_all(value, count, axes):
    return jnp.sum(exchange(jnp.broadcast_to(value, (count, *value.shape)), axes), axis=0)


def sum_slices(value, axes):
    return jnp.sum(exchange(value.reshape(16, -1, R), axes), axis=0)


def spread_slices(value, axes):
    return exchange(jnp.broadcast_to(value, (16, *value.shape)), axes).reshape(-1, R)


def split(a):
    hi = a.astype(BF16)
    return hi, (a - hi.astype(F32)).astype(BF16)


def dot3(a, b):
    ah, al = a
    bh, bl = b
    dot = functools.partial(jnp.dot, preferred_element_type=F32)
    return dot(ah, bh) + (dot(ah, bl) + dot(al, bh))


def dot6(a, b):
    return jnp.dot(a, b, precision=lax.Precision.HIGHEST, preferred_element_type=F32)


def gram_of(a, precision=None):
    return lax.dot_general(
        a, a, (((0,), (0,)), ((), ())), precision=precision, preferred_element_type=F32
    )


def eye(n):
    return (
        lax.broadcasted_iota(jnp.int32, (n, n), 0) == lax.broadcasted_iota(jnp.int32, (n, n), 1)
    ).astype(F32)


def total(a):
    return jnp.sum(jnp.sum(a, axis=1, keepdims=True), axis=0, keepdims=True)


def shifted_inverse(hess, mat_ref, x_ref):
    n = hess.shape[0]
    ident = eye(n)
    rho = total(hess * ident) * (1.0 / n)
    mat = hess * (1.0 / rho) + ident
    mat_ref[...] = mat
    mat_parts = split(mat)
    low, high = 0.999, n + 1.5
    c0 = 2.0 / (low + high)

    def grow(a):
        up = a * (2.0 - a)
        s = 2.0 / (1.0 + up)
        return s, s * up

    s, a = grow(low * c0)
    x_ref[...] = (s * c0) * (2.0 * ident - c0 * mat)

    def coarse(_, a):
        s, a = grow(a)
        x_parts = split(x_ref[...])
        y = 2.0 * ident - dot3(mat_parts, x_parts)
        x_ref[...] = s * dot3(x_parts, split(y))
        return a

    lax.fori_loop(0, 5, coarse, jnp.float32(a))

    def fine(_, carry):
        x = x_ref[...]
        x_ref[...] = dot6(x, 2.0 * ident - dot6(mat_ref[...], x))
        return carry

    lax.fori_loop(0, 2, fine, 0)
    return rho


def block_row(place, k, b):
    j, i = b // 4, b % 4
    first = lax.rem(place[0] + k, 4)
    second = lax.rem(place[1] + j, 4)
    depth = lax.rem(place[2] + i, 4)
    block = depth * 16 + first * place[5] + second * place[6]
    return pl.multiple_of(block * SHARE, 8)


def head_kernel(
    place, patient_hbm, month_hbm, tiles_hbm, duals_hbm,
    near, rho_ref, weights, prod_hbm, a0, a1, a2, a3,
    patient, month, tiles, duals, prod, mat, square, grad, u_part, g_part, held, sems, outs,
):
    copies = [
        pltpu.make_async_copy(src, dst, sems.at[n])
        for n, (src, dst) in enumerate(
            [
                (month_hbm, month), (patient_hbm, patient), (tiles_hbm, tiles), (duals_hbm, duals),
            ]
        )
    ]
    for copy in copies:
        copy.start()
    copies[0].wait()
    mf = month[...]
    month_gram = gram_of(mf, lax.Precision.HIGHEST)
    copies[1].wait()
    gram = gram_of(patient[...])
    rho = shifted_inverse(gram * month_gram, mat, near)
    rho_ref[...] = jnp.broadcast_to(rho, rho_ref.shape)
    core = place[4]
    mat[...] = near[...]

    @pl.when(core == 1)
    def _():
        mat[...] = dot6(near[...], near[...])

    square[...] = gram
    half = pl.multiple_of(core * 128, 128)
    for p in range(16):
        weights[p * 24 : p * 24 + 16, :] = rho * mat[p * 16 : p * 16 + 16, :]
        weights[p * 24 + 16 : p * 24 + 24, :] = square[pl.ds(half + p * 8, 8), :]

    grad[...] = jnp.zeros_like(grad)
    copies[2].wait()

    def visit(k, _):
        pat = patient[pl.ds(pl.multiple_of(place[8 + k] * BLOCK, BLOCK), BLOCK), :]
        product = lax.dot_general(
            tiles[k], pat, (((0,), (0,)), ((), ())), preferred_element_type=F32
        )
        prod[k] = product
        at = pl.ds(pl.multiple_of(place[8 + CAP + k] * BLOCK, BLOCK), BLOCK)
        grad[at, :] += product * month[pl.ds(place[8 + 2 * CAP + k], 1), :]
        return 0

    lax.fori_loop(0, place[7], visit, 0)
    prod_out = pltpu.make_async_copy(prod, prod_hbm, outs.at[4])
    prod_out.start()
    near_parts = split(near[...])
    copies[3].wait()

    def chunk(k, _):
        for b in range(16):
            at = pl.ds(block_row(place, k, b), SHARE)
            u_part[b * SHARE : (b + 1) * SHARE, :] = duals[at, :]
            g_part[b * SHARE : (b + 1) * SHARE, :] = grad[at, :]
        u = u_part[...]
        g = g_part[...] * (1.0 / rho)
        once = u + dot3(split(g - u), near_parts)
        twice = once + dot3(split(g - once), near_parts)
        once = rho * once
        twice = rho * twice
        for b in range(16):
            held[k, b * 80 : b * 80 + SHARE, :] = once[b * SHARE : (b + 1) * SHARE]
            held[k, b * 80 + SHARE : b * 80 + 80, :] = twice[b * SHARE : (b + 1) * SHARE]
        for n, out in enumerate((a0, a1, a2, a3)):

            @pl.when(k == n)
            def _(n=n, out=out):
                pltpu.make_async_copy(held.at[n], out, outs.at[n]).start()

        return 0

    lax.fori_loop(0, 4, chunk, 0)
    for n, out in enumerate((a0, a1, a2, a3)):
        pltpu.make_async_copy(held.at[n], out, outs.at[n]).wait()
    prod_out.wait()


def owner_kernel(
    place, s0, s1, s2, s3, z0_ref, mine, other, month,
    both_ref, z2_ref, code_ref, gram_ref, own, oth,
):
    summed = (s0[...] + s1[...]) + (s2[...] + s3[...])
    core = place[4]
    half = pl.multiple_of(core * 128, 128)
    rest = pl.multiple_of(128 - core * 128, 128)
    for p in range(16):
        own[p * 16 : p * 16 + 16, :] = mine[p * 24 : p * 24 + 16, :]
        oth[p * 16 : p * 16 + 16, :] = other[p * 24 : p * 24 + 16, :]
        gram_ref[pl.ds(half + p * 8, 8), :] = mine[p * 24 + 16 : p * 24 + 24, :]
        gram_ref[pl.ds(rest + p * 8, 8), :] = other[p * 24 + 16 : p * 24 + 24, :]
    mf = month[...]
    diagonal = jnp.sum(gram_ref[...] * eye(R), axis=0, keepdims=True)
    rho_total = total(jnp.sum(mf * mf, axis=0, keepdims=True) * diagonal) * (1.0 / R)
    a = own[...]
    b = oth[...]
    plain = jnp.where(core == 0, a, b)
    square = jnp.where(core == 0, b, a)
    z0 = z0_ref[...]
    first = summed[0:SHARE] + dot6(z0, plain)
    z1 = jnp.maximum(first / rho_total, 0.0)
    second = summed[SHARE:] + dot6(z0, plain - square) + 2.0 * dot6(z1, plain) - rho_total * z1
    z2 = jnp.maximum(second / rho_total, 0.0)
    both_ref[0:SHARE, :] = z0
    both_ref[SHARE:, :] = z1
    z2_ref[...] = z2
    code_ref[...] = gram_of(z2, lax.Precision.HIGHEST)


def month_kernel(place, w0, w1, w2, w3, prod, code, out, natural):
    for k, w in enumerate((w0, w1, w2, w3)):
        for b in range(16):
            natural[pl.ds(block_row(place, k, b), SHARE), :] = w[b * SHARE : (b + 1) * SHARE, :]
    for p in range(16):
        out[p * 24 : p * 24 + 8, :] = jnp.zeros((8, R), F32)
        out[p * 24 + 8 : p * 24 + 24, :] = code[p * 16 : p * 16 + 16, :]

    def visit(k, _):
        at = pl.ds(pl.multiple_of(place[8 + CAP + k] * BLOCK, BLOCK), BLOCK)
        column = jnp.sum(prod[k] * natural[at, :], axis=0, keepdims=True)
        m = place[8 + 2 * CAP + k]
        out[pl.ds((m // 8) * 24 + m % 8, 1), :] += column
        return 0

    lax.fori_loop(0, place[7], visit, 0)


def duals_kernel(place, *refs):
    parts, both, two = refs[0:4], refs[4:8], refs[8:12]
    near, rho_ref, out, v_part, z0_part, z1_part = refs[12:]
    scale = 1.0 / rho_ref[0:1, 0:1]
    near_parts = split(near[...])

    def chunk(k, _):
        for n in range(4):

            @pl.when(k == n)
            def _(n=n):
                for b in range(16):
                    rows = pl.ds(b * SHARE, SHARE)
                    v_part[rows, :] = scale * parts[n][b * 80 + SHARE : b * 80 + 80, :] - two[n][rows, :]
                    z0_part[rows, :] = both[n][b * 80 : b * 80 + SHARE, :]
                    z1_part[rows, :] = both[n][b * 80 + SHARE : b * 80 + 80, :]

        z0 = z0_part[...]
        z1 = z1_part[...]
        inner = z0 - dot3(split(z0), near_parts) + 2.0 * z1
        v_part[...] = v_part[...] + dot3(split(inner), near_parts) - z1
        for b in range(16):
            out[pl.ds(block_row(place, k, b), SHARE), :] = v_part[b * SHARE : (b + 1) * SHARE, :]
        return 0

    lax.fori_loop(0, 4, chunk, 0)


def tail_kernel(sums, gram, month, out, mat, near, grad):
    for p in range(16):
        grad[p * 8 : p * 8 + 8, :] = sums[p * 24 : p * 24 + 8, :]
        mat[p * 16 : p * 16 + 16, :] = sums[p * 24 + 8 : p * 24 + 24, :]
    rho = shifted_inverse(gram[...] * mat[...], mat, near)
    scaled = grad[0:MONTHS, :] * (1.0 / rho) + month[...]
    solved = jnp.maximum(dot6(scaled, near[...]), 0.0)
    mean = jnp.sum(solved, axis=0, keepdims=True) * (1.0 / MONTHS)
    out[...] = solved / (mean + 1e-06)


def call(body, outs, spaces, scratch, *args, limit=48 << 20):
    n = len(args)
    space = {"s": pltpu.SMEM, "h": pltpu.HBM, "v": pltpu.VMEM}
    return pl.pallas_call(
        body,
        out_shape=[jax.ShapeDtypeStruct(s, F32) for s in outs],
        in_specs=[pl.BlockSpec(memory_space=space[c]) for c in spaces[:n]],
        out_specs=[pl.BlockSpec(memory_space=space[c]) for c in spaces[n:]],
        scratch_shapes=[pltpu.VMEM(s, F32) if isinstance(s, tuple) else s for s in scratch],
        compiler_params=pltpu.CompilerParams(vmem_limit_bytes=limit),
    )(*args)


def on_device(
    tile_values, patient_block, code_block, month_index, live_count,
    patient_factor, month_factor, consensus, scaled_duals,
):
    z, y, x, h, core = [lax.axis_index(a) for a in AXES]
    flat = core == 0
    place = jnp.stack(
        [jnp.where(flat, x, y), jnp.where(flat, y, x), z, h, core,
         jnp.where(flat, 1, 4), jnp.where(flat, 4, 1), live_count[0]]
    ).astype(jnp.int32)
    place = jnp.concatenate([place, patient_block, code_block, month_index])

    near, rho, weights, prod, *parts = call(
        head_kernel,
        [(R, R), (8, 128), (384, R), (CAP, BLOCK, R)] + [(2 * CHUNK, R)] * 4,
        "shhhh" + "vvvhhhhh",
        [
            pltpu.VMEM((1024, R), BF16), (MONTHS, R), pltpu.VMEM((CAP, BLOCK, BLOCK), BF16),
            (ROWS, R), (CAP, BLOCK, R), (R, R), (R, R), (ROWS, R), (CHUNK, R), (CHUNK, R),
            (4, 2 * CHUNK, R), pltpu.SemaphoreType.DMA((4,)), pltpu.SemaphoreType.DMA((5,)),
        ],
        place, patient_factor, month_factor, tile_values, scaled_duals, limit=None,
    )
    with jax.named_scope("rs_first"):
        s = scatter_sum(parts, first_move)
    with jax.named_scope("weights_plane"):
        m = sum_slices(weights, PLANE)
    m = sum_to_all(m, 4, "z")
    mine = spread_slices(m, PLANE)
    other = send(mine, CORE_MOVE)
    s = [
        (s[0][j : j + 320] + s[1][j : j + 320]) + (s[2][j : j + 320] + s[3][j : j + 320])
        for j in (0, 320, 640, 960)
    ]
    s = scatter_sum(s, second_move)
    s = [
        (s[0][i : i + 80] + s[1][i : i + 80]) + (s[2][i : i + 80] + s[3][i : i + 80])
        for i in (0, 80, 160, 240)
    ]
    s = scatter_sum(s, depth_move)
    both, z2, code_gram, gram = call(
        owner_kernel, [(2 * SHARE, R), (SHARE, R), (R, R), (R, R)], "svvvvvvvv" + "vvvv", [(R, R), (R, R)],
        place, *s, consensus, mine, other, month_factor,
    )
    two = gather_rows(z2, "two")
    both = gather_rows(both, "both")
    (sums,) = call(
        month_kernel, [(384, R)], "svvvvvv" + "v", [(ROWS, R)],
        place, *two, prod, code_gram,
    )
    t = sum_slices(sums, PLANE)
    t = sum_to_all(t, 16, COLUMN)
    t = spread_slices(t, PLANE)
    (duals,) = call(
        duals_kernel, [(ROWS, R)], "s" + "v" * 15, [(CHUNK, R)] * 3,
        place, *parts, *both, *two, near, rho,
    )
    (new_months,) = call(
        tail_kernel, [(MONTHS, R)], "vvvv", [(R, R), (R, R), (BLOCK, R)], t, gram, month_factor
    )
    return (z2, duals, new_months)


def solution(mesh):
    mesh = Mesh(mesh.devices.reshape(4, 4, 4, 2, 2), AXES)
    site, cons = ("z", "y", "x"), ("h", "c")
    every = site + cons
    placed = (
        P(every, None, None), P(every), P(every), P(every), P(every),
        P(site, None), P(), P(site, cons), P(site, cons),
    )
    return jax.shard_map(
        on_device,
        mesh=mesh,
        in_specs=placed,
        out_specs=(P(site, cons), P(site, cons), P()),
        check_vma=False,
    )
```

```python
import functools

import jax
import jax.numpy as jnp
from jax import lax
from jax.experimental import pallas as pl
from jax.experimental.pallas import tpu as pltpu
from jax.sharding import Mesh
from jax.sharding import PartitionSpec as P


R = 256
MONTHS = 120
BLOCK = 128
SHARE = 40
CHUNK = 640
ROWS = 2560
CAP = 20
F32 = jnp.float32
BF16 = jnp.bfloat16
AXES = ("z", "y", "x", "h", "c")
PLANE = ("y", "x")
COLUMN = ("z", "h", "c")


def number(z, y, x, h, c):
    return ((z * 4 + y) * 4 + x) * 4 + h * 2 + c


def pairs_of(move):
    out = []
    for z in range(4):
        for y in range(4):
            for x in range(4):
                for h in range(2):
                    for c in range(2):
                        out.append((number(z, y, x, h, c), number(*move(z, y, x, h, c))))
    return out


def first_move(k):
    def move(z, y, x, h, c):
        return (z, y, (x + k) % 4, h, c) if c == 0 else (z, (y + k) % 4, x, h, c)

    return pairs_of(move)


def second_move(k):
    def move(z, y, x, h, c):
        return (z, (y + k) % 4, x, h, c) if c == 0 else (z, y, (x + k) % 4, h, c)

    return pairs_of(move)


def depth_move(k):
    return pairs_of(lambda z, y, x, h, c: ((z + k) % 4, y, x, h, c))


CORE_MOVE = pairs_of(lambda z, y, x, h, c: (z, y, x, h, 1 - c))


def send(value, pairs):
    return lax.ppermute(value, AXES, pairs)


def scatter_sum(parts, moves):
    return [parts[0]] + [send(parts[k], moves(k)) for k in (1, 2, 3)]


def gather(value, moves):
    return [value] + [send(value, moves((4 - k) % 4)) for k in (1, 2, 3)]


def gather_rows(own):
    rows = jnp.concatenate(gather(own, depth_move), 0)
    rows = jnp.concatenate(gather(rows, second_move), 0)
    return gather(rows, first_move)


def exchange(value, axes):
    return lax.all_to_all(value, axes, 0, 0, tiled=True)


def sum_to_all(value, count, axes):
    return jnp.sum(exchange(jnp.broadcast_to(value, (count, *value.shape)), axes), axis=0)


def sum_slices(value, axes):
    return jnp.sum(exchange(value.reshape(16, -1, R), axes), axis=0)


def spread_slices(value, axes):
    return exchange(jnp.broadcast_to(value, (16, *value.shape)), axes).reshape(-1, R)


def split(a):
    hi = a.astype(BF16)
    return hi, (a - hi.astype(F32)).astype(BF16)


def dot3(a, b):
    ah, al = a
    bh, bl = b
    dot = functools.partial(jnp.dot, preferred_element_type=F32)
    return dot(ah, bh) + (dot(ah, bl) + dot(al, bh))


def dot6(a, b):
    return jnp.dot(a, b, precision=lax.Precision.HIGHEST, preferred_element_type=F32)


def gram_of(a, precision=None):
    return lax.dot_general(
        a, a, (((0,), (0,)), ((), ())), precision=precision, preferred_element_type=F32
    )


def eye(n):
    return (
        lax.broadcasted_iota(jnp.int32, (n, n), 0) == lax.broadcasted_iota(jnp.int32, (n, n), 1)
    ).astype(F32)


def total(a):
    return jnp.sum(jnp.sum(a, axis=1, keepdims=True), axis=0, keepdims=True)


def shifted_inverse(hess, mat_ref, x_ref):
    n = hess.shape[0]
    ident = eye(n)
    rho = total(hess * ident) * (1.0 / n)
    mat = hess * (1.0 / rho) + ident
    mat_ref[...] = mat
    mat_parts = split(mat)
    low, high = 0.999, n + 1.5
    c0 = 2.0 / (low + high)

    def grow(a):
        up = a * (2.0 - a)
        s = 2.0 / (1.0 + up)
        return s, s * up

    s, a = grow(low * c0)
    x_ref[...] = (s * c0) * (2.0 * ident - c0 * mat)

    def coarse(_, a):
        s, a = grow(a)
        x_parts = split(x_ref[...])
        y = 2.0 * ident - dot3(mat_parts, x_parts)
        x_ref[...] = s * dot3(x_parts, split(y))
        return a

    lax.fori_loop(0, 5, coarse, jnp.float32(a))

    def fine(_, carry):
        x = x_ref[...]
        x_ref[...] = dot6(x, 2.0 * ident - dot6(mat_ref[...], x))
        return carry

    lax.fori_loop(0, 2, fine, 0)
    return rho


STEP = 1.0 / 128.0
ROOM = 14.98


def encode(block):
    top = jnp.max(jnp.abs(block), axis=0, keepdims=True)
    code = jnp.ceil(jnp.log2(jnp.maximum(top, 1e-30)) * 128.0)
    return jnp.round(block * jnp.exp2(ROOM - code * STEP)), code


def decode(whole, code):
    return whole * jnp.exp2(code * STEP - ROOM)


def to_codes(a):
    return a.astype(jnp.int32).astype(jnp.int16)


def from_codes(a):
    return a.astype(jnp.int32).astype(F32)


def block_row(place, k, b):
    j, i = b // 4, b % 4
    first = lax.rem(place[0] + k, 4)
    second = lax.rem(place[1] + j, 4)
    depth = lax.rem(place[2] + i, 4)
    block = depth * 16 + first * place[5] + second * place[6]
    return pl.multiple_of(block * SHARE, 8)


def inverse_kernel(place, patient, month, near, rho_ref, weights, mat, square):
    month_gram = gram_of(month[...], lax.Precision.HIGHEST)
    gram = gram_of(patient[...])
    rho = shifted_inverse(gram * month_gram, mat, near)
    rho_ref[...] = jnp.broadcast_to(rho, rho_ref.shape)
    core = place[4]
    mat[...] = near[...]

    @pl.when(core == 1)
    def _():
        mat[...] = dot6(near[...], near[...])

    square[...] = gram
    half = pl.multiple_of(core * 128, 128)
    for p in range(16):
        weights[p * 24 : p * 24 + 16, :] = rho * mat[p * 16 : p * 16 + 16, :]
        weights[p * 24 + 16 : p * 24 + 24, :] = square[pl.ds(half + p * 8, 8), :]


def local_kernel(
    place, near, rho_ref, patient_hbm, month_hbm, tiles_hbm, duals_hbm,
    prod_hbm, v_hbm, a0, q1, q2, q3,
    patient, month, tiles, duals, prod, grad, u_part, g_part, v, own, coded, held, sems, outs,
):
    copies = [
        pltpu.make_async_copy(src, dst, sems.at[n])
        for n, (src, dst) in enumerate(
            [
                (month_hbm, month), (patient_hbm, patient), (tiles_hbm, tiles), (duals_hbm, duals),
            ]
        )
    ]
    for copy in copies:
        copy.start()
    rho = rho_ref[0:1, 0:1]
    grad[...] = jnp.zeros_like(grad)
    for copy in copies[:3]:
        copy.wait()

    def visit(k, _):
        pat = patient[pl.ds(pl.multiple_of(place[8 + k] * BLOCK, BLOCK), BLOCK), :]
        product = lax.dot_general(
            tiles[k], pat, (((0,), (0,)), ((), ())), preferred_element_type=F32
        )
        prod[k] = product
        at = pl.ds(pl.multiple_of(place[8 + CAP + k] * BLOCK, BLOCK), BLOCK)
        grad[at, :] += product * month[pl.ds(place[8 + 2 * CAP + k], 1), :]
        return 0

    lax.fori_loop(0, place[7], visit, 0)
    prod_out = pltpu.make_async_copy(prod, prod_hbm, outs.at[4])
    prod_out.start()
    near_parts = split(near[...])
    copies[3].wait()

    def chunk(step, _):
        k = lax.rem(step + 1, 4)
        for b in range(16):
            at = pl.ds(block_row(place, k, b), SHARE)
            u_part[b * SHARE : (b + 1) * SHARE, :] = duals[at, :]
            g_part[b * SHARE : (b + 1) * SHARE, :] = grad[at, :]
        u = u_part[...]
        g = g_part[...] * (1.0 / rho)
        once = u + dot3(split(g - u), near_parts)
        twice = once + dot3(split(g - once), near_parts)
        v[k] = twice
        u_part[...] = rho * once
        g_part[...] = rho * twice

        @pl.when(k > 0)
        def _():
            for b in range(16):
                for q, part in enumerate((u_part, g_part)):
                    whole, code = encode(part[b * SHARE : (b + 1) * SHARE, :])
                    row = b * 80 + q * SHARE
                    coded[row : row + SHARE, :] = whole
                    coded[1280 + 2 * b + q : 1281 + 2 * b + q, :] = code
            held[k - 1] = to_codes(coded[...])

        for n, out in enumerate((q1, q2, q3)):

            @pl.when(k == n + 1)
            def _(n=n, out=out):
                pltpu.make_async_copy(held.at[n], out, outs.at[n]).start()

        return 0

    lax.fori_loop(0, 4, chunk, 0)
    for b in range(16):
        own[b * 80 : b * 80 + SHARE, :] = u_part[b * SHARE : (b + 1) * SHARE, :]
        own[b * 80 + SHARE : b * 80 + 80, :] = g_part[b * SHARE : (b + 1) * SHARE, :]
    own_out = pltpu.make_async_copy(own, a0, outs.at[3])
    own_out.start()
    v_out = pltpu.make_async_copy(v, v_hbm, outs.at[5])
    v_out.start()
    for n, out in enumerate((q1, q2, q3)):
        pltpu.make_async_copy(held.at[n], out, outs.at[n]).wait()
    prod_out.wait()
    own_out.wait()
    v_out.wait()


def sum_kernel(a0, r1, r2, r3, s0, s1, s2, s3, acc, part):
    acc[...] = a0[...]
    for r in (r1, r2, r3):
        part[...] = from_codes(r[...])
        for b in range(32):
            acc[b * SHARE : (b + 1) * SHARE, :] += decode(
                part[b * SHARE : (b + 1) * SHARE, :], part[1280 + b : 1281 + b, :]
            )
    for j, out in enumerate((s0, s1, s2, s3)):
        out[...] = acc[j * 320 : j * 320 + 320, :]


def owner_kernel(
    place, s0, s1, s2, s3, z0_ref, mine, other, month,
    both_ref, two_ref, z2_ref, code_ref, gram_ref, own, oth, both, two,
):
    summed = (s0[...] + s1[...]) + (s2[...] + s3[...])
    core = place[4]
    half = pl.multiple_of(core * 128, 128)
    rest = pl.multiple_of(128 - core * 128, 128)
    for p in range(16):
        own[p * 16 : p * 16 + 16, :] = mine[p * 24 : p * 24 + 16, :]
        oth[p * 16 : p * 16 + 16, :] = other[p * 24 : p * 24 + 16, :]
        gram_ref[pl.ds(half + p * 8, 8), :] = mine[p * 24 + 16 : p * 24 + 24, :]
        gram_ref[pl.ds(rest + p * 8, 8), :] = other[p * 24 + 16 : p * 24 + 24, :]
    mf = month[...]
    diagonal = jnp.sum(gram_ref[...] * eye(R), axis=0, keepdims=True)
    rho_total = total(jnp.sum(mf * mf, axis=0, keepdims=True) * diagonal) * (1.0 / R)
    a = own[...]
    b = oth[...]
    plain = jnp.where(core == 0, a, b)
    square = jnp.where(core == 0, b, a)
    z0 = z0_ref[...]
    first = summed[0:SHARE] + dot6(z0, plain)
    z1 = jnp.maximum(first / rho_total, 0.0)
    second = summed[SHARE:] + dot6(z0, plain - square) + 2.0 * dot6(z1, plain) - rho_total * z1
    z2 = jnp.maximum(second / rho_total, 0.0)
    both[...] = jnp.zeros_like(both)
    two[...] = jnp.zeros_like(two)
    both[0:SHARE, :], both[80:81, :] = encode(z0)
    both[SHARE:80, :], both[81:82, :] = encode(z1)
    two[0:SHARE, :], two[SHARE : SHARE + 1, :] = encode(z2)
    both_ref[...] = to_codes(both[...])
    two_ref[...] = to_codes(two[...])
    z2_ref[...] = z2
    code_ref[...] = gram_of(z2, lax.Precision.HIGHEST)


def month_kernel(place, w0, w1, w2, w3, prod, code, out, natural, part):
    for k, w in enumerate((w0, w1, w2, w3)):
        part[...] = from_codes(w[...])
        for b in range(16):
            natural[pl.ds(block_row(place, k, b), SHARE), :] = decode(
                part[b * 48 : b * 48 + SHARE, :], part[b * 48 + SHARE : b * 48 + SHARE + 1, :]
            )
    for p in range(16):
        out[p * 24 : p * 24 + 8, :] = jnp.zeros((8, R), F32)
        out[p * 24 + 8 : p * 24 + 24, :] = code[p * 16 : p * 16 + 16, :]

    def visit(k, _):
        at = pl.ds(pl.multiple_of(place[8 + CAP + k] * BLOCK, BLOCK), BLOCK)
        column = jnp.sum(prod[k] * natural[at, :], axis=0, keepdims=True)
        m = place[8 + 2 * CAP + k]
        out[pl.ds((m // 8) * 24 + m % 8, 1), :] += column
        return 0

    lax.fori_loop(0, place[7], visit, 0)


def duals_kernel(place, *refs):
    both, two = refs[0:4], refs[4:8]
    v, near, _, out, part, z0_part, z1_part, z2_part = refs[8:]
    near_parts = split(near[...])

    def chunk(k, _):
        for n in range(4):

            @pl.when(k == n)
            def _(n=n):
                part[0:1536, :] = from_codes(both[n][...])
                part[1536:, :] = from_codes(two[n][...])

        for b in range(16):
            rows = slice(b * SHARE, (b + 1) * SHARE)
            at = b * 96
            z0_part[rows, :] = decode(part[at : at + 40, :], part[at + 80 : at + 81, :])
            z1_part[rows, :] = decode(part[at + 40 : at + 80, :], part[at + 81 : at + 82, :])
            at = 1536 + b * 48
            z2_part[rows, :] = decode(part[at : at + 40, :], part[at + 40 : at + 41, :])
        z0 = z0_part[...]
        z1 = z1_part[...]
        inner = z0 - dot3(split(z0), near_parts) + 2.0 * z1
        z2_part[...] = v[k] + dot3(split(inner), near_parts) - z1 - z2_part[...]
        for b in range(16):
            out[pl.ds(block_row(place, k, b), SHARE), :] = z2_part[b * SHARE : (b + 1) * SHARE, :]
        return 0

    lax.fori_loop(0, 4, chunk, 0)


def tail_kernel(sums, gram, month, out, mat, near, grad):
    for p in range(16):
        grad[p * 8 : p * 8 + 8, :] = sums[p * 24 : p * 24 + 8, :]
        mat[p * 16 : p * 16 + 16, :] = sums[p * 24 + 8 : p * 24 + 24, :]
    rho = shifted_inverse(gram[...] * mat[...], mat, near)
    scaled = grad[0:MONTHS, :] * (1.0 / rho) + month[...]
    solved = jnp.maximum(dot6(scaled, near[...]), 0.0)
    mean = jnp.sum(solved, axis=0, keepdims=True) * (1.0 / MONTHS)
    out[...] = solved / (mean + 1e-06)


def call(body, outs, spaces, scratch, *args, limit=48 << 20):
    n = len(args)
    space = {"s": pltpu.SMEM, "h": pltpu.HBM, "v": pltpu.VMEM}
    return pl.pallas_call(
        body,
        out_shape=[s if isinstance(s, jax.ShapeDtypeStruct) else jax.ShapeDtypeStruct(s, F32) for s in outs],
        in_specs=[pl.BlockSpec(memory_space=space[c]) for c in spaces[:n]],
        out_specs=[pl.BlockSpec(memory_space=space[c]) for c in spaces[n:]],
        scratch_shapes=[pltpu.VMEM(s, F32) if isinstance(s, tuple) else s for s in scratch],
        compiler_params=pltpu.CompilerParams(vmem_limit_bytes=limit),
    )(*args)


def compute(
    tile_values, patient_block, code_block, month_index, live_count,
    patient_factor, month_factor, consensus, scaled_duals,
):
    z, y, x, h, core = [lax.axis_index(a) for a in AXES]
    flat = core == 0
    place = jnp.stack(
        [jnp.where(flat, x, y), jnp.where(flat, y, x), z, h, core,
         jnp.where(flat, 1, 4), jnp.where(flat, 4, 1), live_count[0]]
    ).astype(jnp.int32)
    place = jnp.concatenate([place, patient_block, code_block, month_index])

    near, rho, weights = call(
        inverse_kernel, [(R, R), (8, 128), (384, R)], "svv" + "vvv", [(R, R), (R, R)],
        place, patient_factor, month_factor, limit=None,
    )
    m = sum_slices(weights, PLANE)
    codes = [jax.ShapeDtypeStruct((1312, R), jnp.int16)] * 3
    prod, v, *parts = call(
        local_kernel,
        [(CAP, BLOCK, R), (4, CHUNK, R), (2 * CHUNK, R)] + codes,
        "svvhhhh" + "hhhhhh",
        [
            pltpu.VMEM((1024, R), BF16), (MONTHS, R), pltpu.VMEM((CAP, BLOCK, BLOCK), BF16),
            (ROWS, R), (CAP, BLOCK, R), (ROWS, R), (CHUNK, R), (CHUNK, R), (4, CHUNK, R),
            (2 * CHUNK, R), (1312, R), pltpu.VMEM((3, 1312, R), jnp.int16),
            pltpu.SemaphoreType.DMA((4,)), pltpu.SemaphoreType.DMA((6,)),
        ],
        place, near, rho, patient_factor, month_factor, tile_values, scaled_duals, limit=None,
    )
    s = scatter_sum(parts, first_move)
    m = sum_to_all(m, 4, "z")
    mine = spread_slices(m, PLANE)
    other = send(mine, CORE_MOVE)
    s = call(sum_kernel, [(320, R)] * 4, "vvvv" + "vvvv", [(2 * CHUNK, R), (1312, R)], *s)
    s = scatter_sum(s, second_move)
    s = [
        (s[0][i : i + 80] + s[1][i : i + 80]) + (s[2][i : i + 80] + s[3][i : i + 80])
        for i in (0, 80, 160, 240)
    ]
    s = scatter_sum(s, depth_move)
    both, two, z2, code_gram, gram = call(
        owner_kernel,
        [jax.ShapeDtypeStruct((96, R), jnp.int16), jax.ShapeDtypeStruct((48, R), jnp.int16),
         (SHARE, R), (R, R), (R, R)],
        "svvvvvvvv" + "vvvvv", [(R, R), (R, R), (96, R), (48, R)],
        place, *s, consensus, mine, other, month_factor,
    )
    two = gather_rows(two)
    both = gather_rows(both)
    (sums,) = call(
        month_kernel, [(384, R)], "svvvvvv" + "v", [(ROWS, R), (768, R)],
        place, *two, prod, code_gram,
    )
    t = sum_slices(sums, PLANE)
    t = sum_to_all(t, 16, COLUMN)
    t = spread_slices(t, PLANE)
    (duals,) = call(
        duals_kernel, [(ROWS, R)], "s" + "v" * 12, [(2304, R)] + [(CHUNK, R)] * 3,
        place, *both, *two, v, near, rho,
    )
    (new_months,) = call(
        tail_kernel, [(MONTHS, R)], "vvvv", [(R, R), (R, R), (BLOCK, R)], t, gram, month_factor
    )
    return (z2, duals, new_months)


def solution(mesh):
    mesh = Mesh(mesh.devices.reshape(4, 4, 4, 2, 2), AXES)
    site, cons = ("z", "y", "x"), ("h", "c")
    every = site + cons
    placed = (
        P(every, None, None), P(every), P(every), P(every), P(every),
        P(site, None), P(), P(site, cons), P(site, cons),
    )
    return jax.shard_map(
        compute,
        mesh=mesh,
        in_specs=placed,
        out_specs=(P(site, cons), P(site, cons), P()),
        check_vma=False,
    )
```

```python
import functools

import jax
import jax.numpy as jnp
from jax import lax
from jax.experimental import pallas as pl
from jax.experimental.pallas import tpu as pltpu
from jax.sharding import Mesh
from jax.sharding import PartitionSpec as P


R = 256
MONTHS = 120
BLOCK = 128
SHARE = 40
CHUNK = 640
ROWS = 2560
CAP = 20
F32 = jnp.float32
BF16 = jnp.bfloat16
AXES = ("z", "y", "x", "h", "c")
PLANE = ("y", "x")


def number(z, y, x, h, c):
    return ((z * 4 + y) * 4 + x) * 4 + h * 2 + c


def pairs_of(move):
    out = []
    for z in range(4):
        for y in range(4):
            for x in range(4):
                for h in range(2):
                    for c in range(2):
                        out.append((number(z, y, x, h, c), number(*move(z, y, x, h, c))))
    return out


def first_move(k):
    def move(z, y, x, h, c):
        return (z, y, (x + k) % 4, h, c) if c == 0 else (z, (y + k) % 4, x, h, c)

    return pairs_of(move)


def second_move(k):
    def move(z, y, x, h, c):
        return (z, (y + k) % 4, x, h, c) if c == 0 else (z, y, (x + k) % 4, h, c)

    return pairs_of(move)


def depth_move(k):
    return pairs_of(lambda z, y, x, h, c: ((z + k) % 4, y, x, h, c))


CORE_MOVE = pairs_of(lambda z, y, x, h, c: (z, y, x, h, 1 - c))


def send(value, pairs):
    return lax.ppermute(value, AXES, pairs)


def scatter_sum(parts, moves):
    return [parts[0]] + [send(parts[k], moves(k)) for k in (1, 2, 3)]


def gather(value, moves):
    return [value] + [send(value, moves((4 - k) % 4)) for k in (1, 2, 3)]


def exchange(value, axes):
    return lax.all_to_all(value, axes, 0, 0, tiled=True)


def sum_to_all(value, count, axes):
    return jnp.sum(exchange(jnp.broadcast_to(value, (count, *value.shape)), axes), axis=0)


def sum_slices(value, axes):
    return jnp.sum(exchange(value.reshape(16, -1, R), axes), axis=0)


def spread_slices(value, axes):
    return exchange(jnp.broadcast_to(value, (16, *value.shape)), axes).reshape(-1, R)


def split(a):
    hi = a.astype(BF16)
    return hi, (a - hi.astype(F32)).astype(BF16)


def dot3(a, b):
    ah, al = a
    bh, bl = b
    dot = functools.partial(jnp.dot, preferred_element_type=F32)
    return dot(ah, bh) + (dot(ah, bl) + dot(al, bh))


def dot6(a, b):
    return jnp.dot(a, b, precision=lax.Precision.HIGHEST, preferred_element_type=F32)


def gram_of(a, precision=None):
    return lax.dot_general(
        a, a, (((0,), (0,)), ((), ())), precision=precision, preferred_element_type=F32
    )


def eye(n):
    return (
        lax.broadcasted_iota(jnp.int32, (n, n), 0) == lax.broadcasted_iota(jnp.int32, (n, n), 1)
    ).astype(F32)


def total(a):
    return jnp.sum(jnp.sum(a, axis=1, keepdims=True), axis=0, keepdims=True)


def shifted_inverse(hess, mat_ref, x_ref):
    n = hess.shape[0]
    ident = eye(n)
    rho = total(hess * ident) * (1.0 / n)
    mat = hess * (1.0 / rho) + ident
    mat_ref[...] = mat
    mat_parts = split(mat)
    low, high = 0.999, n + 1.5
    c0 = 2.0 / (low + high)

    def grow(a):
        up = a * (2.0 - a)
        s = 2.0 / (1.0 + up)
        return s, s * up

    s, a = grow(low * c0)
    x_ref[...] = (s * c0) * (2.0 * ident - c0 * mat)

    def coarse(_, a):
        s, a = grow(a)
        x_parts = split(x_ref[...])
        y = 2.0 * ident - dot3(mat_parts, x_parts)
        x_ref[...] = s * dot3(x_parts, split(y))
        return a

    lax.fori_loop(0, 5, coarse, jnp.float32(a))
    x = x_ref[...]
    x_ref[...] = dot6(x, 2.0 * ident - dot6(mat_ref[...], x))
    return rho


STEP = 1.0 / 128.0
ROOM = 14.98


def encode(block):
    top = jnp.max(jnp.abs(block), axis=0, keepdims=True)
    code = jnp.ceil(jnp.log2(jnp.maximum(top, 1e-30)) * 128.0)
    return jnp.round(block * jnp.exp2(ROOM - code * STEP)), code


def decode(whole, code):
    return whole * jnp.exp2(code * STEP - ROOM)


def to_codes(a):
    return a.astype(jnp.int32).astype(jnp.int16)


def from_codes(a):
    return a.astype(jnp.int32).astype(F32)


def placed():
    z, y, x, _, core = [lax.axis_index(a) for a in AXES]
    flat = core == 0
    return (
        jnp.where(flat, x, y), jnp.where(flat, y, x), z, core,
        jnp.where(flat, 1, 4), jnp.where(flat, 4, 1),
    )


def block_row(place, k, b):
    j, i = b // 4, b % 4
    first = lax.rem(place[0] + k, 4)
    second = lax.rem(place[1] + j, 4)
    depth = lax.rem(place[2] + i, 4)
    block = depth * 16 + first * place[4] + second * place[5]
    return pl.multiple_of(block * SHARE, 8)


def coded_rows(blocks):
    return -(-blocks * (SHARE + 1) // 16) * 16


def encode_blocks(source, first, blocks, coded, out):
    coded[blocks * SHARE :, :] = jnp.zeros((coded.shape[0] - blocks * SHARE, R), F32)
    for b in range(blocks):
        whole, code = encode(source[(first + b) * SHARE : (first + b + 1) * SHARE, :])
        coded[b * SHARE : (b + 1) * SHARE, :] = whole
        coded[blocks * SHARE + b : blocks * SHARE + b + 1, :] = code
    out[...] = to_codes(coded[...])


def add_blocks(acc, blocks, part, r):
    part[...] = from_codes(r[...])
    for b in range(blocks):
        acc[b * SHARE : (b + 1) * SHARE, :] += decode(
            part[b * SHARE : (b + 1) * SHARE, :],
            part[blocks * SHARE + b : blocks * SHARE + b + 1, :],
        )


def inverse_kernel(patient, month, near, rho_ref, weights, mat, square):
    month_gram = gram_of(month[...], lax.Precision.HIGHEST)
    gram = gram_of(patient[...])
    rho = shifted_inverse(gram * month_gram, mat, near)
    rho_ref[...] = jnp.broadcast_to(rho, rho_ref.shape)
    core = placed()[3]
    mat[...] = near[...]

    @pl.when(core == 1)
    def _():
        mat[...] = dot6(near[...], near[...])

    square[...] = gram
    half = pl.multiple_of(core * 128, 128)
    for p in range(16):
        weights[p * 24 : p * 24 + 16, :] = rho * mat[p * 16 : p * 16 + 16, :]
        weights[p * 24 + 16 : p * 24 + 24, :] = square[pl.ds(half + p * 8, 8), :]


def local_kernel(
    live, patient_at, code_at, month_at, near, rho_ref, patient_hbm, month_hbm, tiles_hbm, duals_hbm,
    prod_hbm, v_hbm, a0, q1, q2, q3,
    patient, month, tiles, duals, prod, grad, u_part, g_part, v, own, coded, held, sems, outs,
):
    copies = [
        pltpu.make_async_copy(src, dst, sems.at[n])
        for n, (src, dst) in enumerate(
            [
                (month_hbm, month), (patient_hbm, patient), (tiles_hbm, tiles), (duals_hbm, duals),
            ]
        )
    ]
    for copy in copies:
        copy.start()
    rho = rho_ref[0:1, 0:1]
    place = placed()
    grad[...] = jnp.zeros_like(grad)
    for copy in copies[:3]:
        copy.wait()

    def visit(turn, _):
        for k in [turn * 4 + n for n in range(4)]:
            pat = patient[pl.ds(pl.multiple_of(patient_at[k] * BLOCK, BLOCK), BLOCK), :]
            prod[k] = lax.dot_general(
                tiles[k], pat, (((0,), (0,)), ((), ())), preferred_element_type=F32
            )
        for k in [turn * 4 + n for n in range(4)]:
            scale = jnp.where(k < live[0], month[pl.ds(month_at[k], 1), :], 0.0)
            at = pl.ds(pl.multiple_of(code_at[k] * BLOCK, BLOCK), BLOCK)
            grad[at, :] += prod[k] * scale
        return 0

    lax.fori_loop(0, (live[0] + 3) // 4, visit, 0)
    prod_out = pltpu.make_async_copy(prod, prod_hbm, outs.at[4])
    prod_out.start()
    near_parts = split(near[...])
    copies[3].wait()

    def chunk(step, _):
        k = lax.rem(step + 1, 4)
        for b in range(16):
            at = pl.ds(block_row(place, k, b), SHARE)
            u_part[b * SHARE : (b + 1) * SHARE, :] = duals[at, :]
            g_part[b * SHARE : (b + 1) * SHARE, :] = grad[at, :]
        u = u_part[...]
        g = g_part[...] * (1.0 / rho)
        once = u + dot3(split(g - u), near_parts)
        twice = once + dot3(split(g - once), near_parts)
        v[k] = twice
        u_part[...] = rho * once
        g_part[...] = rho * twice

        @pl.when(k > 0)
        def _():
            for b in range(16):
                for q, part in enumerate((u_part, g_part)):
                    whole, code = encode(part[b * SHARE : (b + 1) * SHARE, :])
                    row = b * 80 + q * SHARE
                    coded[row : row + SHARE, :] = whole
                    coded[1280 + 2 * b + q : 1281 + 2 * b + q, :] = code
            held[k - 1] = to_codes(coded[...])

        for n, out in enumerate((q1, q2, q3)):

            @pl.when(k == n + 1)
            def _(n=n, out=out):
                pltpu.make_async_copy(held.at[n], out, outs.at[n]).start()

        return 0

    lax.fori_loop(0, 4, chunk, 0)
    for b in range(16):
        own[b * 80 : b * 80 + SHARE, :] = u_part[b * SHARE : (b + 1) * SHARE, :]
        own[b * 80 + SHARE : b * 80 + 80, :] = g_part[b * SHARE : (b + 1) * SHARE, :]
    own_out = pltpu.make_async_copy(own, a0, outs.at[3])
    own_out.start()
    v_out = pltpu.make_async_copy(v, v_hbm, outs.at[5])
    v_out.start()
    for n, out in enumerate((q1, q2, q3)):
        pltpu.make_async_copy(held.at[n], out, outs.at[n]).wait()
    prod_out.wait()
    own_out.wait()
    v_out.wait()


def sum_kernel(own, r1, r2, r3, s0, q1, q2, q3, acc, part, coded):
    blocks = own.shape[0] // SHARE
    few = blocks // 4
    acc[...] = own[...]
    for r in (r1, r2, r3):
        add_blocks(acc, blocks, part, r)
    s0[...] = acc[0 : few * SHARE, :]
    for j, out in enumerate((q1, q2, q3)):
        encode_blocks(acc, (j + 1) * few, few, coded, out)


def owner_kernel(
    s0, s1, s2, s3, z0_ref, mine, other, month,
    codes_ref, z2_ref, code_ref, gram_ref, own, oth, coded, acc, part,
):
    acc[...] = s0[...]
    for r in (s1, s2, s3):
        add_blocks(acc, 2, part, r)
    summed = acc[...]
    core = placed()[3]
    half = pl.multiple_of(core * 128, 128)
    rest = pl.multiple_of(128 - core * 128, 128)
    for p in range(16):
        own[p * 16 : p * 16 + 16, :] = mine[p * 24 : p * 24 + 16, :]
        oth[p * 16 : p * 16 + 16, :] = other[p * 24 : p * 24 + 16, :]
        gram_ref[pl.ds(half + p * 8, 8), :] = mine[p * 24 + 16 : p * 24 + 24, :]
        gram_ref[pl.ds(rest + p * 8, 8), :] = other[p * 24 + 16 : p * 24 + 24, :]
    mf = month[...]
    diagonal = jnp.sum(gram_ref[...] * eye(R), axis=0, keepdims=True)
    rho_total = total(jnp.sum(mf * mf, axis=0, keepdims=True) * diagonal) * (1.0 / R)
    a = own[...]
    b = oth[...]
    plain = jnp.where(core == 0, a, b)
    square = jnp.where(core == 0, b, a)
    z0 = z0_ref[...]
    first = summed[0:SHARE] + dot6(z0, plain)
    z1 = jnp.maximum(first / rho_total, 0.0)
    second = summed[SHARE:] + dot6(z0, plain - square) + 2.0 * dot6(z1, plain) - rho_total * z1
    z2 = jnp.maximum(second / rho_total, 0.0)
    coded[...] = jnp.zeros_like(coded)
    coded[0:40, :], coded[40:41, :] = encode(z2)
    coded[48:88, :], coded[41:42, :] = encode(z0)
    coded[88:128, :], coded[42:43, :] = encode(z1)
    codes_ref[...] = to_codes(coded[...])
    z2_ref[...] = z2
    code_ref[...] = gram_of(z2, lax.Precision.HIGHEST)


def month_kernel(live, code_at, month_at, w0, w1, w2, w3, prod, code, out, natural, part):
    place = placed()
    for k, w in enumerate((w0, w1, w2, w3)):
        part[...] = from_codes(w[...])
        for b in range(16):
            natural[pl.ds(block_row(place, k, b), SHARE), :] = decode(
                part[b * 48 : b * 48 + SHARE, :], part[b * 48 + SHARE : b * 48 + SHARE + 1, :]
            )
    for p in range(16):
        out[p * 24 : p * 24 + 8, :] = jnp.zeros((8, R), F32)
        out[p * 24 + 8 : p * 24 + 24, :] = code[p * 16 : p * 16 + 16, :]

    def visit(k, _):
        at = pl.ds(pl.multiple_of(code_at[k] * BLOCK, BLOCK), BLOCK)
        column = jnp.sum(prod[k] * natural[at, :], axis=0, keepdims=True)
        m = month_at[k]
        out[pl.ds((m // 8) * 24 + m % 8, 1), :] += column
        return 0

    lax.fori_loop(0, live[0], visit, 0)


def duals_kernel(*refs):
    place = placed()
    both, two = refs[0:4], refs[4:8]
    v, near, _, out, part, z0_part, z1_part, z2_part = refs[8:]
    near_parts = split(near[...])

    def chunk(k, _):
        for n in range(4):

            @pl.when(k == n)
            def _(n=n):
                part[0:1280, :] = from_codes(both[n][...])
                part[1280:, :] = from_codes(two[n][...])

        for b in range(16):
            rows = slice(b * SHARE, (b + 1) * SHARE)
            at = b * 80
            to = 1280 + b * 48
            z0_part[rows, :] = decode(part[at : at + 40, :], part[to + 41 : to + 42, :])
            z1_part[rows, :] = decode(part[at + 40 : at + 80, :], part[to + 42 : to + 43, :])
            z2_part[rows, :] = decode(part[to : to + 40, :], part[to + 40 : to + 41, :])
        z0 = z0_part[...]
        z1 = z1_part[...]
        inner = z0 - dot3(split(z0), near_parts) + 2.0 * z1
        z2_part[...] = v[k] + dot3(split(inner), near_parts) - z1 - z2_part[...]
        for b in range(16):
            out[pl.ds(block_row(place, k, b), SHARE), :] = z2_part[b * SHARE : (b + 1) * SHARE, :]
        return 0

    lax.fori_loop(0, 4, chunk, 0)


def tail_kernel(sums, gram, month, out, mat, near, grad):
    for p in range(16):
        grad[p * 8 : p * 8 + 8, :] = sums[p * 24 : p * 24 + 8, :]
        mat[p * 16 : p * 16 + 16, :] = sums[p * 24 + 8 : p * 24 + 24, :]
    rho = shifted_inverse(gram[...] * mat[...], mat, near)
    scaled = grad[0:MONTHS, :] * (1.0 / rho) + month[...]
    solved = jnp.maximum(dot6(scaled, near[...]), 0.0)
    mean = jnp.sum(solved, axis=0, keepdims=True) * (1.0 / MONTHS)
    out[...] = solved / (mean + 1e-06)


def call(body, outs, spaces, scratch, *args, limit=48 << 20):
    n = len(args)
    space = {"s": pltpu.SMEM, "h": pltpu.HBM, "v": pltpu.VMEM}
    return pl.pallas_call(
        body,
        out_shape=[s if isinstance(s, jax.ShapeDtypeStruct) else jax.ShapeDtypeStruct(s, F32) for s in outs],
        in_specs=[pl.BlockSpec(memory_space=space[c]) for c in spaces[:n]],
        out_specs=[pl.BlockSpec(memory_space=space[c]) for c in spaces[n:]],
        scratch_shapes=[pltpu.VMEM(s, F32) if isinstance(s, tuple) else s for s in scratch],
        compiler_params=pltpu.CompilerParams(vmem_limit_bytes=limit),
    )(*args)


def compute(
    tile_values, patient_block, code_block, month_index, live_count,
    patient_factor, month_factor, consensus, scaled_duals,
):
    near, rho, weights = call(
        inverse_kernel, [(R, R), (8, 128), (384, R)], "vv" + "vvv", [(R, R), (R, R)],
        patient_factor, month_factor, limit=None,
    )
    m = sum_slices(weights, PLANE)

    def codes(rows):
        return jax.ShapeDtypeStruct((rows, R), jnp.int16)

    tops = [coded_rows(n) for n in (32, 8, 2)]
    prod, v, *s = call(
        local_kernel,
        [(CAP, BLOCK, R), (4, CHUNK, R), (2 * CHUNK, R)] + [codes(tops[0])] * 3,
        "ssssvvhhhh" + "hhhhhh",
        [
            pltpu.VMEM((1024, R), BF16), (MONTHS, R), pltpu.VMEM((CAP, BLOCK, BLOCK), BF16),
            (ROWS, R), (CAP, BLOCK, R), (ROWS, R), (CHUNK, R), (CHUNK, R), (4, CHUNK, R),
            (2 * CHUNK, R), (tops[0], R), pltpu.VMEM((3, tops[0], R), jnp.int16),
            pltpu.SemaphoreType.DMA((4,)), pltpu.SemaphoreType.DMA((6,)),
        ],
        live_count, patient_block, code_block, month_index,
        near, rho, patient_factor, month_factor, tile_values, scaled_duals, limit=None,
    )
    s = scatter_sum(s, first_move)
    m = sum_to_all(m, 4, "z")
    mine = spread_slices(m, PLANE)
    other = send(mine, CORE_MOVE)
    s = call(
        sum_kernel, [(320, R)] + [codes(tops[1])] * 3, "vvvv" + "vvvv",
        [(2 * CHUNK, R), (tops[0], R), (tops[1], R)], *s,
    )
    s = scatter_sum(s, second_move)
    s = call(
        sum_kernel, [(80, R)] + [codes(tops[2])] * 3, "vvvv" + "vvvv",
        [(320, R), (tops[1], R), (tops[2], R)], *s,
    )
    s = scatter_sum(s, depth_move)
    rows, z2, code_gram, gram = call(
        owner_kernel, [codes(128), (SHARE, R), (R, R), (R, R)], "vvvvvvvv" + "vvvv",
        [(R, R), (R, R), (128, R), (80, R), (tops[2], R)],
        *s, consensus, mine, other, month_factor,
    )
    rows = jnp.concatenate(gather(rows, depth_move), 0)
    rows = [r.reshape(4, 128, R) for r in gather(rows, second_move)]
    two = jnp.concatenate([r[:, :48].reshape(192, R) for r in rows], 0)
    both = jnp.concatenate([r[:, 48:].reshape(320, R) for r in rows], 0)
    two = gather(two, first_move)
    both = gather(both, first_move)
    (sums,) = call(
        month_kernel, [(384, R)], "sssvvvvvv" + "v", [(ROWS, R), (768, R)],
        live_count, code_block, month_index, *two, prod, code_gram,
    )
    t = sum_slices(sums, PLANE)
    t = t + send(t, CORE_MOVE)
    t = sum_to_all(t, 8, ("z", "h"))
    t = spread_slices(t, PLANE)
    (duals,) = call(
        duals_kernel, [(ROWS, R)], "v" * 12, [(2048, R)] + [(CHUNK, R)] * 3,
        *both, *two, v, near, rho,
    )
    (new_months,) = call(
        tail_kernel, [(MONTHS, R)], "vvvv", [(R, R), (R, R), (BLOCK, R)], t, gram, month_factor
    )
    return (z2, duals, new_months)


def solution(mesh):
    mesh = Mesh(mesh.devices.reshape(4, 4, 4, 2, 2), AXES)
    site, cons = ("z", "y", "x"), ("h", "c")
    every = site + cons
    placed = (
        P(every, None, None), P(every), P(every), P(every), P(every),
        P(site, None), P(), P(site, cons), P(site, cons),
    )
    return jax.shard_map(
        compute,
        mesh=mesh,
        in_specs=placed,
        out_specs=(P(site, cons), P(site, cons), P()),
        check_vma=False,
    )
```

```python
import functools

import jax
import jax.numpy as jnp
from jax import lax
from jax.experimental import pallas as pl
from jax.experimental.pallas import tpu as pltpu
from jax.sharding import Mesh
from jax.sharding import PartitionSpec as P


R = 256
MONTHS = 120
BLOCK = 128
SHARE = 40
CHUNK = 640
ROWS = 2560
CAP = 20
F32 = jnp.float32
BF16 = jnp.bfloat16
AXES = ("z", "y", "x", "h", "c")
PLANE = ("y", "x")


def number(z, y, x, h, c):
    return ((z * 4 + y) * 4 + x) * 4 + h * 2 + c


def pairs_of(move):
    out = []
    for z in range(4):
        for y in range(4):
            for x in range(4):
                for h in range(2):
                    for c in range(2):
                        out.append((number(z, y, x, h, c), number(*move(z, y, x, h, c))))
    return out


def first_move(k):
    def move(z, y, x, h, c):
        return (z, y, (x + k) % 4, h, c) if c == 0 else (z, (y + k) % 4, x, h, c)

    return pairs_of(move)


def second_move(k):
    def move(z, y, x, h, c):
        return (z, (y + k) % 4, x, h, c) if c == 0 else (z, y, (x + k) % 4, h, c)

    return pairs_of(move)


def depth_move(k):
    return pairs_of(lambda z, y, x, h, c: ((z + k) % 4, y, x, h, c))


CORE_MOVE = pairs_of(lambda z, y, x, h, c: (z, y, x, h, 1 - c))


def send(value, pairs):
    return lax.ppermute(value, AXES, pairs)


def scatter_sum(parts, moves):
    return [parts[0]] + [send(parts[k], moves(k)) for k in (1, 2, 3)]


def gather(value, moves):
    return [value] + [send(value, moves((4 - k) % 4)) for k in (1, 2, 3)]


def exchange(value, axes):
    return lax.all_to_all(value, axes, 0, 0, tiled=True)


def sum_to_all(value, count, axes):
    return jnp.sum(exchange(jnp.broadcast_to(value, (count, *value.shape)), axes), axis=0)


def sum_slices(value, axes):
    return jnp.sum(exchange(value.reshape(16, -1, R), axes), axis=0)


def spread_slices(value, axes):
    return exchange(jnp.broadcast_to(value, (16, *value.shape)), axes).reshape(-1, R)


def split(a):
    hi = a.astype(BF16)
    return hi, (a - hi.astype(F32)).astype(BF16)


def dot3(a, b):
    ah, al = a
    bh, bl = b
    dot = functools.partial(jnp.dot, preferred_element_type=F32)
    return dot(ah, bh) + (dot(ah, bl) + dot(al, bh))


def dot6(a, b):
    return jnp.dot(a, b, precision=lax.Precision.HIGHEST, preferred_element_type=F32)


def gram_of(a, precision=None):
    return lax.dot_general(
        a, a, (((0,), (0,)), ((), ())), precision=precision, preferred_element_type=F32
    )


def eye(n):
    return (
        lax.broadcasted_iota(jnp.int32, (n, n), 0) == lax.broadcasted_iota(jnp.int32, (n, n), 1)
    ).astype(F32)


def total(a):
    return jnp.sum(jnp.sum(a, axis=1, keepdims=True), axis=0, keepdims=True)


def shifted_inverse(hess, mat_ref, x_ref):
    n = hess.shape[0]
    ident = eye(n)
    rho = total(hess * ident) * (1.0 / n)
    mat = hess * (1.0 / rho) + ident
    mat_ref[...] = mat
    mat_parts = split(mat)
    low, high = 0.999, n + 1.5
    c0 = 2.0 / (low + high)

    def grow(a):
        up = a * (2.0 - a)
        s = 2.0 / (1.0 + up)
        return s, s * up

    s, a = grow(low * c0)
    x_ref[...] = (s * c0) * (2.0 * ident - c0 * mat)

    def coarse(_, a):
        s, a = grow(a)
        x_parts = split(x_ref[...])
        y = 2.0 * ident - dot3(mat_parts, x_parts)
        x_ref[...] = s * dot3(x_parts, split(y))
        return a

    lax.fori_loop(0, 5, coarse, jnp.float32(a))
    x = x_ref[...]
    x_ref[...] = dot6(x, 2.0 * ident - dot6(mat_ref[...], x))
    return rho


STEP = 1.0 / 128.0
ROOM = 14.98


def encode(block):
    top = jnp.max(jnp.abs(block), axis=0, keepdims=True)
    code = jnp.ceil(jnp.log2(jnp.maximum(top, 1e-30)) * 128.0)
    return jnp.round(block * jnp.exp2(ROOM - code * STEP)), code


def decode(whole, code):
    return whole * jnp.exp2(code * STEP - ROOM)


def to_codes(a):
    return a.astype(jnp.int32).astype(jnp.int16)


def from_codes(a):
    return a.astype(jnp.int32).astype(F32)


def placed():
    z, y, x, _, core = [lax.axis_index(a) for a in AXES]
    flat = core == 0
    return (
        jnp.where(flat, x, y), jnp.where(flat, y, x), z, core,
        jnp.where(flat, 1, 4), jnp.where(flat, 4, 1),
    )


def block_row(place, k, b):
    j, i = b // 4, b % 4
    first = lax.rem(place[0] + k, 4)
    second = lax.rem(place[1] + j, 4)
    depth = lax.rem(place[2] + i, 4)
    block = depth * 16 + first * place[4] + second * place[5]
    return pl.multiple_of(block * SHARE, 8)


def coded_rows(blocks):
    return -(-blocks * (SHARE + 1) // 16) * 16


def encode_blocks(source, first, blocks, coded, out):
    coded[blocks * SHARE :, :] = jnp.zeros((coded.shape[0] - blocks * SHARE, R), F32)
    for b in range(blocks):
        whole, code = encode(source[(first + b) * SHARE : (first + b + 1) * SHARE, :])
        coded[b * SHARE : (b + 1) * SHARE, :] = whole
        coded[blocks * SHARE + b : blocks * SHARE + b + 1, :] = code
    out[...] = to_codes(coded[...])


def add_blocks(acc, blocks, part, r):
    part[...] = from_codes(r[...])
    for b in range(blocks):
        acc[b * SHARE : (b + 1) * SHARE, :] += decode(
            part[b * SHARE : (b + 1) * SHARE, :],
            part[blocks * SHARE + b : blocks * SHARE + b + 1, :],
        )


def inverse_kernel(patient, month, near, rho_ref, weights, mat, square):
    month_gram = gram_of(month[...], lax.Precision.HIGHEST)
    gram = gram_of(patient[...])
    rho = shifted_inverse(gram * month_gram, mat, near)
    rho_ref[...] = jnp.broadcast_to(rho, rho_ref.shape)
    core = placed()[3]
    mat[...] = near[...]

    @pl.when(core == 1)
    def _():
        mat[...] = dot6(near[...], near[...])

    square[...] = gram
    half = pl.multiple_of(core * 128, 128)
    for p in range(16):
        weights[p * 24 : p * 24 + 16, :] = rho * mat[p * 16 : p * 16 + 16, :]
        weights[p * 24 + 16 : p * 24 + 24, :] = square[pl.ds(half + p * 8, 8), :]


def local_kernel(
    live, patient_at, code_at, month_at, near, rho_ref, patient_hbm, month_hbm, tiles_hbm, duals_hbm,
    prod_hbm, v_hbm, a0, q1, q2, q3,
    patient, month, tiles, duals, prod, grad, u_part, g_part, v, own, coded, held, sems, outs,
):
    copies = [
        pltpu.make_async_copy(src, dst, sems.at[n])
        for n, (src, dst) in enumerate(
            [
                (month_hbm, month), (patient_hbm, patient), (tiles_hbm, tiles), (duals_hbm, duals),
            ]
        )
    ]
    for copy in copies:
        copy.start()
    rho = rho_ref[0:1, 0:1]
    place = placed()
    grad[...] = jnp.zeros_like(grad)
    for copy in copies[:3]:
        copy.wait()

    def visit(turn, _):
        for k in [turn * 4 + n for n in range(4)]:
            pat = patient[pl.ds(pl.multiple_of(patient_at[k] * BLOCK, BLOCK), BLOCK), :]
            prod[k] = lax.dot_general(
                tiles[k], pat, (((0,), (0,)), ((), ())), preferred_element_type=F32
            )
        for k in [turn * 4 + n for n in range(4)]:
            scale = jnp.where(k < live[0], month[pl.ds(month_at[k], 1), :], 0.0)
            at = pl.ds(pl.multiple_of(code_at[k] * BLOCK, BLOCK), BLOCK)
            grad[at, :] += prod[k] * scale
        return 0

    lax.fori_loop(0, (live[0] + 3) // 4, visit, 0)
    prod_out = pltpu.make_async_copy(prod, prod_hbm, outs.at[4])
    prod_out.start()
    near_parts = split(near[...])
    copies[3].wait()

    def chunk(k, _):
        for b in range(16):
            at = pl.ds(block_row(place, k, b), SHARE)
            u_part[b * SHARE : (b + 1) * SHARE, :] = duals[at, :]
            g_part[b * SHARE : (b + 1) * SHARE, :] = grad[at, :]
        u = u_part[...]
        g = g_part[...] * (1.0 / rho)
        once = u + dot3(split(g - u), near_parts)
        twice = once + dot3(split(g - once), near_parts)
        v[k] = twice
        pltpu.make_async_copy(v.at[k], v_hbm.at[k], outs.at[5 + k]).start()
        u_part[...] = rho * once
        g_part[...] = rho * twice

        @pl.when(k == 0)
        def _():
            for b in range(16):
                own[b * 80 : b * 80 + SHARE, :] = u_part[b * SHARE : (b + 1) * SHARE, :]
                own[b * 80 + SHARE : b * 80 + 80, :] = g_part[b * SHARE : (b + 1) * SHARE, :]
            pltpu.make_async_copy(own, a0, outs.at[3]).start()

        @pl.when(k > 0)
        def _():
            for b in range(16):
                for q, part in enumerate((u_part, g_part)):
                    whole, code = encode(part[b * SHARE : (b + 1) * SHARE, :])
                    row = b * 80 + q * SHARE
                    coded[row : row + SHARE, :] = whole
                    coded[1280 + 2 * b + q : 1281 + 2 * b + q, :] = code
            held[k - 1] = to_codes(coded[...])

        for n, out in enumerate((q1, q2, q3)):

            @pl.when(k == n + 1)
            def _(n=n, out=out):
                pltpu.make_async_copy(held.at[n], out, outs.at[n]).start()

        return 0

    lax.fori_loop(0, 4, chunk, 0)
    for n, out in enumerate((q1, q2, q3)):
        pltpu.make_async_copy(held.at[n], out, outs.at[n]).wait()
    prod_out.wait()
    pltpu.make_async_copy(own, a0, outs.at[3]).wait()
    for k in range(4):
        pltpu.make_async_copy(v.at[k], v_hbm.at[k], outs.at[5 + k]).wait()


def sum_kernel(own, r1, r2, r3, s0, q1, q2, q3, acc, part, coded):
    blocks = own.shape[0] // SHARE
    few = blocks // 4
    acc[...] = own[...]
    for r in (r1, r2, r3):
        add_blocks(acc, blocks, part, r)
    s0[...] = acc[0 : few * SHARE, :]
    for j, out in enumerate((q1, q2, q3)):
        encode_blocks(acc, (j + 1) * few, few, coded, out)


def cut_kernel(r0, r1, r2, r3, out):
    for j, r in enumerate((r0, r1, r2, r3)):
        for i in range(4):
            at = (j * 4 + i) * 80
            out[at : at + 80, :] = r[i * 128 + 48 : i * 128 + 128, :]


def owner_kernel(
    s0, s1, s2, s3, z0_ref, mine, other, month,
    codes_ref, z2_ref, code_ref, gram_ref, own, oth, coded, acc, part,
):
    acc[...] = s0[...]
    for r in (s1, s2, s3):
        add_blocks(acc, 2, part, r)
    summed = acc[...]
    core = placed()[3]
    half = pl.multiple_of(core * 128, 128)
    rest = pl.multiple_of(128 - core * 128, 128)
    for p in range(16):
        own[p * 16 : p * 16 + 16, :] = mine[p * 24 : p * 24 + 16, :]
        oth[p * 16 : p * 16 + 16, :] = other[p * 24 : p * 24 + 16, :]
        gram_ref[pl.ds(half + p * 8, 8), :] = mine[p * 24 + 16 : p * 24 + 24, :]
        gram_ref[pl.ds(rest + p * 8, 8), :] = other[p * 24 + 16 : p * 24 + 24, :]
    mf = month[...]
    diagonal = jnp.sum(gram_ref[...] * eye(R), axis=0, keepdims=True)
    rho_total = total(jnp.sum(mf * mf, axis=0, keepdims=True) * diagonal) * (1.0 / R)
    a = own[...]
    b = oth[...]
    plain = jnp.where(core == 0, a, b)
    square = jnp.where(core == 0, b, a)
    z0 = z0_ref[...]
    first = summed[0:SHARE] + dot6(z0, plain)
    z1 = jnp.maximum(first / rho_total, 0.0)
    second = summed[SHARE:] + dot6(z0, plain - square) + 2.0 * dot6(z1, plain) - rho_total * z1
    z2 = jnp.maximum(second / rho_total, 0.0)
    coded[...] = jnp.zeros_like(coded)
    coded[0:40, :], coded[40:41, :] = encode(z2)
    coded[48:88, :], coded[41:42, :] = encode(z0)
    coded[88:128, :], coded[42:43, :] = encode(z1)
    codes_ref[...] = to_codes(coded[...])
    z2_ref[...] = z2
    code_ref[...] = gram_of(z2, lax.Precision.HIGHEST)


def month_kernel(live, code_at, month_at, w0, w1, w2, w3, prod, code, out, natural, part):
    place = placed()
    for k, w in enumerate((w0, w1, w2, w3)):
        part[...] = from_codes(w[...])
        for b in range(16):
            natural[pl.ds(block_row(place, k, b), SHARE), :] = decode(
                part[b * 48 : b * 48 + SHARE, :], part[b * 48 + SHARE : b * 48 + SHARE + 1, :]
            )
    for p in range(16):
        out[p * 24 : p * 24 + 8, :] = jnp.zeros((8, R), F32)
        out[p * 24 + 8 : p * 24 + 24, :] = code[p * 16 : p * 16 + 16, :]

    def visit(k, _):
        at = pl.ds(pl.multiple_of(code_at[k] * BLOCK, BLOCK), BLOCK)
        column = jnp.sum(prod[k] * natural[at, :], axis=0, keepdims=True)
        m = month_at[k]
        out[pl.ds((m // 8) * 24 + m % 8, 1), :] += column
        return 0

    lax.fori_loop(0, live[0], visit, 0)


def duals_kernel(*refs):
    place = placed()
    both, two = refs[0:4], refs[4:8]
    v, near, _, out, part, z0_part, z1_part, z2_part = refs[8:]
    near_parts = split(near[...])

    def chunk(k, _):
        for n in range(4):

            @pl.when(k == n)
            def _(n=n):
                part[0:1280, :] = from_codes(both[n][...])
                part[1280:, :] = from_codes(two[n][...])

        for b in range(16):
            rows = slice(b * SHARE, (b + 1) * SHARE)
            at = b * 80
            to = 1280 + b * 48
            z0_part[rows, :] = decode(part[at : at + 40, :], part[to + 41 : to + 42, :])
            z1_part[rows, :] = decode(part[at + 40 : at + 80, :], part[to + 42 : to + 43, :])
            z2_part[rows, :] = decode(part[to : to + 40, :], part[to + 40 : to + 41, :])
        z0 = z0_part[...]
        z1 = z1_part[...]
        inner = z0 - dot3(split(z0), near_parts) + 2.0 * z1
        z2_part[...] = v[k] + dot3(split(inner), near_parts) - z1 - z2_part[...]
        for b in range(16):
            out[pl.ds(block_row(place, k, b), SHARE), :] = z2_part[b * SHARE : (b + 1) * SHARE, :]
        return 0

    lax.fori_loop(0, 4, chunk, 0)


def tail_kernel(sums, gram, month, out, mat, near, grad):
    for p in range(16):
        grad[p * 8 : p * 8 + 8, :] = sums[p * 24 : p * 24 + 8, :]
        mat[p * 16 : p * 16 + 16, :] = sums[p * 24 + 8 : p * 24 + 24, :]
    rho = shifted_inverse(gram[...] * mat[...], mat, near)
    scaled = grad[0:MONTHS, :] * (1.0 / rho) + month[...]
    solved = jnp.maximum(dot6(scaled, near[...]), 0.0)
    mean = jnp.sum(solved, axis=0, keepdims=True) * (1.0 / MONTHS)
    out[...] = solved / (mean + 1e-06)


def call(body, outs, spaces, scratch, *args, limit=48 << 20):
    n = len(args)
    space = {"s": pltpu.SMEM, "h": pltpu.HBM, "v": pltpu.VMEM}
    return pl.pallas_call(
        body,
        out_shape=[s if isinstance(s, jax.ShapeDtypeStruct) else jax.ShapeDtypeStruct(s, F32) for s in outs],
        in_specs=[pl.BlockSpec(memory_space=space[c]) for c in spaces[:n]],
        out_specs=[pl.BlockSpec(memory_space=space[c]) for c in spaces[n:]],
        scratch_shapes=[pltpu.VMEM(s, F32) if isinstance(s, tuple) else s for s in scratch],
        compiler_params=pltpu.CompilerParams(vmem_limit_bytes=limit),
    )(*args)


def compute(
    tile_values, patient_block, code_block, month_index, live_count,
    patient_factor, month_factor, consensus, scaled_duals,
):
    near, rho, weights = call(
        inverse_kernel, [(R, R), (8, 128), (384, R)], "vv" + "vvv", [(R, R), (R, R)],
        patient_factor, month_factor, limit=None,
    )
    m = sum_slices(weights, PLANE)

    def codes(rows):
        return jax.ShapeDtypeStruct((rows, R), jnp.int16)

    tops = [coded_rows(n) for n in (32, 8, 2)]
    prod, v, *s = call(
        local_kernel,
        [(CAP, BLOCK, R), (4, CHUNK, R), (2 * CHUNK, R)] + [codes(tops[0])] * 3,
        "ssssvvhhhh" + "hhhhhh",
        [
            pltpu.VMEM((1024, R), BF16), (MONTHS, R), pltpu.VMEM((CAP, BLOCK, BLOCK), BF16),
            (ROWS, R), (CAP, BLOCK, R), (ROWS, R), (CHUNK, R), (CHUNK, R), (4, CHUNK, R),
            (2 * CHUNK, R), (tops[0], R), pltpu.VMEM((3, tops[0], R), jnp.int16),
            pltpu.SemaphoreType.DMA((4,)), pltpu.SemaphoreType.DMA((9,)),
        ],
        live_count, patient_block, code_block, month_index,
        near, rho, patient_factor, month_factor, tile_values, scaled_duals, limit=None,
    )
    s = scatter_sum(s, first_move)
    m = sum_to_all(m, 4, "z")
    mine = spread_slices(m, PLANE)
    other = send(mine, CORE_MOVE)
    s = call(
        sum_kernel, [(320, R)] + [codes(tops[1])] * 3, "vvvv" + "vvvv",
        [(2 * CHUNK, R), (tops[0], R), (tops[1], R)], *s,
    )
    s = scatter_sum(s, second_move)
    s = call(
        sum_kernel, [(80, R)] + [codes(tops[2])] * 3, "vvvv" + "vvvv",
        [(320, R), (tops[1], R), (tops[2], R)], *s,
    )
    s = scatter_sum(s, depth_move)
    rows, z2, code_gram, gram = call(
        owner_kernel, [codes(128), (SHARE, R), (R, R), (R, R)], "vvvvvvvv" + "vvvv",
        [(R, R), (R, R), (128, R), (80, R), (tops[2], R)],
        *s, consensus, mine, other, month_factor,
    )
    rows = jnp.concatenate(gather(rows, depth_move), 0)
    rows = gather(rows, second_move)
    two = jnp.concatenate([r.reshape(4, 128, R)[:, :48].reshape(192, R) for r in rows], 0)
    (both,) = call(cut_kernel, [codes(1280)], "vvvv" + "v", [], *rows)
    two = gather(two, first_move)
    both = gather(both, first_move)
    (sums,) = call(
        month_kernel, [(384, R)], "sssvvvvvv" + "v", [(ROWS, R), (768, R)],
        live_count, code_block, month_index, *two, prod, code_gram,
    )
    t = sum_slices(sums, PLANE)
    t = t + send(t, CORE_MOVE)
    t = sum_to_all(t, 8, ("z", "h"))
    t = spread_slices(t, PLANE)
    (duals,) = call(
        duals_kernel, [(ROWS, R)], "v" * 12, [(2048, R)] + [(CHUNK, R)] * 3,
        *both, *two, v, near, rho,
    )
    (new_months,) = call(
        tail_kernel, [(MONTHS, R)], "vvvv", [(R, R), (R, R), (BLOCK, R)], t, gram, month_factor
    )
    return (z2, duals, new_months)


def solution(mesh):
    mesh = Mesh(mesh.devices.reshape(4, 4, 4, 2, 2), AXES)
    site, cons = ("z", "y", "x"), ("h", "c")
    every = site + cons
    placed = (
        P(every, None, None), P(every), P(every), P(every), P(every),
        P(site, None), P(), P(site, cons), P(site, cons),
    )
    return jax.shard_map(
        compute,
        mesh=mesh,
        in_specs=placed,
        out_specs=(P(site, cons), P(site, cons), P()),
        check_vma=False,
    )
```

```python
import functools

import jax
import jax.numpy as jnp
from jax import lax
from jax.experimental import pallas as pl
from jax.experimental.pallas import tpu as pltpu
from jax.sharding import Mesh
from jax.sharding import PartitionSpec as P


R = 256
MONTHS = 120
BLOCK = 128
SHARE = 40
CHUNK = 640
ROWS = 2560
CAP = 20
SLOTS = 120
F32 = jnp.float32
BF16 = jnp.bfloat16
AXES = ("z", "y", "x", "h", "c")
PLANE = ("y", "x")


def number(z, y, x, h, c):
    return ((z * 4 + y) * 4 + x) * 4 + h * 2 + c


def pairs_of(move):
    out = []
    for z in range(4):
        for y in range(4):
            for x in range(4):
                for h in range(2):
                    for c in range(2):
                        out.append((number(z, y, x, h, c), number(*move(z, y, x, h, c))))
    return out


def first_move(k):
    def move(z, y, x, h, c):
        return (z, y, (x + k) % 4, h, c) if c == 0 else (z, (y + k) % 4, x, h, c)

    return pairs_of(move)


def second_move(k):
    def move(z, y, x, h, c):
        return (z, (y + k) % 4, x, h, c) if c == 0 else (z, y, (x + k) % 4, h, c)

    return pairs_of(move)


def depth_move(k):
    return pairs_of(lambda z, y, x, h, c: ((z + k) % 4, y, x, h, c))


CORE_MOVE = pairs_of(lambda z, y, x, h, c: (z, y, x, h, 1 - c))


def send(value, pairs):
    return lax.ppermute(value, AXES, pairs)


def scatter_sum(parts, moves):
    return [parts[0]] + [send(parts[k], moves(k)) for k in (1, 2, 3)]


def gather(value, moves):
    return [value] + [send(value, moves((4 - k) % 4)) for k in (1, 2, 3)]


def exchange(value, axes):
    return lax.all_to_all(value, axes, 0, 0, tiled=True)


def fan_kernel(got, out):
    count = got.shape[0]
    total_ = got[0]
    for n in range(1, count):
        total_ = total_ + got[n]
    for n in range(out.shape[0]):
        out[n] = total_


def fan(got, copies):
    return call(fan_kernel, [(copies, *got.shape[1:])], "v" + "v", [], got)[0]


def split(a):
    hi = a.astype(BF16)
    return hi, (a - hi.astype(F32)).astype(BF16)


def dot3(a, b):
    ah, al = a
    bh, bl = b
    dot = functools.partial(jnp.dot, preferred_element_type=F32)
    return dot(ah, bh) + (dot(ah, bl) + dot(al, bh))


def dot6(a, b):
    return jnp.dot(a, b, precision=lax.Precision.HIGHEST, preferred_element_type=F32)


def gram_of(a, precision=None):
    return lax.dot_general(
        a, a, (((0,), (0,)), ((), ())), precision=precision, preferred_element_type=F32
    )


def eye(n):
    return (
        lax.broadcasted_iota(jnp.int32, (n, n), 0) == lax.broadcasted_iota(jnp.int32, (n, n), 1)
    ).astype(F32)


def total(a):
    return jnp.sum(jnp.sum(a, axis=1, keepdims=True), axis=0, keepdims=True)


def shifted_inverse(hess, mat_ref, x_ref):
    n = hess.shape[0]
    ident = eye(n)
    rho = total(hess * ident) * (1.0 / n)
    mat = hess * (1.0 / rho) + ident
    mat_ref[...] = mat
    mat_parts = split(mat)
    low, high = 0.999, n + 1.5
    c0 = 2.0 / (low + high)

    def grow(a):
        up = a * (2.0 - a)
        s = 2.0 / (1.0 + up)
        return s, s * up

    s, a = grow(low * c0)
    x_ref[...] = (s * c0) * (2.0 * ident - c0 * mat)

    def coarse(_, a):
        s, a = grow(a)
        x_parts = split(x_ref[...])
        y = 2.0 * ident - dot3(mat_parts, x_parts)
        x_ref[...] = s * dot3(x_parts, split(y))
        return a

    lax.fori_loop(0, 5, coarse, jnp.float32(a))
    x = x_ref[...]
    x_ref[...] = dot6(x, 2.0 * ident - dot6(mat_ref[...], x))
    return rho


STEP = 1.0 / 128.0
ROOM = 14.98


def encode(block):
    top = jnp.max(jnp.abs(block), axis=0, keepdims=True)
    code = jnp.ceil(jnp.log2(jnp.maximum(top, 1e-30)) * 128.0)
    return jnp.round(block * jnp.exp2(ROOM - code * STEP)), code


def decode(whole, code):
    return whole * jnp.exp2(code * STEP - ROOM)


def to_codes(a):
    return a.astype(jnp.int32).astype(jnp.int16)


def from_codes(a):
    return a.astype(jnp.int32).astype(F32)


def placed():
    z, y, x, _, core = [lax.axis_index(a) for a in AXES]
    flat = core == 0
    return (
        jnp.where(flat, x, y), jnp.where(flat, y, x), z, core,
        jnp.where(flat, 1, 4), jnp.where(flat, 4, 1),
    )


def block_row(place, k, b):
    j, i = b // 4, b % 4
    first = lax.rem(place[0] + k, 4)
    second = lax.rem(place[1] + j, 4)
    depth = lax.rem(place[2] + i, 4)
    block = depth * 16 + first * place[4] + second * place[5]
    return pl.multiple_of(block * SHARE, 8)


def coded_rows(blocks):
    return -(-blocks * (SHARE + 1) // 16) * 16


def encode_blocks(source, first, blocks, coded, out):
    coded[blocks * SHARE :, :] = jnp.zeros((coded.shape[0] - blocks * SHARE, R), F32)
    for b in range(blocks):
        whole, code = encode(source[(first + b) * SHARE : (first + b + 1) * SHARE, :])
        coded[b * SHARE : (b + 1) * SHARE, :] = whole
        coded[blocks * SHARE + b : blocks * SHARE + b + 1, :] = code
    out[...] = to_codes(coded[...])


def add_blocks(acc, blocks, part, r):
    part[...] = from_codes(r[...])
    for b in range(blocks):
        acc[b * SHARE : (b + 1) * SHARE, :] += decode(
            part[b * SHARE : (b + 1) * SHARE, :],
            part[blocks * SHARE + b : blocks * SHARE + b + 1, :],
        )


def inverse_kernel(patient, month, near, rho_ref, weights, mat, square):
    month_gram = gram_of(month[...], lax.Precision.HIGHEST)
    gram = gram_of(patient[...])
    rho = shifted_inverse(gram * month_gram, mat, near)
    rho_ref[...] = jnp.broadcast_to(rho, rho_ref.shape)
    core = placed()[3]
    mat[...] = near[...]

    @pl.when(core == 1)
    def _():
        mat[...] = dot6(near[...], near[...])

    square[...] = gram
    half = pl.multiple_of(core * 128, 128)
    for p in range(16):
        weights[p * 24 : p * 24 + 16, :] = rho * mat[p * 16 : p * 16 + 16, :]
        weights[p * 24 + 16 : p * 24 + 24, :] = square[pl.ds(half + p * 8, 8), :]


def local_kernel(
    live, patient_at, code_at, month_at, near, rho_ref, patient_hbm, month_hbm, tiles_hbm, duals_hbm,
    prod_hbm, v_hbm, g_hbm, q1, q2, q3,
    patient, month, tiles, duals, prod, grad, u_part, g_part, v, g_own, coded, held, sems, outs,
):
    copies = [
        pltpu.make_async_copy(src, dst, sems.at[n])
        for n, (src, dst) in enumerate(
            [
                (month_hbm, month), (patient_hbm, patient), (tiles_hbm, tiles), (duals_hbm, duals),
            ]
        )
    ]
    for copy in copies:
        copy.start()
    rho = rho_ref[0:1, 0:1]
    place = placed()
    grad[...] = jnp.zeros_like(grad)
    for copy in copies[:3]:
        copy.wait()

    def visit(turn, _):
        for k in [turn * 4 + n for n in range(4)]:
            pat = patient[pl.ds(pl.multiple_of(patient_at[k] * BLOCK, BLOCK), BLOCK), :]
            prod[k] = lax.dot_general(
                tiles[k], pat, (((0,), (0,)), ((), ())), preferred_element_type=F32
            )
        for k in [turn * 4 + n for n in range(4)]:
            scale = jnp.where(k < live[0], month[pl.ds(month_at[k], 1), :], 0.0)
            at = pl.ds(pl.multiple_of(code_at[k] * BLOCK, BLOCK), BLOCK)
            grad[at, :] += prod[k] * scale
        return 0

    lax.fori_loop(0, (live[0] + 3) // 4, visit, 0)
    prod_out = pltpu.make_async_copy(prod, prod_hbm.at[pl.ds(0, CAP)], outs.at[4])
    prod_out.start()
    near_parts = split(near[...])
    copies[3].wait()

    for b in range(16):
        g_own[b * SHARE : (b + 1) * SHARE, :] = grad[pl.ds(block_row(place, 0, b), SHARE), :]
    g_out = pltpu.make_async_copy(g_own, g_hbm, outs.at[3])
    g_out.start()

    def chunk(step, _):
        k = lax.rem(step + 1, 3) + 1
        for b in range(16):
            at = pl.ds(block_row(place, k, b), SHARE)
            u_part[b * SHARE : (b + 1) * SHARE, :] = duals[at, :]
            g_part[b * SHARE : (b + 1) * SHARE, :] = grad[at, :]
        once, twice = two_rounds(u_part[...], g_part[...], rho, near_parts)
        v[k - 1] = twice
        pltpu.make_async_copy(v.at[k - 1], v_hbm.at[k - 1], outs.at[4 + k]).start()
        u_part[...] = rho * once
        g_part[...] = rho * twice
        for b in range(16):
            for q, part in enumerate((u_part, g_part)):
                whole, code = encode(part[b * SHARE : (b + 1) * SHARE, :])
                row = b * 80 + q * SHARE
                coded[row : row + SHARE, :] = whole
                coded[1280 + 2 * b + q : 1281 + 2 * b + q, :] = code
        held[k - 1] = to_codes(coded[...])
        for n, out in enumerate((q1, q2, q3)):

            @pl.when(k == n + 1)
            def _(n=n, out=out):
                pltpu.make_async_copy(held.at[n], out, outs.at[n]).start()

        return 0

    lax.fori_loop(0, 3, chunk, 0)
    for n, out in enumerate((q1, q2, q3)):
        pltpu.make_async_copy(held.at[n], out, outs.at[n]).wait()
    prod_out.wait()
    g_out.wait()
    for k in range(3):
        pltpu.make_async_copy(v.at[k], v_hbm.at[k], outs.at[5 + k]).wait()


def two_rounds(u, g, rho, near_parts):
    g = g * (1.0 / rho)
    once = u + dot3(split(g - u), near_parts)
    return once, once + dot3(split(g - once), near_parts)


def own_kernel(near, rho_ref, g_part, duals_hbm, a0, v0, u_part, sems):
    place = placed()
    copies = [
        pltpu.make_async_copy(
            duals_hbm.at[pl.ds(block_row(place, 0, b), SHARE), :],
            u_part.at[pl.ds(b * SHARE, SHARE), :],
            sems.at[b],
        )
        for b in range(16)
    ]
    for copy in copies:
        copy.start()
    rho = rho_ref[0:1, 0:1]
    near_parts = split(near[...])
    for copy in copies:
        copy.wait()
    once, twice = two_rounds(u_part[...], g_part[...], rho, near_parts)
    v0[...] = twice
    u_part[...] = rho * once
    for b in range(16):
        a0[b * 80 : b * 80 + SHARE, :] = u_part[b * SHARE : (b + 1) * SHARE, :]
        a0[b * 80 + SHARE : b * 80 + 80, :] = rho * v0[b * SHARE : (b + 1) * SHARE, :]


def sum_kernel(own, r1, r2, r3, s0, q1, q2, q3, acc, part, coded):
    blocks = own.shape[0] // SHARE
    few = blocks // 4
    acc[...] = own[...]
    for r in (r1, r2, r3):
        add_blocks(acc, blocks, part, r)
    s0[...] = acc[0 : few * SHARE, :]
    for j, out in enumerate((q1, q2, q3)):
        encode_blocks(acc, (j + 1) * few, few, coded, out)


def cut_kernel(r0, r1, r2, r3, out):
    for j, r in enumerate((r0, r1, r2, r3)):
        for i in range(4):
            at = (j * 4 + i) * 80
            out[at : at + 80, :] = r[i * 128 + 48 : i * 128 + 128, :]


def owner_kernel(
    s0, s1, s2, s3, z0_ref, mine, other, month,
    codes_ref, z2_ref, code_ref, gram_ref, own, oth, coded, acc, part,
):
    acc[...] = s0[...]
    for r in (s1, s2, s3):
        add_blocks(acc, 2, part, r)
    summed = acc[...]
    core = placed()[3]
    half = pl.multiple_of(core * 128, 128)
    rest = pl.multiple_of(128 - core * 128, 128)
    for p in range(16):
        own[p * 16 : p * 16 + 16, :] = mine[p * 24 : p * 24 + 16, :]
        oth[p * 16 : p * 16 + 16, :] = other[p * 24 : p * 24 + 16, :]
        gram_ref[pl.ds(half + p * 8, 8), :] = mine[p * 24 + 16 : p * 24 + 24, :]
        gram_ref[pl.ds(rest + p * 8, 8), :] = other[p * 24 + 16 : p * 24 + 24, :]
    mf = month[...]
    diagonal = jnp.sum(gram_ref[...] * eye(R), axis=0, keepdims=True)
    rho_total = total(jnp.sum(mf * mf, axis=0, keepdims=True) * diagonal) * (1.0 / R)
    a = own[...]
    b = oth[...]
    plain = jnp.where(core == 0, a, b)
    square = jnp.where(core == 0, b, a)
    z0 = z0_ref[...]
    first = summed[0:SHARE] + dot6(z0, plain)
    z1 = jnp.maximum(first / rho_total, 0.0)
    second = summed[SHARE:] + dot6(z0, plain - square) + 2.0 * dot6(z1, plain) - rho_total * z1
    z2 = jnp.maximum(second / rho_total, 0.0)
    coded[...] = jnp.zeros_like(coded)
    coded[0:40, :], coded[40:41, :] = encode(z2)
    coded[48:88, :], coded[41:42, :] = encode(z0)
    coded[88:128, :], coded[42:43, :] = encode(z1)
    codes_ref[...] = to_codes(coded[...])
    z2_ref[...] = z2
    code_ref[...] = gram_of(z2, lax.Precision.HIGHEST)


def month_kernel(
    live, code_at, month_at, w0, w1, w2, w3, prod_hbm, code, out, natural, part, prod, sems
):
    place = placed()

    def fetch(k, _):
        pltpu.make_async_copy(prod_hbm.at[k], prod.at[k], sems.at[k]).start()
        return 0

    lax.fori_loop(0, live[0], fetch, 0)
    for k, w in enumerate((w0, w1, w2, w3)):
        part[...] = from_codes(w[...])
        for b in range(16):
            natural[pl.ds(block_row(place, k, b), SHARE), :] = decode(
                part[b * 48 : b * 48 + SHARE, :], part[b * 48 + SHARE : b * 48 + SHARE + 1, :]
            )
    for p in range(16):
        out[p * 24 : p * 24 + 8, :] = jnp.zeros((8, R), F32)
        out[p * 24 + 8 : p * 24 + 24, :] = code[p * 16 : p * 16 + 16, :]

    def visit(k, _):
        at = pl.ds(pl.multiple_of(code_at[k] * BLOCK, BLOCK), BLOCK)
        pltpu.make_async_copy(prod_hbm.at[k], prod.at[k], sems.at[k]).wait()
        column = jnp.sum(prod[k] * natural[at, :], axis=0, keepdims=True)
        m = month_at[k]
        out[pl.ds((m // 8) * 24 + m % 8, 1), :] += column
        return 0

    lax.fori_loop(0, live[0], visit, 0)


def duals_kernel(*refs):
    place = placed()
    both, two = refs[0:4], refs[4:8]
    v0, v, near, _, out, part, z0_part, z1_part, z2_part, v_part = refs[8:]
    near_parts = split(near[...])

    def chunk(k, _):
        for n in range(4):

            @pl.when(k == n)
            def _(n=n):
                part[0:1280, :] = from_codes(both[n][...])
                part[1280:, :] = from_codes(two[n][...])
                v_part[...] = v0[...] if n == 0 else v[n - 1]

        for b in range(16):
            rows = slice(b * SHARE, (b + 1) * SHARE)
            at = b * 80
            to = 1280 + b * 48
            z0_part[rows, :] = decode(part[at : at + 40, :], part[to + 41 : to + 42, :])
            z1_part[rows, :] = decode(part[at + 40 : at + 80, :], part[to + 42 : to + 43, :])
            z2_part[rows, :] = decode(part[to : to + 40, :], part[to + 40 : to + 41, :])
        z0 = z0_part[...]
        z1 = z1_part[...]
        inner = z0 - dot3(split(z0), near_parts) + 2.0 * z1
        z2_part[...] = v_part[...] + dot3(split(inner), near_parts) - z1 - z2_part[...]
        for b in range(16):
            out[pl.ds(block_row(place, k, b), SHARE), :] = z2_part[b * SHARE : (b + 1) * SHARE, :]
        return 0

    lax.fori_loop(0, 4, chunk, 0)


def tail_kernel(sums, gram, month, out, mat, near, grad):
    for p in range(16):
        grad[p * 8 : p * 8 + 8, :] = sums[p * 24 : p * 24 + 8, :]
        mat[p * 16 : p * 16 + 16, :] = sums[p * 24 + 8 : p * 24 + 24, :]
    rho = shifted_inverse(gram[...] * mat[...], mat, near)
    scaled = grad[0:MONTHS, :] * (1.0 / rho) + month[...]
    solved = jnp.maximum(dot6(scaled, near[...]), 0.0)
    mean = jnp.sum(solved, axis=0, keepdims=True) * (1.0 / MONTHS)
    out[...] = solved / (mean + 1e-06)


def call(body, outs, spaces, scratch, *args, limit=48 << 20):
    n = len(args)
    space = {"s": pltpu.SMEM, "h": pltpu.HBM, "v": pltpu.VMEM}
    return pl.pallas_call(
        body,
        out_shape=[s if isinstance(s, jax.ShapeDtypeStruct) else jax.ShapeDtypeStruct(s, F32) for s in outs],
        in_specs=[pl.BlockSpec(memory_space=space[c]) for c in spaces[:n]],
        out_specs=[pl.BlockSpec(memory_space=space[c]) for c in spaces[n:]],
        scratch_shapes=[pltpu.VMEM(s, F32) if isinstance(s, tuple) else s for s in scratch],
        compiler_params=pltpu.CompilerParams(vmem_limit_bytes=limit),
    )(*args)


def compute(
    tile_values, patient_block, code_block, month_index, live_count,
    patient_factor, month_factor, consensus, scaled_duals,
):
    near, rho, weights = call(
        inverse_kernel, [(R, R), (8, 128), (384, R)], "vv" + "vvv", [(R, R), (R, R)],
        patient_factor, month_factor, limit=None,
    )
    m = exchange(weights.reshape(16, -1, R), PLANE)

    def codes(rows):
        return jax.ShapeDtypeStruct((rows, R), jnp.int16)

    tops = [coded_rows(n) for n in (32, 8, 2)]
    prod, v, g_own, *s = call(
        local_kernel,
        [(SLOTS, BLOCK, R), (3, CHUNK, R), (CHUNK, R)] + [codes(tops[0])] * 3,
        "ssssvvhhhh" + "hhhhhh",
        [
            pltpu.VMEM((1024, R), BF16), (MONTHS, R), pltpu.VMEM((CAP, BLOCK, BLOCK), BF16),
            (ROWS, R), (CAP, BLOCK, R), (ROWS, R), (CHUNK, R), (CHUNK, R), (3, CHUNK, R),
            (CHUNK, R), (tops[0], R), pltpu.VMEM((3, tops[0], R), jnp.int16),
            pltpu.SemaphoreType.DMA((4,)), pltpu.SemaphoreType.DMA((8,)),
        ],
        live_count, patient_block, code_block, month_index,
        near, rho, patient_factor, month_factor, tile_values, scaled_duals, limit=None,
    )
    s = [send(s[k - 1], first_move(k)) for k in (1, 2, 3)]
    a0, v0 = call(
        own_kernel, [(2 * CHUNK, R), (CHUNK, R)], "vvvh" + "vv",
        [(CHUNK, R), pltpu.SemaphoreType.DMA((16,))], near, rho, g_own, scaled_duals,
    )
    m = exchange(fan(m, 4), "z")
    mine = exchange(fan(m, 16), PLANE).reshape(-1, R)
    other = send(mine, CORE_MOVE)
    s = call(
        sum_kernel, [(320, R)] + [codes(tops[1])] * 3, "vvvv" + "vvvv",
        [(2 * CHUNK, R), (tops[0], R), (tops[1], R)], a0, *s,
    )
    s = scatter_sum(s, second_move)
    s = call(
        sum_kernel, [(80, R)] + [codes(tops[2])] * 3, "vvvv" + "vvvv",
        [(320, R), (tops[1], R), (tops[2], R)], *s,
    )
    s = scatter_sum(s, depth_move)
    rows, z2, code_gram, gram = call(
        owner_kernel, [codes(128), (SHARE, R), (R, R), (R, R)], "vvvvvvvv" + "vvvv",
        [(R, R), (R, R), (128, R), (80, R), (tops[2], R)],
        *s, consensus, mine, other, month_factor,
    )
    rows = jnp.concatenate(gather(rows, depth_move), 0)
    rows = gather(rows, second_move)
    two = jnp.concatenate([r.reshape(4, 128, R)[:, :48].reshape(192, R) for r in rows], 0)
    (both,) = call(cut_kernel, [codes(1280)], "vvvv" + "v", [], *rows)
    two = gather(two, first_move)
    both = gather(both, first_move)
    (sums,) = call(
        month_kernel, [(384, R)], "sssvvvvhv" + "v",
        [(ROWS, R), (768, R), (CAP, BLOCK, R), pltpu.SemaphoreType.DMA((CAP,))],
        live_count, code_block, month_index, *two, prod, code_gram,
    )
    t = exchange(sums.reshape(16, -1, R), PLANE)
    t = fan(t, 1)
    t = jnp.concatenate([t, send(t, CORE_MOVE)], 0)
    t = exchange(fan(t, 8), ("z", "h"))
    t = exchange(fan(t, 16), PLANE).reshape(-1, R)
    (duals,) = call(
        duals_kernel, [(ROWS, R)], "v" * 13, [(2048, R)] + [(CHUNK, R)] * 4,
        *both, *two, v0, v, near, rho,
    )
    (new_months,) = call(
        tail_kernel, [(MONTHS, R)], "vvvv", [(R, R), (R, R), (BLOCK, R)], t, gram, month_factor
    )
    return (z2, duals, new_months)


def solution(mesh):
    mesh = Mesh(mesh.devices.reshape(4, 4, 4, 2, 2), AXES)
    site, cons = ("z", "y", "x"), ("h", "c")
    every = site + cons
    placed = (
        P(every, None, None), P(every), P(every), P(every), P(every),
        P(site, None), P(), P(site, cons), P(site, cons),
    )
    return jax.shard_map(
        compute,
        mesh=mesh,
        in_specs=placed,
        out_specs=(P(site, cons), P(site, cons), P()),
        check_vma=False,
    )
```

```python
import functools

import jax
import jax.numpy as jnp
from jax import lax
from jax.experimental import pallas as pl
from jax.experimental.pallas import tpu as pltpu
from jax.sharding import Mesh
from jax.sharding import PartitionSpec as P


R = 256
MONTHS = 120
BLOCK = 128
SHARE = 40
CHUNK = 640
ROWS = 2560
CAP = 20
SLOTS = 120
ROOM_ROWS = 15360
F32 = jnp.float32
BF16 = jnp.bfloat16
AXES = ("z", "y", "x", "h", "c")
PLANE = ("y", "x")


def number(z, y, x, h, c):
    return ((z * 4 + y) * 4 + x) * 4 + h * 2 + c


def pairs_of(move):
    out = []
    for z in range(4):
        for y in range(4):
            for x in range(4):
                for h in range(2):
                    for c in range(2):
                        out.append((number(z, y, x, h, c), number(*move(z, y, x, h, c))))
    return out


def first_move(k):
    def move(z, y, x, h, c):
        return (z, y, (x + k) % 4, h, c) if c == 0 else (z, (y + k) % 4, x, h, c)

    return pairs_of(move)


def second_move(k):
    def move(z, y, x, h, c):
        return (z, (y + k) % 4, x, h, c) if c == 0 else (z, y, (x + k) % 4, h, c)

    return pairs_of(move)


def depth_move(k):
    return pairs_of(lambda z, y, x, h, c: ((z + k) % 4, y, x, h, c))


CORE_MOVE = pairs_of(lambda z, y, x, h, c: (z, y, x, h, 1 - c))


def send(value, pairs):
    return lax.ppermute(value, AXES, pairs)


def scatter_sum(parts, moves):
    return [parts[0]] + [send(parts[k], moves(k)) for k in (1, 2, 3)]


def gather(value, moves):
    return [value] + [send(value, moves((4 - k) % 4)) for k in (1, 2, 3)]


def exchange(value, axes):
    return lax.all_to_all(value, axes, 0, 0, tiled=True)


def fan_kernel(got, out):
    count = got.shape[0]
    total_ = got[0]
    for n in range(1, count):
        total_ = total_ + got[n]
    for n in range(out.shape[0]):
        out[n] = total_


def fan(got, copies):
    return call(fan_kernel, [(copies, *got.shape[1:])], "v" + "v", [], got)[0]


def split(a):
    hi = a.astype(BF16)
    return hi, (a - hi.astype(F32)).astype(BF16)


def dot3(a, b):
    ah, al = a
    bh, bl = b
    dot = functools.partial(jnp.dot, preferred_element_type=F32)
    return dot(ah, bh) + (dot(ah, bl) + dot(al, bh))


def dot6(a, b):
    return jnp.dot(a, b, precision=lax.Precision.HIGHEST, preferred_element_type=F32)


def gram_of(a, precision=None):
    return lax.dot_general(
        a, a, (((0,), (0,)), ((), ())), precision=precision, preferred_element_type=F32
    )


def eye(n):
    return (
        lax.broadcasted_iota(jnp.int32, (n, n), 0) == lax.broadcasted_iota(jnp.int32, (n, n), 1)
    ).astype(F32)


def total(a):
    return jnp.sum(jnp.sum(a, axis=1, keepdims=True), axis=0, keepdims=True)


def shifted_inverse(hess, mat_ref, x_ref):
    n = hess.shape[0]
    ident = eye(n)
    rho = total(hess * ident) * (1.0 / n)
    mat = hess * (1.0 / rho) + ident
    mat_ref[...] = mat
    mat_parts = split(mat)
    low, high = 0.999, n + 1.5
    c0 = 2.0 / (low + high)

    def grow(a):
        up = a * (2.0 - a)
        s = 2.0 / (1.0 + up)
        return s, s * up

    s, a = grow(low * c0)
    x_ref[...] = (s * c0) * (2.0 * ident - c0 * mat)

    def coarse(_, a):
        s, a = grow(a)
        x_parts = split(x_ref[...])
        y = 2.0 * ident - dot3(mat_parts, x_parts)
        x_ref[...] = s * dot3(x_parts, split(y))
        return a

    lax.fori_loop(0, 5, coarse, jnp.float32(a))
    x = x_ref[...]
    x_ref[...] = dot6(x, 2.0 * ident - dot6(mat_ref[...], x))
    return rho


STEP = 1.0 / 128.0
ROOM = 14.98


def encode(block):
    top = jnp.max(jnp.abs(block), axis=0, keepdims=True)
    code = jnp.ceil(jnp.log2(jnp.maximum(top, 1e-30)) * 128.0)
    return jnp.round(block * jnp.exp2(ROOM - code * STEP)), code


def decode(whole, code):
    return whole * jnp.exp2(code * STEP - ROOM)


def to_codes(a):
    return a.astype(jnp.int32).astype(jnp.int16)


def from_codes(a):
    return a.astype(jnp.int32).astype(F32)


def placed():
    z, y, x, _, core = [lax.axis_index(a) for a in AXES]
    flat = core == 0
    return (
        jnp.where(flat, x, y), jnp.where(flat, y, x), z, core,
        jnp.where(flat, 1, 4), jnp.where(flat, 4, 1),
    )


def block_row(place, k, b):
    j, i = b // 4, b % 4
    first = lax.rem(place[0] + k, 4)
    second = lax.rem(place[1] + j, 4)
    depth = lax.rem(place[2] + i, 4)
    block = depth * 16 + first * place[4] + second * place[5]
    return pl.multiple_of(block * SHARE, 8)


def coded_rows(blocks):
    return -(-blocks * (SHARE + 1) // 16) * 16


def encode_blocks(source, first, blocks, coded, out):
    coded[blocks * SHARE :, :] = jnp.zeros((coded.shape[0] - blocks * SHARE, R), F32)
    for b in range(blocks):
        whole, code = encode(source[(first + b) * SHARE : (first + b + 1) * SHARE, :])
        coded[b * SHARE : (b + 1) * SHARE, :] = whole
        coded[blocks * SHARE + b : blocks * SHARE + b + 1, :] = code
    out[...] = to_codes(coded[...])


def add_blocks(acc, blocks, part, r):
    part[...] = from_codes(r[...])
    for b in range(blocks):
        acc[b * SHARE : (b + 1) * SHARE, :] += decode(
            part[b * SHARE : (b + 1) * SHARE, :],
            part[blocks * SHARE + b : blocks * SHARE + b + 1, :],
        )


def inverse_kernel(patient, month, near, rho_ref, weights, mat, square):
    month_gram = gram_of(month[...], lax.Precision.HIGHEST)
    gram = gram_of(patient[...])
    rho = shifted_inverse(gram * month_gram, mat, near)
    rho_ref[...] = jnp.broadcast_to(rho, rho_ref.shape)
    core = placed()[3]
    mat[...] = near[...]

    @pl.when(core == 1)
    def _():
        mat[...] = dot6(near[...], near[...])

    square[...] = gram
    half = pl.multiple_of(core * 128, 128)
    for p in range(16):
        weights[p * 24 : p * 24 + 16, :] = rho * mat[p * 16 : p * 16 + 16, :]
        weights[p * 24 + 16 : p * 24 + 24, :] = square[pl.ds(half + p * 8, 8), :]


def local_kernel(
    live, patient_at, code_at, month_at, near, rho_ref, patient_hbm, month_hbm, tiles_hbm, duals_hbm,
    prod_hbm, v1, v2, v3, g_hbm, q1, q2, q3,
    patient, month, tiles, duals, prod, grad, u_part, g_part, v, g_own, coded, held, sems, outs,
):
    copies = [
        pltpu.make_async_copy(src, dst, sems.at[n])
        for n, (src, dst) in enumerate(
            [
                (month_hbm, month), (patient_hbm, patient), (tiles_hbm, tiles), (duals_hbm, duals),
            ]
        )
    ]
    for copy in copies:
        copy.start()
    rho = rho_ref[0:1, 0:1]
    place = placed()
    grad[...] = jnp.zeros_like(grad)
    for copy in copies[:3]:
        copy.wait()

    def visit(turn, _):
        for k in [turn * 4 + n for n in range(4)]:
            pat = patient[pl.ds(pl.multiple_of(patient_at[k] * BLOCK, BLOCK), BLOCK), :]
            prod[k] = lax.dot_general(
                tiles[k], pat, (((0,), (0,)), ((), ())), preferred_element_type=F32
            )
        for k in [turn * 4 + n for n in range(4)]:
            scale = jnp.where(k < live[0], month[pl.ds(month_at[k], 1), :], 0.0)
            at = pl.ds(pl.multiple_of(code_at[k] * BLOCK, BLOCK), BLOCK)
            grad[at, :] += prod[k] * scale
        return 0

    lax.fori_loop(0, (live[0] + 3) // 4, visit, 0)
    prod_out = pltpu.make_async_copy(prod, prod_hbm.at[pl.ds(0, CAP)], outs.at[4])
    prod_out.start()
    near_parts = split(near[...])
    copies[3].wait()

    for b in range(16):
        g_own[b * SHARE : (b + 1) * SHARE, :] = grad[pl.ds(block_row(place, 0, b), SHARE), :]
    g_out = pltpu.make_async_copy(g_own, g_hbm, outs.at[3])
    g_out.start()

    def chunk(step, _):
        k = lax.rem(step + 1, 3) + 1
        for b in range(16):
            at = pl.ds(block_row(place, k, b), SHARE)
            u_part[b * SHARE : (b + 1) * SHARE, :] = duals[at, :]
            g_part[b * SHARE : (b + 1) * SHARE, :] = grad[at, :]
        once, twice = two_rounds(u_part[...], g_part[...], rho, near_parts)
        v[k - 1] = twice
        u_part[...] = rho * once
        g_part[...] = rho * twice
        for b in range(16):
            for q, part in enumerate((u_part, g_part)):
                whole, code = encode(part[b * SHARE : (b + 1) * SHARE, :])
                row = b * 80 + q * SHARE
                coded[row : row + SHARE, :] = whole
                coded[1280 + 2 * b + q : 1281 + 2 * b + q, :] = code
        held[k - 1] = to_codes(coded[...])
        for n, (out, v_out) in enumerate(((q1, v1), (q2, v2), (q3, v3))):

            @pl.when(k == n + 1)
            def _(n=n, out=out, v_out=v_out):
                pltpu.make_async_copy(held.at[n], out, outs.at[n]).start()
                pltpu.make_async_copy(v.at[n], v_out, outs.at[5 + n]).start()

        return 0

    lax.fori_loop(0, 3, chunk, 0)
    for n, out in enumerate((q1, q2, q3)):
        pltpu.make_async_copy(held.at[n], out, outs.at[n]).wait()
    prod_out.wait()
    g_out.wait()
    for k, v_out in enumerate((v1, v2, v3)):
        pltpu.make_async_copy(v.at[k], v_out, outs.at[5 + k]).wait()


def two_rounds(u, g, rho, near_parts):
    g = g * (1.0 / rho)
    once = u + dot3(split(g - u), near_parts)
    return once, once + dot3(split(g - once), near_parts)


def own_kernel(near, rho_ref, g_part, duals_hbm, a0_hbm, v0, u_part, a0, sems):
    place = placed()
    copies = [
        pltpu.make_async_copy(
            duals_hbm.at[pl.ds(block_row(place, 0, b), SHARE), :],
            u_part.at[pl.ds(b * SHARE, SHARE), :],
            sems.at[b],
        )
        for b in range(16)
    ]
    for copy in copies:
        copy.start()
    rho = rho_ref[0:1, 0:1]
    near_parts = split(near[...])
    for copy in copies:
        copy.wait()
    once, twice = two_rounds(u_part[...], g_part[...], rho, near_parts)
    v0[...] = twice
    u_part[...] = rho * once
    for b in range(16):
        a0[b * 80 : b * 80 + SHARE, :] = u_part[b * SHARE : (b + 1) * SHARE, :]
        a0[b * 80 + SHARE : b * 80 + 80, :] = rho * v0[b * SHARE : (b + 1) * SHARE, :]
    out = pltpu.make_async_copy(a0, a0_hbm.at[pl.ds(0, 2 * CHUNK), :], sems.at[16])
    out.start()
    out.wait()


def first_sum_kernel(own_hbm, r1, r2, r3, s0, q1, q2, q3, acc, part, coded, own, sem):
    copy = pltpu.make_async_copy(own_hbm.at[pl.ds(0, 2 * CHUNK), :], own, sem)
    copy.start()
    acc[...] = jnp.zeros_like(acc)
    for r in (r1, r2, r3):
        add_blocks(acc, 32, part, r)
    copy.wait()
    acc[...] += own[...]
    s0[...] = acc[0:320, :]
    for j, out in enumerate((q1, q2, q3)):
        encode_blocks(acc, (j + 1) * 8, 8, coded, out)


def sum_kernel(own, r1, r2, r3, s0, q1, q2, q3, acc, part, coded):
    blocks = own.shape[0] // SHARE
    few = blocks // 4
    acc[...] = own[...]
    for r in (r1, r2, r3):
        add_blocks(acc, blocks, part, r)
    s0[...] = acc[0 : few * SHARE, :]
    for j, out in enumerate((q1, q2, q3)):
        encode_blocks(acc, (j + 1) * few, few, coded, out)


def cut_kernel(r0, r1, r2, r3, out):
    for j, r in enumerate((r0, r1, r2, r3)):
        for i in range(4):
            at = (j * 4 + i) * 80
            out[at : at + 80, :] = r[i * 128 + 48 : i * 128 + 128, :]


def owner_kernel(
    s0, s1, s2, s3, z0_ref, mine, other, month,
    codes_ref, z2_ref, code_ref, gram_ref, own, oth, coded, acc, part,
):
    acc[...] = s0[...]
    for r in (s1, s2, s3):
        add_blocks(acc, 2, part, r)
    summed = acc[...]
    core = placed()[3]
    half = pl.multiple_of(core * 128, 128)
    rest = pl.multiple_of(128 - core * 128, 128)
    for p in range(16):
        own[p * 16 : p * 16 + 16, :] = mine[p * 24 : p * 24 + 16, :]
        oth[p * 16 : p * 16 + 16, :] = other[p * 24 : p * 24 + 16, :]
        gram_ref[pl.ds(half + p * 8, 8), :] = mine[p * 24 + 16 : p * 24 + 24, :]
        gram_ref[pl.ds(rest + p * 8, 8), :] = other[p * 24 + 16 : p * 24 + 24, :]
    mf = month[...]
    diagonal = jnp.sum(gram_ref[...] * eye(R), axis=0, keepdims=True)
    rho_total = total(jnp.sum(mf * mf, axis=0, keepdims=True) * diagonal) * (1.0 / R)
    a = own[...]
    b = oth[...]
    plain = jnp.where(core == 0, a, b)
    square = jnp.where(core == 0, b, a)
    z0 = z0_ref[...]
    first = summed[0:SHARE] + dot6(z0, plain)
    z1 = jnp.maximum(first / rho_total, 0.0)
    second = summed[SHARE:] + dot6(z0, plain - square) + 2.0 * dot6(z1, plain) - rho_total * z1
    z2 = jnp.maximum(second / rho_total, 0.0)
    coded[...] = jnp.zeros_like(coded)
    coded[0:40, :], coded[40:41, :] = encode(z2)
    coded[48:88, :], coded[41:42, :] = encode(z0)
    coded[88:128, :], coded[42:43, :] = encode(z1)
    codes_ref[...] = to_codes(coded[...])
    z2_ref[...] = z2
    code_ref[...] = gram_of(z2, lax.Precision.HIGHEST)


def month_kernel(
    live, code_at, month_at, w0, w1, w2, w3, prod_hbm, code, out, natural, part, prod, sems
):
    place = placed()

    def fetch(k, _):
        pltpu.make_async_copy(prod_hbm.at[k], prod.at[k], sems.at[k]).start()
        return 0

    lax.fori_loop(0, live[0], fetch, 0)
    for k, w in enumerate((w0, w1, w2, w3)):
        part[...] = from_codes(w[...])
        for b in range(16):
            natural[pl.ds(block_row(place, k, b), SHARE), :] = decode(
                part[b * 48 : b * 48 + SHARE, :], part[b * 48 + SHARE : b * 48 + SHARE + 1, :]
            )
    for p in range(16):
        out[p * 24 : p * 24 + 8, :] = jnp.zeros((8, R), F32)
        out[p * 24 + 8 : p * 24 + 24, :] = code[p * 16 : p * 16 + 16, :]

    def visit(k, _):
        at = pl.ds(pl.multiple_of(code_at[k] * BLOCK, BLOCK), BLOCK)
        pltpu.make_async_copy(prod_hbm.at[k], prod.at[k], sems.at[k]).wait()
        column = jnp.sum(prod[k] * natural[at, :], axis=0, keepdims=True)
        m = month_at[k]
        out[pl.ds((m // 8) * 24 + m % 8, 1), :] += column
        return 0

    lax.fori_loop(0, live[0], visit, 0)


def duals_kernel(first, near, rho_ref, *refs):
    both, two, v = refs[0:2], refs[2:4], refs[4:6]
    out, part, z0_part, z1_part, value, sems = refs[-6:]
    place = placed()
    near_parts = split(near[...])

    def chunk(k, _):
        for n in range(2):

            @pl.when(k == n)
            def _(n=n):
                part[0:1280, :] = from_codes(both[n][...])
                part[1280:, :] = from_codes(two[n][...])
                value[n] = v[n][...]

        for b in range(16):
            rows = slice(b * SHARE, (b + 1) * SHARE)
            at = b * 80
            to = 1280 + b * 48
            z1 = decode(part[at + 40 : at + 80, :], part[to + 42 : to + 43, :])
            z0_part[rows, :] = decode(part[at : at + 40, :], part[to + 41 : to + 42, :])
            z1_part[rows, :] = 2.0 * z1
            z2 = decode(part[to : to + 40, :], part[to + 40 : to + 41, :])
            value[k, rows, :] = value[k, rows, :] - z1 - z2
        z0 = z0_part[...]
        inner = z0 - dot3(split(z0), near_parts) + z1_part[...]
        value[k] = value[k] + dot3(split(inner), near_parts)
        for b in range(16):
            pltpu.make_async_copy(
                value.at[k, pl.ds(b * SHARE, SHARE), :],
                out.at[pl.ds(block_row(place, first + k, b), SHARE), :],
                sems.at[k * 16 + b],
            ).start()
        return 0

    lax.fori_loop(0, 2, chunk, 0)
    for k in range(2):
        for b in range(16):
            pltpu.make_async_copy(
                value.at[k, pl.ds(b * SHARE, SHARE), :],
                out.at[pl.ds(block_row(place, first + k, b), SHARE), :],
                sems.at[k * 16 + b],
            ).wait()


def tail_kernel(sums, gram, month, out, mat, near, grad):
    for p in range(16):
        grad[p * 8 : p * 8 + 8, :] = sums[p * 24 : p * 24 + 8, :]
        mat[p * 16 : p * 16 + 16, :] = sums[p * 24 + 8 : p * 24 + 24, :]
    rho = shifted_inverse(gram[...] * mat[...], mat, near)
    scaled = grad[0:MONTHS, :] * (1.0 / rho) + month[...]
    solved = jnp.maximum(dot6(scaled, near[...]), 0.0)
    mean = jnp.sum(solved, axis=0, keepdims=True) * (1.0 / MONTHS)
    out[...] = solved / (mean + 1e-06)


def call(body, outs, spaces, scratch, *args, limit=48 << 20, aliases=None):
    n = len(args)
    space = {"s": pltpu.SMEM, "h": pltpu.HBM, "v": pltpu.VMEM}
    return pl.pallas_call(
        body,
        input_output_aliases=aliases or {},
        out_shape=[s if isinstance(s, jax.ShapeDtypeStruct) else jax.ShapeDtypeStruct(s, F32) for s in outs],
        in_specs=[pl.BlockSpec(memory_space=space[c]) for c in spaces[:n]],
        out_specs=[pl.BlockSpec(memory_space=space[c]) for c in spaces[n:]],
        scratch_shapes=[pltpu.VMEM(s, F32) if isinstance(s, tuple) else s for s in scratch],
        compiler_params=pltpu.CompilerParams(vmem_limit_bytes=limit),
    )(*args)


def compute(
    tile_values, patient_block, code_block, month_index, live_count,
    patient_factor, month_factor, consensus, scaled_duals,
):
    near, rho, weights = call(
        inverse_kernel, [(R, R), (8, 128), (384, R)], "vv" + "vvv", [(R, R), (R, R)],
        patient_factor, month_factor, limit=None,
    )
    m = exchange(weights.reshape(16, -1, R), PLANE)

    def codes(rows):
        return jax.ShapeDtypeStruct((rows, R), jnp.int16)

    tops = [coded_rows(n) for n in (32, 8, 2)]
    prod, v1, v2, v3, g_own, *s = call(
        local_kernel,
        [(SLOTS, BLOCK, R)] + [(CHUNK, R)] * 4 + [codes(tops[0])] * 3,
        "ssssvvhhhh" + "hhhhhhhh",
        [
            pltpu.VMEM((1024, R), BF16), (MONTHS, R), pltpu.VMEM((CAP, BLOCK, BLOCK), BF16),
            (ROWS, R), (CAP, BLOCK, R), (ROWS, R), (CHUNK, R), (CHUNK, R), (3, CHUNK, R),
            (CHUNK, R), (tops[0], R), pltpu.VMEM((3, tops[0], R), jnp.int16),
            pltpu.SemaphoreType.DMA((4,)), pltpu.SemaphoreType.DMA((8,)),
        ],
        live_count, patient_block, code_block, month_index,
        near, rho, patient_factor, month_factor, tile_values, scaled_duals, limit=None,
    )
    s = [send(s[k - 1], first_move(k)) for k in (1, 2, 3)]
    a0, v0 = call(
        own_kernel, [(ROOM_ROWS, R), (CHUNK, R)], "vvvh" + "hv",
        [(CHUNK, R), (2 * CHUNK, R), pltpu.SemaphoreType.DMA((17,))],
        near, rho, g_own, scaled_duals, limit=None,
    )
    m = exchange(fan(m, 4), "z")
    mine = exchange(fan(m, 16), PLANE).reshape(-1, R)
    other = send(mine, CORE_MOVE)
    s = call(
        first_sum_kernel, [(320, R)] + [codes(tops[1])] * 3, "hvvv" + "vvvv",
        [(2 * CHUNK, R), (tops[0], R), (tops[1], R), (2 * CHUNK, R), pltpu.SemaphoreType.DMA],
        a0, *s,
    )
    s = scatter_sum(s, second_move)
    s = call(
        sum_kernel, [(80, R)] + [codes(tops[2])] * 3, "vvvv" + "vvvv",
        [(320, R), (tops[1], R), (tops[2], R)], *s,
    )
    s = scatter_sum(s, depth_move)
    rows, z2, code_gram, gram = call(
        owner_kernel, [codes(128), (SHARE, R), (R, R), (R, R)], "vvvvvvvv" + "vvvv",
        [(R, R), (R, R), (128, R), (80, R), (tops[2], R)],
        *s, consensus, mine, other, month_factor,
    )
    rows = jnp.concatenate(gather(rows, depth_move), 0)
    rows = gather(rows, second_move)
    two = jnp.concatenate([r.reshape(4, 128, R)[:, :48].reshape(192, R) for r in rows], 0)
    (both,) = call(cut_kernel, [codes(1280)], "vvvv" + "v", [], *rows)
    two = gather(two, first_move)
    both = gather(both, first_move)
    (sums,) = call(
        month_kernel, [(384, R)], "sssvvvvhv" + "v",
        [(ROWS, R), (768, R), (CAP, BLOCK, R), pltpu.SemaphoreType.DMA((CAP,))],
        live_count, code_block, month_index, *two, prod, code_gram,
    )
    t = exchange(sums.reshape(16, -1, R), PLANE)
    t = exchange(fan(t, 16), ("z", "h", "c"))
    t = exchange(fan(t, 16), PLANE).reshape(-1, R)
    scratch = [(2048, R), (CHUNK, R), (CHUNK, R), (2, CHUNK, R), pltpu.SemaphoreType.DMA((32,))]
    (duals,) = call(
        functools.partial(duals_kernel, 0), [(ROWS, R)], "v" * 8 + "h", scratch,
        near, rho, *both[:2], *two[:2], v0, v1,
    )
    (duals,) = call(
        functools.partial(duals_kernel, 2), [(ROWS, R)], "v" * 8 + "h" + "h", scratch,
        near, rho, *both[2:], *two[2:], v2, v3, duals, aliases={8: 0},
    )
    (new_months,) = call(
        tail_kernel, [(MONTHS, R)], "vvvv", [(R, R), (R, R), (BLOCK, R)], t, gram, month_factor
    )
    return (z2, duals, new_months)


def solution(mesh):
    mesh = Mesh(mesh.devices.reshape(4, 4, 4, 2, 2), AXES)
    site, cons = ("z", "y", "x"), ("h", "c")
    every = site + cons
    placed = (
        P(every, None, None), P(every), P(every), P(every), P(every),
        P(site, None), P(), P(site, cons), P(site, cons),
    )
    return jax.shard_map(
        compute,
        mesh=mesh,
        in_specs=placed,
        out_specs=(P(site, cons), P(site, cons), P()),
        check_vma=False,
    )
```

```python
import functools

import jax
import jax.numpy as jnp
from jax import lax
from jax.experimental import pallas as pl
from jax.experimental.pallas import tpu as pltpu
from jax.sharding import Mesh
from jax.sharding import PartitionSpec as P


R = 256
MONTHS = 120
BLOCK = 128
SHARE = 40
CHUNK = 640
ROWS = 2560
CAP = 20
SLOTS = 120
ROOM_ROWS = 15360
F32 = jnp.float32
BF16 = jnp.bfloat16
AXES = ("z", "y", "x", "h", "c")
PLANE = ("y", "x")


def number(z, y, x, h, c):
    return ((z * 4 + y) * 4 + x) * 4 + h * 2 + c


def pairs_of(move):
    out = []
    for z in range(4):
        for y in range(4):
            for x in range(4):
                for h in range(2):
                    for c in range(2):
                        out.append((number(z, y, x, h, c), number(*move(z, y, x, h, c))))
    return out


def first_move(k):
    def move(z, y, x, h, c):
        return (z, y, (x + k) % 4, h, c) if c == 0 else (z, (y + k) % 4, x, h, c)

    return pairs_of(move)


def second_move(k):
    def move(z, y, x, h, c):
        return (z, (y + k) % 4, x, h, c) if c == 0 else (z, y, (x + k) % 4, h, c)

    return pairs_of(move)


def depth_move(k):
    return pairs_of(lambda z, y, x, h, c: ((z + k) % 4, y, x, h, c))


CORE_MOVE = pairs_of(lambda z, y, x, h, c: (z, y, x, h, 1 - c))


def send(value, pairs):
    return lax.ppermute(value, AXES, pairs)


def scatter_sum(parts, moves):
    return [parts[0]] + [send(parts[k], moves(k)) for k in (1, 2, 3)]


def gather(value, moves):
    return [value] + [send(value, moves((4 - k) % 4)) for k in (1, 2, 3)]


def exchange(value, axes):
    return lax.all_to_all(value, axes, 0, 0, tiled=True)


def fan_kernel(got, out):
    count = got.shape[0]
    total_ = got[0]
    for n in range(1, count):
        total_ = total_ + got[n]
    for n in range(out.shape[0]):
        out[n] = total_


def fan(got, copies):
    return call(fan_kernel, [(copies, *got.shape[1:])], "v" + "v", [], got)[0]


def split(a):
    hi = a.astype(BF16)
    return hi, (a - hi.astype(F32)).astype(BF16)


def dot3(a, b):
    ah, al = a
    bh, bl = b
    dot = functools.partial(jnp.dot, preferred_element_type=F32)
    return dot(ah, bh) + (dot(ah, bl) + dot(al, bh))


def dot6(a, b):
    return jnp.dot(a, b, precision=lax.Precision.HIGHEST, preferred_element_type=F32)


def gram_of(a, precision=None):
    return lax.dot_general(
        a, a, (((0,), (0,)), ((), ())), precision=precision, preferred_element_type=F32
    )


def eye(n):
    return (
        lax.broadcasted_iota(jnp.int32, (n, n), 0) == lax.broadcasted_iota(jnp.int32, (n, n), 1)
    ).astype(F32)


def total(a):
    return jnp.sum(jnp.sum(a, axis=1, keepdims=True), axis=0, keepdims=True)


def shifted_inverse(hess, mat_ref, x_ref):
    n = hess.shape[0]
    ident = eye(n)
    rho = total(hess * ident) * (1.0 / n)
    mat = hess * (1.0 / rho) + ident
    mat_ref[...] = mat
    mat_parts = split(mat)
    low, high = 0.999, n + 1.5
    c0 = 2.0 / (low + high)

    def grow(a):
        up = a * (2.0 - a)
        s = 2.0 / (1.0 + up)
        return s, s * up

    s, a = grow(low * c0)
    x_ref[...] = (s * c0) * (2.0 * ident - c0 * mat)

    def coarse(_, a):
        s, a = grow(a)
        x_parts = split(x_ref[...])
        y = 2.0 * ident - dot3(mat_parts, x_parts)
        x_ref[...] = s * dot3(x_parts, split(y))
        return a

    lax.fori_loop(0, 5, coarse, jnp.float32(a))
    x = x_ref[...]
    x_ref[...] = dot6(x, 2.0 * ident - dot6(mat_ref[...], x))
    return rho


STEP = 1.0 / 128.0
ROOM = 14.98


def encode(block):
    top = jnp.max(jnp.abs(block), axis=0, keepdims=True)
    code = jnp.ceil(jnp.log2(jnp.maximum(top, 1e-30)) * 128.0)
    return jnp.round(block * jnp.exp2(ROOM - code * STEP)), code


def decode(whole, code):
    return whole * jnp.exp2(code * STEP - ROOM)


def to_codes(a):
    return a.astype(jnp.int32).astype(jnp.int16)


def from_codes(a):
    return a.astype(jnp.int32).astype(F32)


def placed():
    z, y, x, _, core = [lax.axis_index(a) for a in AXES]
    flat = core == 0
    return (
        jnp.where(flat, x, y), jnp.where(flat, y, x), z, core,
        jnp.where(flat, 1, 4), jnp.where(flat, 4, 1),
    )


def block_row(place, k, b):
    j, i = b // 4, b % 4
    first = lax.rem(place[0] + k, 4)
    second = lax.rem(place[1] + j, 4)
    depth = lax.rem(place[2] + i, 4)
    block = depth * 16 + first * place[4] + second * place[5]
    return pl.multiple_of(block * SHARE, 8)


def coded_rows(blocks):
    return -(-blocks * (SHARE + 1) // 16) * 16


def encode_blocks(source, first, blocks, coded, out):
    coded[blocks * SHARE :, :] = jnp.zeros((coded.shape[0] - blocks * SHARE, R), F32)
    for b in range(blocks):
        whole, code = encode(source[(first + b) * SHARE : (first + b + 1) * SHARE, :])
        coded[b * SHARE : (b + 1) * SHARE, :] = whole
        coded[blocks * SHARE + b : blocks * SHARE + b + 1, :] = code
    out[...] = to_codes(coded[...])


def add_blocks(acc, blocks, part, r):
    part[...] = from_codes(r[...])
    for b in range(blocks):
        acc[b * SHARE : (b + 1) * SHARE, :] += decode(
            part[b * SHARE : (b + 1) * SHARE, :],
            part[blocks * SHARE + b : blocks * SHARE + b + 1, :],
        )


def inverse_kernel(patient, month, near, rho_ref, weights, mat, square):
    month_gram = gram_of(month[...], lax.Precision.HIGHEST)
    gram = gram_of(patient[...])
    rho = shifted_inverse(gram * month_gram, mat, near)
    rho_ref[...] = jnp.broadcast_to(rho, rho_ref.shape)
    core = placed()[3]
    mat[...] = near[...]

    @pl.when(core == 1)
    def _():
        mat[...] = dot6(near[...], near[...])

    square[...] = gram
    half = pl.multiple_of(core * 128, 128)
    for p in range(16):
        weights[p * 24 : p * 24 + 16, :] = rho * mat[p * 16 : p * 16 + 16, :]
        weights[p * 24 + 16 : p * 24 + 24, :] = square[pl.ds(half + p * 8, 8), :]


def local_kernel(
    live, patient_at, code_at, month_at, near, rho_ref, patient_hbm, month_hbm, tiles_hbm, duals_hbm,
    store, g_hbm, q1, q2, q3,
    patient, month, tiles, duals, prod, grad, u_part, g_part, v, g_own, coded, held, sems, outs,
):
    copies = [
        pltpu.make_async_copy(src, dst, sems.at[n])
        for n, (src, dst) in enumerate(
            [
                (month_hbm, month), (patient_hbm, patient), (tiles_hbm, tiles), (duals_hbm, duals),
            ]
        )
    ]
    for copy in copies:
        copy.start()
    rho = rho_ref[0:1, 0:1]
    place = placed()
    grad[...] = jnp.zeros_like(grad)
    for copy in copies[:3]:
        copy.wait()

    def visit(turn, _):
        for k in [turn * 4 + n for n in range(4)]:
            pat = patient[pl.ds(pl.multiple_of(patient_at[k] * BLOCK, BLOCK), BLOCK), :]
            prod[k] = lax.dot_general(
                tiles[k], pat, (((0,), (0,)), ((), ())), preferred_element_type=F32
            )
        for k in [turn * 4 + n for n in range(4)]:
            scale = jnp.where(k < live[0], month[pl.ds(month_at[k], 1), :], 0.0)
            at = pl.ds(pl.multiple_of(code_at[k] * BLOCK, BLOCK), BLOCK)
            grad[at, :] += prod[k] * scale
        return 0

    lax.fori_loop(0, (live[0] + 3) // 4, visit, 0)
    prod_out = pltpu.make_async_copy(prod, store.at[pl.ds(0, CAP)], outs.at[4])
    prod_out.start()
    near_parts = split(near[...])
    copies[3].wait()

    for b in range(16):
        g_own[b * SHARE : (b + 1) * SHARE, :] = grad[pl.ds(block_row(place, 0, b), SHARE), :]
    g_out = pltpu.make_async_copy(g_own, g_hbm, outs.at[3])
    g_out.start()

    def chunk(step, _):
        k = lax.rem(step + 1, 3) + 1
        for b in range(16):
            at = pl.ds(block_row(place, k, b), SHARE)
            u_part[b * SHARE : (b + 1) * SHARE, :] = duals[at, :]
            g_part[b * SHARE : (b + 1) * SHARE, :] = grad[at, :]
        once, twice = two_rounds(u_part[...], g_part[...], rho, near_parts)
        v[k - 1] = twice.reshape(5, BLOCK, R)
        u_part[...] = rho * once
        g_part[...] = rho * twice
        for b in range(16):
            for q, part in enumerate((u_part, g_part)):
                whole, code = encode(part[b * SHARE : (b + 1) * SHARE, :])
                row = b * 80 + q * SHARE
                coded[row : row + SHARE, :] = whole
                coded[1280 + 2 * b + q : 1281 + 2 * b + q, :] = code
        held[k - 1] = to_codes(coded[...])
        for n, out in enumerate((q1, q2, q3)):

            @pl.when(k == n + 1)
            def _(n=n, out=out):
                pltpu.make_async_copy(held.at[n], out, outs.at[n]).start()
                at = pl.ds(CAP + 5 * n, 5)
                pltpu.make_async_copy(v.at[n], store.at[at], outs.at[5 + n]).start()

        return 0

    lax.fori_loop(0, 3, chunk, 0)
    for n, out in enumerate((q1, q2, q3)):
        pltpu.make_async_copy(held.at[n], out, outs.at[n]).wait()
    prod_out.wait()
    g_out.wait()
    for n in range(3):
        pltpu.make_async_copy(v.at[n], store.at[pl.ds(CAP + 5 * n, 5)], outs.at[5 + n]).wait()


def two_rounds(u, g, rho, near_parts):
    g = g * (1.0 / rho)
    once = u + dot3(split(g - u), near_parts)
    return once, once + dot3(split(g - once), near_parts)


def own_kernel(near, rho_ref, g_part, duals_hbm, room, v0, u_part, a0, sems):
    place = placed()
    copies = [
        pltpu.make_async_copy(
            duals_hbm.at[pl.ds(block_row(place, 0, b), SHARE), :],
            u_part.at[pl.ds(b * SHARE, SHARE), :],
            sems.at[b],
        )
        for b in range(16)
    ]
    for copy in copies:
        copy.start()
    rho = rho_ref[0:1, 0:1]
    near_parts = split(near[...])
    for copy in copies:
        copy.wait()
    once, twice = two_rounds(u_part[...], g_part[...], rho, near_parts)
    v0[...] = twice
    u_part[...] = rho * once
    for b in range(16):
        a0[b * 80 : b * 80 + SHARE, :] = u_part[b * SHARE : (b + 1) * SHARE, :]
        a0[b * 80 + SHARE : b * 80 + 80, :] = rho * v0[b * SHARE : (b + 1) * SHARE, :]
    out = pltpu.make_async_copy(a0, room.at[pl.ds(0, 2 * CHUNK), :], sems.at[16])
    out.start()
    v_out = pltpu.make_async_copy(v0, room.at[pl.ds(2 * CHUNK, CHUNK), :], sems.at[17])
    v_out.start()
    out.wait()
    v_out.wait()


def first_sum_kernel(own_hbm, r1, r2, r3, s0, q1, q2, q3, acc, part, coded, own, sem):
    copy = pltpu.make_async_copy(own_hbm.at[pl.ds(0, 2 * CHUNK), :], own, sem)
    copy.start()
    acc[...] = jnp.zeros_like(acc)
    for r in (r1, r2, r3):
        add_blocks(acc, 32, part, r)
    copy.wait()
    acc[...] += own[...]
    s0[...] = acc[0:320, :]
    for j, out in enumerate((q1, q2, q3)):
        encode_blocks(acc, (j + 1) * 8, 8, coded, out)


def sum_kernel(own, r1, r2, r3, s0, q1, q2, q3, acc, part, coded):
    blocks = own.shape[0] // SHARE
    few = blocks // 4
    acc[...] = own[...]
    for r in (r1, r2, r3):
        add_blocks(acc, blocks, part, r)
    s0[...] = acc[0 : few * SHARE, :]
    for j, out in enumerate((q1, q2, q3)):
        encode_blocks(acc, (j + 1) * few, few, coded, out)


def cut_kernel(r0, r1, r2, r3, out):
    for j, r in enumerate((r0, r1, r2, r3)):
        for i in range(4):
            at = (j * 4 + i) * 80
            out[at : at + 80, :] = r[i * 128 + 48 : i * 128 + 128, :]


def owner_kernel(
    s0, s1, s2, s3, z0_ref, mine, other, month,
    codes_ref, z2_ref, code_ref, gram_ref, own, oth, coded, acc, part,
):
    acc[...] = s0[...]
    for r in (s1, s2, s3):
        add_blocks(acc, 2, part, r)
    summed = acc[...]
    core = placed()[3]
    half = pl.multiple_of(core * 128, 128)
    rest = pl.multiple_of(128 - core * 128, 128)
    for p in range(16):
        own[p * 16 : p * 16 + 16, :] = mine[p * 24 : p * 24 + 16, :]
        oth[p * 16 : p * 16 + 16, :] = other[p * 24 : p * 24 + 16, :]
        gram_ref[pl.ds(half + p * 8, 8), :] = mine[p * 24 + 16 : p * 24 + 24, :]
        gram_ref[pl.ds(rest + p * 8, 8), :] = other[p * 24 + 16 : p * 24 + 24, :]
    mf = month[...]
    diagonal = jnp.sum(gram_ref[...] * eye(R), axis=0, keepdims=True)
    rho_total = total(jnp.sum(mf * mf, axis=0, keepdims=True) * diagonal) * (1.0 / R)
    a = own[...]
    b = oth[...]
    plain = jnp.where(core == 0, a, b)
    square = jnp.where(core == 0, b, a)
    z0 = z0_ref[...]
    first = summed[0:SHARE] + dot6(z0, plain)
    z1 = jnp.maximum(first / rho_total, 0.0)
    second = summed[SHARE:] + dot6(z0, plain - square) + 2.0 * dot6(z1, plain) - rho_total * z1
    z2 = jnp.maximum(second / rho_total, 0.0)
    coded[...] = jnp.zeros_like(coded)
    coded[0:40, :], coded[40:41, :] = encode(z2)
    coded[48:88, :], coded[41:42, :] = encode(z0)
    coded[88:128, :], coded[42:43, :] = encode(z1)
    codes_ref[...] = to_codes(coded[...])
    z2_ref[...] = z2
    code_ref[...] = gram_of(z2, lax.Precision.HIGHEST)


def month_kernel(
    live, code_at, month_at, w0, w1, w2, w3, prod_hbm, code, out, natural, part, prod, sems
):
    place = placed()

    def fetch(k, _):
        pltpu.make_async_copy(prod_hbm.at[k], prod.at[k], sems.at[k]).start()
        return 0

    lax.fori_loop(0, live[0], fetch, 0)
    for k, w in enumerate((w0, w1, w2, w3)):
        part[...] = from_codes(w[...])
        for b in range(16):
            natural[pl.ds(block_row(place, k, b), SHARE), :] = decode(
                part[b * 48 : b * 48 + SHARE, :], part[b * 48 + SHARE : b * 48 + SHARE + 1, :]
            )
    for p in range(16):
        out[p * 24 : p * 24 + 8, :] = jnp.zeros((8, R), F32)
        out[p * 24 + 8 : p * 24 + 24, :] = code[p * 16 : p * 16 + 16, :]

    def visit(k, _):
        at = pl.ds(pl.multiple_of(code_at[k] * BLOCK, BLOCK), BLOCK)
        pltpu.make_async_copy(prod_hbm.at[k], prod.at[k], sems.at[k]).wait()
        column = jnp.sum(prod[k] * natural[at, :], axis=0, keepdims=True)
        m = month_at[k]
        out[pl.ds((m // 8) * 24 + m % 8, 1), :] += column
        return 0

    lax.fori_loop(0, live[0], visit, 0)


def duals_kernel(first, near, rho_ref, *refs):
    both, two, store, room = refs[0:2], refs[2:4], refs[4], refs[5]
    out, part, z0_part, z1_part, value, own, less, done, sems = refs[-9:]
    place = placed()
    fetches = []
    for n in range(2):
        at = CAP + 5 * (first + n - 1)
        source = store.at[pl.ds(at, 5)]
        target = value.at[pl.ds(n * 5, 5)]
        if first + n == 0:
            source, target = room.at[pl.ds(2 * CHUNK, CHUNK), :], own
        fetches.append(pltpu.make_async_copy(source, target, sems.at[32 + n]))
        fetches[n].start()
    near_parts = split(near[...])

    def chunk(k, _):
        for n in range(2):

            @pl.when(k == n)
            def _(n=n):
                part[0:1280, :] = from_codes(both[n][...])
                part[1280:, :] = from_codes(two[n][...])

        for b in range(16):
            rows = slice(b * SHARE, (b + 1) * SHARE)
            at = b * 80
            to = 1280 + b * 48
            z1 = decode(part[at + 40 : at + 80, :], part[to + 42 : to + 43, :])
            z0_part[rows, :] = decode(part[at : at + 40, :], part[to + 41 : to + 42, :])
            z1_part[rows, :] = 2.0 * z1
            z2 = decode(part[to : to + 40, :], part[to + 40 : to + 41, :])
            less[rows, :] = z1 + z2
        z0 = z0_part[...]
        inner = z0 - dot3(split(z0), near_parts) + z1_part[...]
        less[...] = dot3(split(inner), near_parts) - less[...]
        for n in range(2):

            @pl.when(k == n)
            def _(n=n):
                fetches[n].wait()
                base = own[...] if first + n == 0 else value[n * 5 : n * 5 + 5].reshape(CHUNK, R)
                done[n] = base + less[...]

        for b in range(16):
            pltpu.make_async_copy(
                done.at[k, pl.ds(b * SHARE, SHARE), :],
                out.at[pl.ds(block_row(place, first + k, b), SHARE), :],
                sems.at[k * 16 + b],
            ).start()
        return 0

    lax.fori_loop(0, 2, chunk, 0)
    for k in range(2):
        for b in range(16):
            pltpu.make_async_copy(
                done.at[k, pl.ds(b * SHARE, SHARE), :],
                out.at[pl.ds(block_row(place, first + k, b), SHARE), :],
                sems.at[k * 16 + b],
            ).wait()


def tail_kernel(sums, gram, month, out, mat, near, grad):
    for p in range(16):
        grad[p * 8 : p * 8 + 8, :] = sums[p * 24 : p * 24 + 8, :]
        mat[p * 16 : p * 16 + 16, :] = sums[p * 24 + 8 : p * 24 + 24, :]
    rho = shifted_inverse(gram[...] * mat[...], mat, near)
    scaled = grad[0:MONTHS, :] * (1.0 / rho) + month[...]
    solved = jnp.maximum(dot6(scaled, near[...]), 0.0)
    mean = jnp.sum(solved, axis=0, keepdims=True) * (1.0 / MONTHS)
    out[...] = solved / (mean + 1e-06)


def call(body, outs, spaces, scratch, *args, limit=48 << 20, aliases=None):
    n = len(args)
    space = {"s": pltpu.SMEM, "h": pltpu.HBM, "v": pltpu.VMEM}
    return pl.pallas_call(
        body,
        input_output_aliases=aliases or {},
        out_shape=[s if isinstance(s, jax.ShapeDtypeStruct) else jax.ShapeDtypeStruct(s, F32) for s in outs],
        in_specs=[pl.BlockSpec(memory_space=space[c]) for c in spaces[:n]],
        out_specs=[pl.BlockSpec(memory_space=space[c]) for c in spaces[n:]],
        scratch_shapes=[pltpu.VMEM(s, F32) if isinstance(s, tuple) else s for s in scratch],
        compiler_params=pltpu.CompilerParams(vmem_limit_bytes=limit),
    )(*args)


def compute(
    tile_values, patient_block, code_block, month_index, live_count,
    patient_factor, month_factor, consensus, scaled_duals,
):
    near, rho, weights = call(
        inverse_kernel, [(R, R), (8, 128), (384, R)], "vv" + "vvv", [(R, R), (R, R)],
        patient_factor, month_factor, limit=None,
    )
    m = exchange(weights.reshape(16, -1, R), PLANE)

    def codes(rows):
        return jax.ShapeDtypeStruct((rows, R), jnp.int16)

    tops = [coded_rows(n) for n in (32, 8, 2)]
    store, g_own, *s = call(
        local_kernel,
        [(SLOTS, BLOCK, R), (CHUNK, R)] + [codes(tops[0])] * 3,
        "ssssvvhhhh" + "hhhhh",
        [
            pltpu.VMEM((1024, R), BF16), (MONTHS, R), pltpu.VMEM((CAP, BLOCK, BLOCK), BF16),
            (ROWS, R), (CAP, BLOCK, R), (ROWS, R), (CHUNK, R), (CHUNK, R), (3, 5, BLOCK, R),
            (CHUNK, R), (tops[0], R), pltpu.VMEM((3, tops[0], R), jnp.int16),
            pltpu.SemaphoreType.DMA((4,)), pltpu.SemaphoreType.DMA((8,)),
        ],
        live_count, patient_block, code_block, month_index,
        near, rho, patient_factor, month_factor, tile_values, scaled_duals, limit=None,
    )
    s = [send(s[k - 1], first_move(k)) for k in (1, 2, 3)]
    (room,) = call(
        own_kernel, [(ROOM_ROWS, R)], "vvvh" + "h",
        [(CHUNK, R), (CHUNK, R), (2 * CHUNK, R), pltpu.SemaphoreType.DMA((18,))],
        near, rho, g_own, scaled_duals, limit=None,
    )
    m = exchange(fan(m, 4), "z")
    mine = exchange(fan(m, 16), PLANE).reshape(-1, R)
    other = send(mine, CORE_MOVE)
    s = call(
        first_sum_kernel, [(320, R)] + [codes(tops[1])] * 3, "hvvv" + "vvvv",
        [(2 * CHUNK, R), (tops[0], R), (tops[1], R), (2 * CHUNK, R), pltpu.SemaphoreType.DMA],
        room, *s,
    )
    s = scatter_sum(s, second_move)
    s = call(
        sum_kernel, [(80, R)] + [codes(tops[2])] * 3, "vvvv" + "vvvv",
        [(320, R), (tops[1], R), (tops[2], R)], *s,
    )
    s = scatter_sum(s, depth_move)
    rows, z2, code_gram, gram = call(
        owner_kernel, [codes(128), (SHARE, R), (R, R), (R, R)], "vvvvvvvv" + "vvvv",
        [(R, R), (R, R), (128, R), (80, R), (tops[2], R)],
        *s, consensus, mine, other, month_factor,
    )
    rows = jnp.concatenate(gather(rows, depth_move), 0)
    rows = gather(rows, second_move)
    two = jnp.concatenate([r.reshape(4, 128, R)[:, :48].reshape(192, R) for r in rows], 0)
    (both,) = call(cut_kernel, [codes(1280)], "vvvv" + "v", [], *rows)
    two = gather(two, first_move)
    both = gather(both, first_move)
    (sums,) = call(
        month_kernel, [(384, R)], "sssvvvvhv" + "v",
        [(ROWS, R), (768, R), (CAP, BLOCK, R), pltpu.SemaphoreType.DMA((CAP,))],
        live_count, code_block, month_index, *two, store, code_gram,
    )
    t = exchange(sums.reshape(16, -1, R), PLANE)
    t = fan(t, 1)
    t = jnp.concatenate([t, send(t, CORE_MOVE)], 0)
    t = exchange(fan(t, 8), ("z", "h"))
    t = exchange(fan(t, 16), PLANE).reshape(-1, R)
    scratch = [
        (2048, R), (CHUNK, R), (CHUNK, R), (10, BLOCK, R), (CHUNK, R), (CHUNK, R), (2, CHUNK, R),
        pltpu.SemaphoreType.DMA((34,)),
    ]
    (duals,) = call(
        functools.partial(duals_kernel, 0), [(ROWS, R)], "vvvvvvhh" + "h", scratch,
        near, rho, *both[:2], *two[:2], store, room,
    )
    (duals,) = call(
        functools.partial(duals_kernel, 2), [(ROWS, R)], "vvvvvvhhh" + "h", scratch,
        near, rho, *both[2:], *two[2:], store, room, duals, aliases={8: 0},
    )
    (new_months,) = call(
        tail_kernel, [(MONTHS, R)], "vvvv", [(R, R), (R, R), (BLOCK, R)], t, gram, month_factor
    )
    return (z2, duals, new_months)


def solution(mesh):
    mesh = Mesh(mesh.devices.reshape(4, 4, 4, 2, 2), AXES)
    site, cons = ("z", "y", "x"), ("h", "c")
    every = site + cons
    placed = (
        P(every, None, None), P(every), P(every), P(every), P(every),
        P(site, None), P(), P(site, cons), P(site, cons),
    )
    return jax.shard_map(
        compute,
        mesh=mesh,
        in_specs=placed,
        out_specs=(P(site, cons), P(site, cons), P()),
        check_vma=False,
    )
```

```python
import functools

import jax
import jax.numpy as jnp
from jax import lax
from jax.experimental import pallas as pl
from jax.experimental.pallas import tpu as pltpu
from jax.sharding import Mesh
from jax.sharding import PartitionSpec as P


R = 256
MONTHS = 120
BLOCK = 128
SHARE = 40
CHUNK = 640
ROWS = 2560
CAP = 20
SLOTS = 120
ROOM_ROWS = 15360
F32 = jnp.float32
BF16 = jnp.bfloat16
AXES = ("z", "y", "x", "h", "c")
PLANE = ("y", "x")


def number(z, y, x, h, c):
    return ((z * 4 + y) * 4 + x) * 4 + h * 2 + c


def pairs_of(move):
    out = []
    for z in range(4):
        for y in range(4):
            for x in range(4):
                for h in range(2):
                    for c in range(2):
                        out.append((number(z, y, x, h, c), number(*move(z, y, x, h, c))))
    return out


def first_move(k):
    def move(z, y, x, h, c):
        return (z, y, (x + k) % 4, h, c) if c == 0 else (z, (y + k) % 4, x, h, c)

    return pairs_of(move)


def second_move(k):
    def move(z, y, x, h, c):
        return (z, (y + k) % 4, x, h, c) if c == 0 else (z, y, (x + k) % 4, h, c)

    return pairs_of(move)


def depth_move(k):
    return pairs_of(lambda z, y, x, h, c: ((z + k) % 4, y, x, h, c))


CORE_MOVE = pairs_of(lambda z, y, x, h, c: (z, y, x, h, 1 - c))


def send(value, pairs):
    return lax.ppermute(value, AXES, pairs)


def scatter_sum(parts, moves):
    return [parts[0]] + [send(parts[k], moves(k)) for k in (1, 2, 3)]


def gather(value, moves):
    return [value] + [send(value, moves((4 - k) % 4)) for k in (1, 2, 3)]


def exchange(value, axes):
    return lax.all_to_all(value, axes, 0, 0, tiled=True)


def fan_kernel(got, out):
    count = got.shape[0]
    total_ = got[0]
    for n in range(1, count):
        total_ = total_ + got[n]
    for n in range(out.shape[0]):
        out[n] = total_


def fan(got, copies):
    return call(fan_kernel, [(copies, *got.shape[1:])], "v" + "v", [], got)[0]


def split(a):
    hi = a.astype(BF16)
    return hi, (a - hi.astype(F32)).astype(BF16)


def dot3(a, b):
    ah, al = a
    bh, bl = b
    dot = functools.partial(jnp.dot, preferred_element_type=F32)
    return dot(ah, bh) + (dot(ah, bl) + dot(al, bh))


def dot6(a, b):
    return jnp.dot(a, b, precision=lax.Precision.HIGHEST, preferred_element_type=F32)


def gram_of(a, precision=None):
    return lax.dot_general(
        a, a, (((0,), (0,)), ((), ())), precision=precision, preferred_element_type=F32
    )


def eye(n):
    return (
        lax.broadcasted_iota(jnp.int32, (n, n), 0) == lax.broadcasted_iota(jnp.int32, (n, n), 1)
    ).astype(F32)


def total(a):
    return jnp.sum(jnp.sum(a, axis=1, keepdims=True), axis=0, keepdims=True)


def shifted_inverse(hess, mat_ref, x_ref):
    n = hess.shape[0]
    ident = eye(n)
    rho = total(hess * ident) * (1.0 / n)
    mat = hess * (1.0 / rho) + ident
    mat_ref[...] = mat
    mat_parts = split(mat)
    low, high = 0.999, n + 1.5
    c0 = 2.0 / (low + high)

    def grow(a):
        up = a * (2.0 - a)
        s = 2.0 / (1.0 + up)
        return s, s * up

    s, a = grow(low * c0)
    x_ref[...] = (s * c0) * (2.0 * ident - c0 * mat)

    def coarse(_, a):
        s, a = grow(a)
        x_parts = split(x_ref[...])
        y = 2.0 * ident - dot3(mat_parts, x_parts)
        x_ref[...] = s * dot3(x_parts, split(y))
        return a

    lax.fori_loop(0, 5, coarse, jnp.float32(a))
    x = x_ref[...]
    x_ref[...] = dot6(x, 2.0 * ident - dot6(mat_ref[...], x))
    return rho


STEP = 1.0 / 128.0
ROOM = 14.98


def encode(block):
    top = jnp.max(jnp.abs(block), axis=0, keepdims=True)
    code = jnp.ceil(jnp.log2(jnp.maximum(top, 1e-30)) * 128.0)
    return jnp.round(block * jnp.exp2(ROOM - code * STEP)), code


def decode(whole, code):
    return whole * jnp.exp2(code * STEP - ROOM)


def to_codes(a):
    return a.astype(jnp.int32).astype(jnp.int16)


def from_codes(a):
    return a.astype(jnp.int32).astype(F32)


def placed():
    z, y, x, _, core = [lax.axis_index(a) for a in AXES]
    flat = core == 0
    return (
        jnp.where(flat, x, y), jnp.where(flat, y, x), z, core,
        jnp.where(flat, 1, 4), jnp.where(flat, 4, 1),
    )


def block_row(place, k, b):
    j, i = b // 4, b % 4
    first = lax.rem(place[0] + k, 4)
    second = lax.rem(place[1] + j, 4)
    depth = lax.rem(place[2] + i, 4)
    block = depth * 16 + first * place[4] + second * place[5]
    return pl.multiple_of(block * SHARE, 8)


def coded_rows(blocks):
    return -(-blocks * (SHARE + 1) // 16) * 16


def encode_blocks(source, first, blocks, coded, out):
    coded[blocks * SHARE :, :] = jnp.zeros((coded.shape[0] - blocks * SHARE, R), F32)
    for b in range(blocks):
        whole, code = encode(source[(first + b) * SHARE : (first + b + 1) * SHARE, :])
        coded[b * SHARE : (b + 1) * SHARE, :] = whole
        coded[blocks * SHARE + b : blocks * SHARE + b + 1, :] = code
    out[...] = to_codes(coded[...])


def add_blocks(acc, blocks, part, r):
    part[...] = from_codes(r[...])
    for b in range(blocks):
        acc[b * SHARE : (b + 1) * SHARE, :] += decode(
            part[b * SHARE : (b + 1) * SHARE, :],
            part[blocks * SHARE + b : blocks * SHARE + b + 1, :],
        )


def inverse_kernel(patient, month, near, rho_ref, weights, mat, square):
    month_gram = gram_of(month[...], lax.Precision.HIGHEST)
    gram = gram_of(patient[...])
    rho = shifted_inverse(gram * month_gram, mat, near)
    rho_ref[...] = jnp.broadcast_to(rho, rho_ref.shape)
    core = placed()[3]
    mat[...] = near[...]

    @pl.when(core == 1)
    def _():
        mat[...] = dot6(near[...], near[...])

    square[...] = gram
    half = pl.multiple_of(core * 128, 128)
    for p in range(16):
        weights[p * 24 : p * 24 + 16, :] = rho * mat[p * 16 : p * 16 + 16, :]
        weights[p * 24 + 16 : p * 24 + 24, :] = square[pl.ds(half + p * 8, 8), :]


def local_kernel(
    live, patient_at, code_at, month_at, near, rho_ref, patient_hbm, month_hbm, tiles_hbm, duals_hbm,
    store, g_hbm, q1, q2, q3,
    patient, month, tiles, duals, prod, grad, u_part, g_part, v, g_own, coded, held, sems, outs,
):
    copies = [
        pltpu.make_async_copy(src, dst, sems.at[n])
        for n, (src, dst) in enumerate(
            [
                (month_hbm, month), (patient_hbm, patient), (tiles_hbm, tiles), (duals_hbm, duals),
            ]
        )
    ]
    for copy in copies:
        copy.start()
    rho = rho_ref[0:1, 0:1]
    place = placed()
    grad[...] = jnp.zeros_like(grad)
    for copy in copies[:3]:
        copy.wait()

    def visit(turn, _):
        for k in [turn * 4 + n for n in range(4)]:
            pat = patient[pl.ds(pl.multiple_of(patient_at[k] * BLOCK, BLOCK), BLOCK), :]
            prod[k] = lax.dot_general(
                tiles[k], pat, (((0,), (0,)), ((), ())), preferred_element_type=F32
            )
        for k in [turn * 4 + n for n in range(4)]:
            scale = jnp.where(k < live[0], month[pl.ds(month_at[k], 1), :], 0.0)
            at = pl.ds(pl.multiple_of(code_at[k] * BLOCK, BLOCK), BLOCK)
            grad[at, :] += prod[k] * scale
        return 0

    lax.fori_loop(0, (live[0] + 3) // 4, visit, 0)
    prod_out = pltpu.make_async_copy(prod, store.at[pl.ds(0, CAP)], outs.at[4])
    prod_out.start()
    near_parts = split(near[...])
    copies[3].wait()

    for b in range(16):
        g_own[b * SHARE : (b + 1) * SHARE, :] = grad[pl.ds(block_row(place, 0, b), SHARE), :]
    g_out = pltpu.make_async_copy(g_own, g_hbm, outs.at[3])
    g_out.start()

    def chunk(step, _):
        k = lax.rem(step + 1, 3) + 1
        for b in range(16):
            at = pl.ds(block_row(place, k, b), SHARE)
            u_part[b * SHARE : (b + 1) * SHARE, :] = duals[at, :]
            g_part[b * SHARE : (b + 1) * SHARE, :] = grad[at, :]
        once, twice = two_rounds(u_part[...], g_part[...], rho, near_parts)
        v[k - 1] = twice.reshape(5, BLOCK, R)
        u_part[...] = rho * once
        g_part[...] = rho * twice
        for b in range(16):
            for q, part in enumerate((u_part, g_part)):
                whole, code = encode(part[b * SHARE : (b + 1) * SHARE, :])
                row = b * 80 + q * SHARE
                coded[row : row + SHARE, :] = whole
                coded[1280 + 2 * b + q : 1281 + 2 * b + q, :] = code
        held[k - 1] = to_codes(coded[...])
        for n, out in enumerate((q1, q2, q3)):

            @pl.when(k == n + 1)
            def _(n=n, out=out):
                pltpu.make_async_copy(held.at[n], out, outs.at[n]).start()
                at = pl.ds(CAP + 5 * n, 5)
                pltpu.make_async_copy(v.at[n], store.at[at], outs.at[5 + n]).start()

        return 0

    lax.fori_loop(0, 3, chunk, 0)
    for n, out in enumerate((q1, q2, q3)):
        pltpu.make_async_copy(held.at[n], out, outs.at[n]).wait()
    prod_out.wait()
    g_out.wait()
    for n in range(3):
        pltpu.make_async_copy(v.at[n], store.at[pl.ds(CAP + 5 * n, 5)], outs.at[5 + n]).wait()


def two_rounds(u, g, rho, near_parts):
    g = g * (1.0 / rho)
    once = u + dot3(split(g - u), near_parts)
    return once, once + dot3(split(g - once), near_parts)


def own_kernel(near, rho_ref, g_part, duals_hbm, room, v0, u_part, a0, sems):
    place = placed()
    copies = [
        pltpu.make_async_copy(
            duals_hbm.at[pl.ds(block_row(place, 0, b), SHARE), :],
            u_part.at[pl.ds(b * SHARE, SHARE), :],
            sems.at[b],
        )
        for b in range(16)
    ]
    for copy in copies:
        copy.start()
    rho = rho_ref[0:1, 0:1]
    near_parts = split(near[...])
    for copy in copies:
        copy.wait()
    once, twice = two_rounds(u_part[...], g_part[...], rho, near_parts)
    v0[...] = twice
    u_part[...] = rho * once
    for b in range(16):
        a0[b * 80 : b * 80 + SHARE, :] = u_part[b * SHARE : (b + 1) * SHARE, :]
        a0[b * 80 + SHARE : b * 80 + 80, :] = rho * v0[b * SHARE : (b + 1) * SHARE, :]
    out = pltpu.make_async_copy(a0, room.at[pl.ds(0, 2 * CHUNK), :], sems.at[16])
    out.start()
    v_out = pltpu.make_async_copy(v0, room.at[pl.ds(2 * CHUNK, CHUNK), :], sems.at[17])
    v_out.start()
    out.wait()
    v_out.wait()


def first_sum_kernel(own_hbm, r1, r2, r3, s0, q1, q2, q3, p1, p2, p3, c1, c2, c3, own, sem):
    copy = pltpu.make_async_copy(own_hbm.at[pl.ds(0, 2 * CHUNK), :], own, sem)
    copy.start()
    parts = (p1, p2, p3)
    for p, r in zip(parts, (r1, r2, r3)):
        p[...] = from_codes(r[...])
    copy.wait()
    for coded in (c1, c2, c3):
        coded[320:, :] = jnp.zeros((coded.shape[0] - 320, R), F32)
    for b in range(32):
        rows = slice(b * SHARE, (b + 1) * SHARE)
        d1, d2, d3 = [decode(p[rows, :], p[1280 + b : 1281 + b, :]) for p in parts]
        value = (own[rows, :] + d1) + (d2 + d3)
        j, at = b // 8, b % 8
        if j == 0:
            s0[rows, :] = value
        else:
            coded = (c1, c2, c3)[j - 1]
            coded[at * SHARE : (at + 1) * SHARE, :], coded[320 + at : 321 + at, :] = encode(value)
    for coded, out in zip((c1, c2, c3), (q1, q2, q3)):
        out[...] = to_codes(coded[...])


def sum_kernel(own, r1, r2, r3, s0, q1, q2, q3, acc, part, coded):
    blocks = own.shape[0] // SHARE
    few = blocks // 4
    acc[...] = own[...]
    for r in (r1, r2, r3):
        add_blocks(acc, blocks, part, r)
    s0[...] = acc[0 : few * SHARE, :]
    for j, out in enumerate((q1, q2, q3)):
        encode_blocks(acc, (j + 1) * few, few, coded, out)


def cut_kernel(r0, r1, r2, r3, out):
    for j, r in enumerate((r0, r1, r2, r3)):
        for i in range(4):
            at = (j * 4 + i) * 80
            out[at : at + 80, :] = r[i * 128 + 48 : i * 128 + 128, :]


def owner_kernel(
    s0, s1, s2, s3, z0_ref, mine, other, month,
    codes_ref, z2_ref, code_ref, gram_ref, own, oth, coded, acc, part,
):
    acc[...] = s0[...]
    for r in (s1, s2, s3):
        add_blocks(acc, 2, part, r)
    summed = acc[...]
    core = placed()[3]
    half = pl.multiple_of(core * 128, 128)
    rest = pl.multiple_of(128 - core * 128, 128)
    for p in range(16):
        own[p * 16 : p * 16 + 16, :] = mine[p * 24 : p * 24 + 16, :]
        oth[p * 16 : p * 16 + 16, :] = other[p * 24 : p * 24 + 16, :]
        gram_ref[pl.ds(half + p * 8, 8), :] = mine[p * 24 + 16 : p * 24 + 24, :]
        gram_ref[pl.ds(rest + p * 8, 8), :] = other[p * 24 + 16 : p * 24 + 24, :]
    mf = month[...]
    diagonal = jnp.sum(gram_ref[...] * eye(R), axis=0, keepdims=True)
    rho_total = total(jnp.sum(mf * mf, axis=0, keepdims=True) * diagonal) * (1.0 / R)
    a = own[...]
    b = oth[...]
    plain = jnp.where(core == 0, a, b)
    square = jnp.where(core == 0, b, a)
    z0 = z0_ref[...]
    first = summed[0:SHARE] + dot6(z0, plain)
    z1 = jnp.maximum(first / rho_total, 0.0)
    second = summed[SHARE:] + dot6(z0, plain - square) + 2.0 * dot6(z1, plain) - rho_total * z1
    z2 = jnp.maximum(second / rho_total, 0.0)
    coded[...] = jnp.zeros_like(coded)
    coded[0:40, :], coded[40:41, :] = encode(z2)
    coded[48:88, :], coded[41:42, :] = encode(z0)
    coded[88:128, :], coded[42:43, :] = encode(z1)
    codes_ref[...] = to_codes(coded[...])
    z2_ref[...] = z2
    code_ref[...] = gram_of(z2, lax.Precision.HIGHEST)


def month_kernel(
    live, code_at, month_at, w0, w1, w2, w3, prod_hbm, code, out, natural, part, prod, sems
):
    place = placed()

    def fetch(k, _):
        pltpu.make_async_copy(prod_hbm.at[k], prod.at[k], sems.at[k]).start()
        return 0

    lax.fori_loop(0, live[0], fetch, 0)
    for k, w in enumerate((w0, w1, w2, w3)):
        part[...] = from_codes(w[...])
        for b in range(16):
            natural[pl.ds(block_row(place, k, b), SHARE), :] = decode(
                part[b * 48 : b * 48 + SHARE, :], part[b * 48 + SHARE : b * 48 + SHARE + 1, :]
            )
    for p in range(16):
        out[p * 24 : p * 24 + 8, :] = jnp.zeros((8, R), F32)
        out[p * 24 + 8 : p * 24 + 24, :] = code[p * 16 : p * 16 + 16, :]

    def visit(k, _):
        at = pl.ds(pl.multiple_of(code_at[k] * BLOCK, BLOCK), BLOCK)
        pltpu.make_async_copy(prod_hbm.at[k], prod.at[k], sems.at[k]).wait()
        column = jnp.sum(prod[k] * natural[at, :], axis=0, keepdims=True)
        m = month_at[k]
        out[pl.ds((m // 8) * 24 + m % 8, 1), :] += column
        return 0

    lax.fori_loop(0, live[0], visit, 0)


def duals_kernel(first, near, rho_ref, *refs):
    both, two, store, room = refs[0:2], refs[2:4], refs[4], refs[5]
    out, part, z0_part, z1_part, value, own, less, done, sems = refs[-9:]
    place = placed()
    fetches = []
    for n in range(2):
        at = CAP + 5 * (first + n - 1)
        source = store.at[pl.ds(at, 5)]
        target = value.at[pl.ds(n * 5, 5)]
        if first + n == 0:
            source, target = room.at[pl.ds(2 * CHUNK, CHUNK), :], own
        fetches.append(pltpu.make_async_copy(source, target, sems.at[32 + n]))
        fetches[n].start()
    near_parts = split(near[...])

    def chunk(k, _):
        for n in range(2):

            @pl.when(k == n)
            def _(n=n):
                part[0:1280, :] = from_codes(both[n][...])
                part[1280:, :] = from_codes(two[n][...])

        for b in range(16):
            rows = slice(b * SHARE, (b + 1) * SHARE)
            at = b * 80
            to = 1280 + b * 48
            z1 = decode(part[at + 40 : at + 80, :], part[to + 42 : to + 43, :])
            z0_part[rows, :] = decode(part[at : at + 40, :], part[to + 41 : to + 42, :])
            z1_part[rows, :] = 2.0 * z1
            z2 = decode(part[to : to + 40, :], part[to + 40 : to + 41, :])
            less[rows, :] = z1 + z2
        z0 = z0_part[...]
        inner = z0 - dot3(split(z0), near_parts) + z1_part[...]
        less[...] = dot3(split(inner), near_parts) - less[...]
        for n in range(2):

            @pl.when(k == n)
            def _(n=n):
                fetches[n].wait()
                base = own[...] if first + n == 0 else value[n * 5 : n * 5 + 5].reshape(CHUNK, R)
                done[n] = base + less[...]

        for b in range(16):
            pltpu.make_async_copy(
                done.at[k, pl.ds(b * SHARE, SHARE), :],
                out.at[pl.ds(block_row(place, first + k, b), SHARE), :],
                sems.at[k * 16 + b],
            ).start()
        return 0

    lax.fori_loop(0, 2, chunk, 0)
    for k in range(2):
        for b in range(16):
            pltpu.make_async_copy(
                done.at[k, pl.ds(b * SHARE, SHARE), :],
                out.at[pl.ds(block_row(place, first + k, b), SHARE), :],
                sems.at[k * 16 + b],
            ).wait()


def tail_kernel(sums, gram, month, out, mat, near, grad):
    for p in range(16):
        grad[p * 8 : p * 8 + 8, :] = sums[p * 24 : p * 24 + 8, :]
        mat[p * 16 : p * 16 + 16, :] = sums[p * 24 + 8 : p * 24 + 24, :]
    rho = shifted_inverse(gram[...] * mat[...], mat, near)
    scaled = grad[0:MONTHS, :] * (1.0 / rho) + month[...]
    solved = jnp.maximum(dot6(scaled, near[...]), 0.0)
    mean = jnp.sum(solved, axis=0, keepdims=True) * (1.0 / MONTHS)
    out[...] = solved / (mean + 1e-06)


def call(body, outs, spaces, scratch, *args, limit=48 << 20, aliases=None):
    n = len(args)
    space = {"s": pltpu.SMEM, "h": pltpu.HBM, "v": pltpu.VMEM}
    return pl.pallas_call(
        body,
        input_output_aliases=aliases or {},
        out_shape=[s if isinstance(s, jax.ShapeDtypeStruct) else jax.ShapeDtypeStruct(s, F32) for s in outs],
        in_specs=[pl.BlockSpec(memory_space=space[c]) for c in spaces[:n]],
        out_specs=[pl.BlockSpec(memory_space=space[c]) for c in spaces[n:]],
        scratch_shapes=[pltpu.VMEM(s, F32) if isinstance(s, tuple) else s for s in scratch],
        compiler_params=pltpu.CompilerParams(vmem_limit_bytes=limit),
    )(*args)


def compute(
    tile_values, patient_block, code_block, month_index, live_count,
    patient_factor, month_factor, consensus, scaled_duals,
):
    near, rho, weights = call(
        inverse_kernel, [(R, R), (8, 128), (384, R)], "vv" + "vvv", [(R, R), (R, R)],
        patient_factor, month_factor, limit=None,
    )
    m = exchange(weights.reshape(16, -1, R), PLANE)

    def codes(rows):
        return jax.ShapeDtypeStruct((rows, R), jnp.int16)

    tops = [coded_rows(n) for n in (32, 8, 2)]
    store, g_own, *s = call(
        local_kernel,
        [(SLOTS, BLOCK, R), (CHUNK, R)] + [codes(tops[0])] * 3,
        "ssssvvhhhh" + "hhhhh",
        [
            pltpu.VMEM((1024, R), BF16), (MONTHS, R), pltpu.VMEM((CAP, BLOCK, BLOCK), BF16),
            (ROWS, R), (CAP, BLOCK, R), (ROWS, R), (CHUNK, R), (CHUNK, R), (3, 5, BLOCK, R),
            (CHUNK, R), (tops[0], R), pltpu.VMEM((3, tops[0], R), jnp.int16),
            pltpu.SemaphoreType.DMA((4,)), pltpu.SemaphoreType.DMA((8,)),
        ],
        live_count, patient_block, code_block, month_index,
        near, rho, patient_factor, month_factor, tile_values, scaled_duals, limit=None,
    )
    s = [send(s[k - 1], first_move(k)) for k in (1, 2, 3)]
    (room,) = call(
        own_kernel, [(ROOM_ROWS, R)], "vvvh" + "h",
        [(CHUNK, R), (CHUNK, R), (2 * CHUNK, R), pltpu.SemaphoreType.DMA((18,))],
        near, rho, g_own, scaled_duals, limit=None,
    )
    m = exchange(fan(m, 4), "z")
    mine = exchange(fan(m, 16), PLANE).reshape(-1, R)
    other = send(mine, CORE_MOVE)
    s = call(
        first_sum_kernel, [(320, R)] + [codes(tops[1])] * 3, "hvvv" + "vvvv",
        [(tops[0], R)] * 3 + [(tops[1], R)] * 3 + [(2 * CHUNK, R), pltpu.SemaphoreType.DMA],
        room, *s,
    )
    s = scatter_sum(s, second_move)
    s = call(
        sum_kernel, [(80, R)] + [codes(tops[2])] * 3, "vvvv" + "vvvv",
        [(320, R), (tops[1], R), (tops[2], R)], *s,
    )
    s = scatter_sum(s, depth_move)
    rows, z2, code_gram, gram = call(
        owner_kernel, [codes(128), (SHARE, R), (R, R), (R, R)], "vvvvvvvv" + "vvvv",
        [(R, R), (R, R), (128, R), (80, R), (tops[2], R)],
        *s, consensus, mine, other, month_factor,
    )
    rows = jnp.concatenate(gather(rows, depth_move), 0)
    rows = gather(rows, second_move)
    two = jnp.concatenate([r.reshape(4, 128, R)[:, :48].reshape(192, R) for r in rows], 0)
    (both,) = call(cut_kernel, [codes(1280)], "vvvv" + "v", [], *rows)
    two = gather(two, first_move)
    both = gather(both, first_move)
    (sums,) = call(
        month_kernel, [(384, R)], "sssvvvvhv" + "v",
        [(ROWS, R), (768, R), (CAP, BLOCK, R), pltpu.SemaphoreType.DMA((CAP,))],
        live_count, code_block, month_index, *two, store, code_gram,
    )
    t = exchange(sums.reshape(16, -1, R), PLANE)
    t = fan(t, 1)
    t = jnp.concatenate([t, send(t, CORE_MOVE)], 0)
    t = exchange(fan(t, 8), ("z", "h"))
    t = exchange(fan(t, 16), PLANE).reshape(-1, R)
    scratch = [
        (2048, R), (CHUNK, R), (CHUNK, R), (10, BLOCK, R), (CHUNK, R), (CHUNK, R), (2, CHUNK, R),
        pltpu.SemaphoreType.DMA((34,)),
    ]
    (duals,) = call(
        functools.partial(duals_kernel, 0), [(ROWS, R)], "vvvvvvhh" + "h", scratch,
        near, rho, *both[:2], *two[:2], store, room,
    )
    (duals,) = call(
        functools.partial(duals_kernel, 2), [(ROWS, R)], "vvvvvvhhh" + "h", scratch,
        near, rho, *both[2:], *two[2:], store, room, duals, aliases={8: 0},
    )
    (new_months,) = call(
        tail_kernel, [(MONTHS, R)], "vvvv", [(R, R), (R, R), (BLOCK, R)], t, gram, month_factor
    )
    return (z2, duals, new_months)


def solution(mesh):
    mesh = Mesh(mesh.devices.reshape(4, 4, 4, 2, 2), AXES)
    site, cons = ("z", "y", "x"), ("h", "c")
    every = site + cons
    placed = (
        P(every, None, None), P(every), P(every), P(every), P(every),
        P(site, None), P(), P(site, cons), P(site, cons),
    )
    return jax.shard_map(
        compute,
        mesh=mesh,
        in_specs=placed,
        out_specs=(P(site, cons), P(site, cons), P()),
        check_vma=False,
    )
```
